32 devices in a mesh: shard: 4 (over z), context: 2 (over x), tensor: 4 (over y, core).
Axes of the slice: x: 2, y: 2, z: 4, core: 2. Of those that a mesh axis runs over, the one named last changes fastest.
Arguments:
- hidden_in: bfloat16 [4, 2048, 1536], P('shard', 'context'), may hold values from -6 to 6
- norm_gain: float32 [1536], replicated, may hold values from 0.5 to 1.5
- w_in_zx: bfloat16 [1536, 2, 3072], P('shard', None, 'tensor'), may hold values from -0.15625 to 0.15625
- w_in_bc: bfloat16 [1536, 256], P('shard'), may hold values from -0.15625 to 0.15625
- w_in_dt: bfloat16 [1536, 48], P('shard', 'tensor'), may hold values from -0.15625 to 0.15625
- conv_x: float32 [5, 3072], P(None, 'tensor'), may hold values from -3 to 3
- conv_bc: float32 [5, 256], replicated, may hold values from -3 to 3
- dt_bias: float32 [48], P('tensor'), may hold values from -6 to -2.5
- a_log: float32 [48], P('tensor'), may hold values from -1 to 1.5
- d_skip: float32 [48], P('tensor'), may hold values from 0.5 to 1.5
- out_gain: float32 [3072], P('tensor'), may hold values from 0.5 to 1.5
- w_out: bfloat16 [3072, 1536], P('tensor', 'shard'), may hold values from -0.109375 to 0.109375
- cotangent: bfloat16 [4, 2048, 1536], P('shard', 'context'), may hold values from -6 to 6
Outputs:
- out: bfloat16 [4, 2048, 1536], P('shard', 'context')
- grad_in: float32 [4, 2048, 1536], P('shard', 'context')
- grad_norm_gain: float32 [1536], replicated
- grad_w_in_zx: float32 [1536, 2, 3072], P(('shard', 'context'), None, 'tensor')
- grad_w_in_bc: float32 [1536, 256], P(('shard', 'context'))
- grad_w_in_dt: float32 [1536, 48], P(('shard', 'context'), 'tensor')
- grad_conv_x: float32 [5, 3072], P(None, 'tensor')
- grad_conv_bc: float32 [5, 256], replicated
- grad_dt_bias: float32 [48], P('tensor')
- grad_a_log: float32 [48], P('tensor')
- grad_d_skip: float32 [48], P('tensor')
- grad_out_gain: float32 [3072], P('tensor')
- grad_w_out: float32 [3072, 1536], P('tensor', ('shard', 'context'))
- rms_stream: float32 [], replicated
- rms_mixer: float32 [], replicated
The draws below stay inside these ranges and needn't reach their ends.
All inputs are finite; a program needn't handle non-finite values.
Results may differ from the reference program's by a relative error of at most 0.012.
Values may be sent and summed in bfloat16 or wider, within the bound.
No kernel may reach another device: no remote copies, remote signals or barrier semaphores. Data moves between devices by JAX's collectives and lax.ppermute only.
A program may use at most 192 MiB of HBM per device.

```python
import jax
import jax.numpy as jnp
from jax import lax

D = 1536
INNER = 3072
HEADS = 48
P_SIZE = 64
N = 128
KW = 4
CH = 256
LEN = 2048
BATCH = 4


def levels(key, dims, cuts, smallest, high):
    def one(axis_at, blocks):
        heights = jax.random.uniform(jax.random.fold_in(jax.random.fold_in(key, 6), axis_at), (blocks,), jnp.float32, smallest / len(cuts), high / len(cuts))
        return jnp.repeat(jnp.exp(heights), dims[axis_at] // blocks).reshape((-1,) + (1,) * (len(dims) - axis_at - 1))

    gain = one(*cuts[0])
    for cut in cuts[1:]:
        gain = gain * one(*cut)
    return gain


def bell_draw(own_key, dims, deviation, most, cuts=(), dtype=jnp.bfloat16):
    entries = deviation * jax.random.normal(own_key, dims, jnp.float32)
    if cuts:
        entries = entries * levels(own_key, dims, cuts, -0.22, 0.18)
    return jnp.clip(entries, -most, most).astype(dtype)


def setup_inputs(seed: int = 0) -> dict:
    streams_of = jax.random.split(jax.random.key(seed), 14)
    hidden_in = bell_draw(streams_of[0], (BATCH, LEN, D), 1.0, 6.0, ((0, 4), (1, 2)))
    norm_gain = jnp.clip(1.0 + 0.1 * jax.random.normal(streams_of[1], (D,), jnp.float32), 0.5, 1.5)
    w_in_zx = bell_draw(streams_of[2], (D, 2, INNER), D ** -0.5, 0.15625, ((0, 4), (2, 4)))
    w_in_bc = bell_draw(streams_of[3], (D, 2 * N), D ** -0.5, 0.15625, ((0, 4),))
    w_in_dt = bell_draw(streams_of[4], (D, HEADS), D ** -0.5, 0.15625, ((0, 4), (1, 4)))
    conv_x = bell_draw(streams_of[5], (KW + 1, INNER), 0.5, 3.0, ((1, 4),), jnp.float32)
    conv_bc = bell_draw(streams_of[6], (KW + 1, 2 * N), 0.5, 3.0, (), jnp.float32)
    dt_bias = jnp.clip(-6.0 + 3.5 * jax.random.uniform(streams_of[7], (HEADS,), jnp.float32) ** levels(streams_of[7], (HEADS,), ((0, 4),), -0.2, 0.2), -6.0, -2.5)
    a_log = jnp.clip(-1.0 + 2.5 * jax.random.uniform(streams_of[8], (HEADS,), jnp.float32) ** levels(streams_of[8], (HEADS,), ((0, 4),), -0.2, 0.2), -1.0, 1.5)
    d_skip = jnp.clip(0.5 + 1.0 * jax.random.uniform(streams_of[9], (HEADS,), jnp.float32) ** levels(streams_of[9], (HEADS,), ((0, 4),), -0.2, 0.2), 0.5, 1.5)
    out_gain = jnp.clip(1.0 + 0.1 * jax.random.normal(streams_of[10], (INNER,), jnp.float32), 0.5, 1.5)
    w_out = bell_draw(streams_of[11], (INNER, D), INNER ** -0.5, 0.109375, ((0, 4), (1, 4)))
    cotangent = bell_draw(streams_of[12], (BATCH, LEN, D), 1.0, 6.0, ((0, 4), (1, 2)))
    return dict(hidden_in=hidden_in, norm_gain=norm_gain, w_in_zx=w_in_zx, w_in_bc=w_in_bc, w_in_dt=w_in_dt, conv_x=conv_x, conv_bc=conv_bc, dt_bias=dt_bias, a_log=a_log, d_skip=d_skip, out_gain=out_gain, w_out=w_out, cotangent=cotangent)


EPSILON = 1e-05
PRECISE = lax.Precision.HIGHEST

@jax.custom_vjp
def low(v):
    return lax.optimization_barrier(v.astype(jnp.bfloat16)).astype(jnp.float32)

@jax.custom_vjp
def low_back(v):
    return v

def low_keep(v):
    return (low(v), None)

def low_pass(kept, grad):
    return (grad,)

def back_keep(v):
    return (v, None)

def back_low(kept, grad):
    return (low(grad),)
low.defvjp(low_keep, low_pass)
low_back.defvjp(back_keep, back_low)

def silu_of(values):
    return values * jax.nn.sigmoid(values)

def product(left_op, right_op):
    return jnp.dot(left_op, right_op, precision=PRECISE, preferred_element_type=jnp.float32)

def sequence_forward(stream_in, norm_gain, w_in_zx, w_in_bc, w_in_dt, conv_x, conv_bc, dt_bias, a_log, d_skip, out_gain, w_out):
    scale_in = lax.rsqrt(lax.optimization_barrier(jnp.mean(stream_in * stream_in, axis=-1, keepdims=True)) + EPSILON)
    normed = low(stream_in * scale_in * norm_gain)
    gate_val = low_back(product(normed, w_in_zx[:, 0, :]))
    xs_val = low_back(product(normed, w_in_zx[:, 1, :]))
    bc_val = low_back(product(normed, w_in_bc))
    dt_raw = low_back(product(normed, w_in_dt))
    pre_conv = jnp.concatenate([xs_val, bc_val], axis=-1)
    conv_all = jnp.concatenate([conv_x, conv_bc], axis=1)
    padded = jnp.pad(pre_conv, ((KW - 1, 0), (0, 0)))
    conv_out = conv_all[KW] + jnp.zeros_like(pre_conv)
    for tap_idx in range(KW):
        conv_out = conv_out + conv_all[tap_idx] * padded[tap_idx:tap_idx + LEN]
    activated = low(silu_of(conv_out))
    block_count = LEN // CH
    xa_all = activated[:, :INNER].reshape(block_count, CH, HEADS, P_SIZE)
    bm_all = activated[:, INNER:INNER + N].reshape(block_count, CH, N)
    cm_all = activated[:, INNER + N:].reshape(block_count, CH, N)
    dt_val = jax.nn.softplus(dt_raw + dt_bias)
    log_dec = -jnp.exp(a_log) * dt_val
    dt_all = dt_val.reshape(block_count, CH, HEADS)
    log_all = log_dec.reshape(block_count, CH, HEADS)
    positions = jnp.arange(CH)
    lower_mask = positions[:, None] >= positions[None, :]
    lower_f = lower_mask.astype(jnp.float32)

    def block_step(state_in, element):
        xa_blk, bm_blk, cm_blk, dt_blk, log_blk = element
        cum_log = jnp.cumsum(log_blk, axis=0)
        block_log = cum_log[-1]
        scores = product(cm_blk, bm_blk.T)
        cum_t = cum_log.T
        log_gap = cum_t[:, :, None] - cum_t[:, None, :]
        decay_mat = jnp.exp(jnp.where(lower_mask[None], log_gap, 0.0)) * lower_f[None]
        weights = low(scores[None] * decay_mat * dt_blk.T[:, None, :])
        y_intra = jnp.einsum('hij,jhp->ihp', weights, xa_blk, precision=PRECISE)
        cm_scaled = low(cm_blk[:, None, :] * jnp.exp(cum_log)[:, :, None])
        y_inter = jnp.einsum('ihn,hnp->ihp', cm_scaled, low(state_in), precision=PRECISE)
        w_end = jnp.exp(block_log[None, :] - cum_log) * dt_blk
        xw_val = low(xa_blk * w_end[:, :, None])
        state_add = low_back(jnp.einsum('jn,jhp->hnp', bm_blk, xw_val, precision=PRECISE))
        state_out = jnp.exp(block_log)[:, None, None] * state_in + state_add
        return (state_out, y_intra + y_inter + d_skip[None, :, None] * xa_blk)
    _, y_blocks = lax.scan(block_step, jnp.zeros((HEADS, N, P_SIZE), jnp.float32), (xa_all, bm_all, cm_all, dt_all, log_all))
    y_val = low_back(y_blocks.reshape(LEN, INNER))
    gated = y_val * silu_of(gate_val)
    scale_out = lax.rsqrt(lax.optimization_barrier(jnp.mean(gated * gated, axis=-1, keepdims=True)) + EPSILON)
    out_in = low(gated * scale_out * out_gain)
    mixed = product(out_in, w_out)
    stream = stream_in + mixed
    return (stream, jnp.sum(stream * stream), jnp.sum(mixed * mixed))

def reference(hidden_in, norm_gain, w_in_zx, w_in_bc, w_in_dt, conv_x, conv_bc, dt_bias, a_log, d_skip, out_gain, w_out, cotangent):
    weights = (norm_gain.astype(jnp.float32), w_in_zx.astype(jnp.float32), w_in_bc.astype(jnp.float32), w_in_dt.astype(jnp.float32), conv_x.astype(jnp.float32), conv_bc.astype(jnp.float32), dt_bias.astype(jnp.float32), a_log.astype(jnp.float32), d_skip.astype(jnp.float32), out_gain.astype(jnp.float32), w_out.astype(jnp.float32))
    inputs = hidden_in.astype(jnp.float32)

    def forward(stream_all, *params):

        def step_fn(totals, stream_in):
            stream, sq_stream, sq_mixed = sequence_forward(stream_in, *params)
            return ((totals[0] + sq_stream, totals[1] + sq_mixed), stream)
        zero_sum = jnp.zeros((), jnp.float32)
        totals, streams = lax.scan(jax.checkpoint(step_fn), (zero_sum, zero_sum), stream_all)
        return (streams, totals[0], totals[1])
    (streams, sum_stream, sum_mixed), pullback = jax.vjp(forward, inputs, *weights)
    gradients = pullback((cotangent.astype(jnp.float32), jnp.zeros_like(sum_stream), jnp.zeros_like(sum_mixed)))
    entry_count = BATCH * LEN * D
    return (streams.astype(jnp.bfloat16), gradients[0], gradients[1], gradients[2], gradients[3], gradients[4], gradients[5], gradients[6], gradients[7], gradients[8], gradients[9], gradients[10], gradients[11], jnp.sqrt(sum_stream / entry_count), jnp.sqrt(sum_mixed / entry_count))
```

```python
import functools

import jax
import jax.numpy as jnp
from jax import lax
from jax.experimental import pallas as pl
from jax.experimental.pallas import tpu as pltpu
from jax.sharding import PartitionSpec as P

CH = 256
EPSILON = 1e-05
LANES = 128
HALO = 8
F32 = jnp.float32
BF16 = jnp.bfloat16


def swap_pairs(size, by):
    return [(i, i ^ by) for i in range(size)]


def butterfly(value, axis):
    size = lax.axis_size(axis)
    if size & (size - 1):
        return lax.psum(value, axis)
    by = 1
    while by < size:
        value = value + lax.ppermute(value, axis, swap_pairs(size, by))
        by *= 2
    return value


def shifted(array, axis, by):
    length = lax.axis_size(axis)
    pairs = [(i, i + by) for i in range(length) if 0 <= i + by < length]
    return lax.ppermute(array, axis, pairs)


def joint_pairs(size, context, sources, move):
    return [(i * context + c, move(i, c)[0] * context + move(i, c)[1]) for i in sources for c in range(context)]


def gather_weights(local):
    shards, parts = lax.axis_size("shard"), lax.axis_size("context")
    here, side = lax.axis_index("shard"), lax.axis_index("context")
    rows = local.shape[0] // parts
    own = lax.dynamic_slice_in_dim(local, side * rows, rows, 0)
    axes = ("shard", "context")
    if parts != 2 or shards > 8:
        return lax.all_gather(own, axes, axis=0, tiled=True)
    whole_rows = shards * parts * rows
    full = jnp.zeros((whole_rows + rows, local.shape[1]), local.dtype)
    full = lax.dynamic_update_slice_in_dim(full, local, here * parts * rows, 0)

    def put(full, piece, valid, source, part):
        at = jnp.where(valid, (source * parts + part) * rows, whole_rows)
        return lax.dynamic_update_slice_in_dim(full, piece, at, 0)

    plus = minus = own
    for k in range(1, shards):
        plus = lax.ppermute(plus, axes, joint_pairs(shards, parts, range(k - 1, shards - 1), lambda i, c: (i + 1, c)))
        minus = lax.ppermute(minus, axes, joint_pairs(shards, parts, range(1, shards - k + 1), lambda i, c: (i - 1, c)))
        across_plus = lax.ppermute(plus, axes, joint_pairs(shards, parts, range(k, shards), lambda i, c: (i, 1 - c)))
        across_minus = lax.ppermute(minus, axes, joint_pairs(shards, parts, range(0, shards - k), lambda i, c: (i, 1 - c)))
        full = put(full, plus, here >= k, here - k, side)
        full = put(full, minus, here + k < shards, here + k, side)
        full = put(full, across_plus, here >= k, here - k, 1 - side)
        full = put(full, across_minus, here + k < shards, here + k, 1 - side)
    return full


def scatter_grad(keep, send):
    shards = lax.axis_size("shard")
    here = lax.axis_index("shard")
    got = lax.ppermute(send, "context", swap_pairs(2, 1))
    summed = (keep.astype(F32) + got.astype(F32)).astype(BF16)
    piece = lambda at: lax.dynamic_index_in_dim(summed, jnp.clip(at, 0, shards - 1), 0, False)
    plus = minus = None
    for k in range(1, shards):
        up, down = piece(here + shards - k), piece(here - shards + k)
        if plus is not None:
            up = (up.astype(F32) + plus.astype(F32)).astype(BF16)
            down = (down.astype(F32) + minus.astype(F32)).astype(BF16)
        plus = lax.ppermute(up, "shard", [(i, i + 1) for i in range(k)])
        minus = lax.ppermute(down, "shard", [(shards - 1 - i, shards - 2 - i) for i in range(k)])
    return piece(here).astype(F32) + plus.astype(F32) + minus.astype(F32)


def tensor_pairs(size, bit):
    return swap_pairs(size, bit)


def reduce_mine(keep, send, size):
    got = lax.ppermute(send, "tensor", swap_pairs(size, 1))
    rows = keep.shape[0] // 2
    other = (keep[rows:].astype(F32) + got[rows:].astype(F32)).astype(BF16)
    got_mine = lax.ppermute(other, "tensor", swap_pairs(size, 2))
    return keep[:rows].astype(F32) + got[:rows].astype(F32) + got_mine.astype(F32)


def assemble_kernel(place, own, chip, core_a, core_b, out):
    r = pl.program_id(0)
    for k, ref in enumerate((own, chip, core_a, core_b)):

        @pl.when(r == k)
        def _():
            out[...] = ref[...].astype(out.dtype)


def gather_quarters(mine, place, size, dtype):
    chip = lax.ppermute(mine, "tensor", swap_pairs(size, 2))
    core_a = lax.ppermute(mine, "tensor", swap_pairs(size, 1))
    core_b = lax.ppermute(chip, "tensor", swap_pairs(size, 1))
    rows, cols = mine.shape
    piece = pl.BlockSpec((rows, cols), lambda r, q: (0, 0))
    return pl.pallas_call(
        assemble_kernel,
        name="assemble",
        grid_spec=pltpu.PrefetchScalarGridSpec(
            num_scalar_prefetch=1,
            grid=(4,),
            in_specs=[piece] * 4,
            out_specs=pl.BlockSpec((rows, cols), lambda r, q: (r ^ q[0], 0)),
        ),
        out_shape=jax.ShapeDtypeStruct((4 * rows, cols), dtype),
        compiler_params=params(),
        cost_estimate=cost(0, 12 * rows * cols + 0, 0),
    )(place, mine, chip, core_a, core_b)


def dot_nn(a, b):
    return lax.dot_general(a, b, (((1,), (0,)), ((), ())), preferred_element_type=F32)


def dot_nt(a, b):
    return lax.dot_general(a, b, (((1,), (1,)), ((), ())), preferred_element_type=F32)


def dot_tn(a, b):
    return lax.dot_general(a, b, (((0,), (0,)), ((), ())), preferred_element_type=F32)


def by_heads(values, onehot):
    high = values.astype(BF16)
    low = (values - high.astype(F32)).astype(BF16)
    return dot_nn(high, onehot) + dot_nn(low, onehot)


def by_heads_t(values, onehot):
    high = values.astype(BF16)
    low = (values - high.astype(F32)).astype(BF16)
    return dot_nt(high, onehot) + dot_nt(low, onehot)


def row_of(values, onehot):
    return by_heads(jnp.broadcast_to(values, (8, values.shape[1])), onehot)[0:1]


def fold_rows(values):
    rows, cols = values.shape
    return jnp.sum(values.reshape(rows // 8, 8, cols), axis=0)


def exact_parts(values):
    high = values.astype(BF16)
    rest = values - high.astype(F32)
    mid = rest.astype(BF16)
    low = (rest - mid.astype(F32)).astype(BF16)
    return high, mid, low


def sigmoid(values):
    return 1.0 / (1.0 + jnp.exp(-values))


def whole(shape):
    zeros = (0,) * len(shape)
    return pl.BlockSpec(shape, lambda *_: zeros)


def params(semantics=("arbitrary",)):
    return pltpu.CompilerParams(dimension_semantics=semantics, vmem_limit_bytes=60 * 1024 * 1024)


def cost(flops, nbytes, exps=0):
    return pl.CostEstimate(flops=int(flops), bytes_accessed=int(nbytes), transcendentals=int(exps))


def conv_kernel(normed, halo, weight, taps, act, pre):
    rows = normed.shape[0]
    tap_count = 4
    w = weight[...]
    pre[0:HALO, :] = dot_nn(halo[...], w)
    pre[HALO:, :] = dot_nn(normed[...], w)
    first = HALO - tap_count + 1
    out = taps[tap_count : tap_count + 1, :] + taps[0:1, :] * pre[first : first + rows, :]
    for k in range(1, tap_count):
        out = out + taps[k : k + 1, :] * pre[first + k : first + k + rows, :]
    act[...] = (out * sigmoid(out)).astype(BF16)


def conv_front(normed, halo, weight, taps):
    rows, dim = normed.shape
    cols = taps.shape[1]
    tile = 256
    return pl.pallas_call(
        conv_kernel,
        name="conv_front",
        grid=(cols // tile,),
        in_specs=[
            whole((rows, dim)),
            whole((HALO, dim)),
            pl.BlockSpec((dim, tile), lambda j: (0, j)),
            pl.BlockSpec((8, tile), lambda j: (0, j)),
        ],
        out_specs=[
            pl.BlockSpec((rows, tile), lambda j: (0, j)),
            pl.BlockSpec((rows + HALO, tile), lambda j: (0, j)),
        ],
        out_shape=[
            jax.ShapeDtypeStruct((rows, cols), BF16),
            jax.ShapeDtypeStruct((rows + HALO, cols), F32),
        ],
        compiler_params=params(),
        cost_estimate=cost(2 * rows * dim * cols, 2 * (rows + cols) * dim + 6 * rows * cols, rows * cols),
    )(normed, halo, weight, taps)


def step_kernel(normed, weight, bias, rate, dt, sig, cum, seq, cum_t, before):
    @pl.when(pl.program_id(0) == 0)
    def _():
        before[...] = jnp.zeros_like(before)

    raw = dot_nn(normed[...], weight[...]) + bias[...]
    small = jnp.exp(-jnp.abs(raw))
    dt_val = jnp.maximum(raw, 0.0) + jnp.log1p(small)
    dt[...] = dt_val
    sig[...] = sigmoid(raw)
    rows = raw.shape[0]
    lower = (
        lax.broadcasted_iota(jnp.int32, (rows, rows), 0) >= lax.broadcasted_iota(jnp.int32, (rows, rows), 1)
    ).astype(BF16)
    total = jnp.zeros_like(raw)
    for part in exact_parts(dt_val * rate[...]):
        total = total + dot_nn(lower, part)
    cum[...] = total
    seq[...] = total + before[0:1, :]
    before[...] = before[...] + jnp.broadcast_to(total[rows - 1 : rows, :], before.shape)
    cum_t[...] = jnp.transpose(total)[0:16, :]


def step_sizes(normed, weight, bias, rate, col):
    rows, dim = normed.shape
    block = pl.BlockSpec((CH, LANES), lambda b: (b, 0))
    wide = jax.ShapeDtypeStruct((rows, LANES), F32)
    return pl.pallas_call(
        step_kernel,
        name="step_sizes",
        grid=(rows // CH,),
        in_specs=[
            pl.BlockSpec((CH, dim), lambda b: (b, 0)),
            pl.BlockSpec((dim, LANES), lambda b: (0, col)),
            whole((1, LANES)),
            whole((1, LANES)),
        ],
        out_specs=[block, block, block, block, pl.BlockSpec((16, CH), lambda b: (0, b))],
        out_shape=[wide, wide, wide, wide, jax.ShapeDtypeStruct((16, rows), F32)],
        scratch_shapes=[pltpu.VMEM((8, LANES), F32)],
        compiler_params=params(),
        cost_estimate=cost(2 * rows * dim * LANES, 2 * rows * dim + 20 * rows * LANES, 3 * rows * LANES),
    )(normed, weight, bias, rate)


def ssd_kernel(heads, xa_ref, bm_ref, cm_ref, dt_ref, cum_ref, cum_t_ref, skip, onehot, y_ref, start_ref, end_ref, state):
    @pl.when(pl.program_id(0) == 0)
    def _():
        state[...] = jnp.zeros_like(state)

    hot = onehot[...]
    xa = xa_ref[...].astype(F32)
    bm, cm, cum, cum_t = bm_ref[...], cm_ref[...], cum_ref[...], cum_t_ref[...]
    rows = cum.shape[0]
    last = cum[rows - 1 : rows, :]
    x_dt = xa * by_heads(dt_ref[...], hot)
    before = state[...]
    start_ref[0] = before
    y_ref[...] = by_heads(jnp.exp(cum), hot) * dot_nn(cm, before.astype(BF16)) + skip[...] * xa
    to_end = (x_dt * by_heads(jnp.exp(last - cum), hot)).astype(BF16)
    after = row_of(jnp.exp(last), hot) * before + dot_tn(bm, to_end)
    state[...] = after
    end_ref[...] = after
    x_low = x_dt.astype(BF16)
    scores = dot_nt(cm, bm)
    mask = lax.broadcasted_iota(jnp.int32, (rows, rows), 0) >= lax.broadcasted_iota(jnp.int32, (rows, rows), 1)
    width = xa.shape[1] // heads
    per = LANES // width
    lane = lax.broadcasted_iota(jnp.int32, (rows, LANES), 1) // width
    for group in range(heads // per):
        at = slice(group * LANES, (group + 1) * LANES)
        x_group = x_low[:, at]
        total = y_ref[:, at]
        for k in range(per):
            h = group * per + k
            gap = jnp.where(mask, cum[:, h : h + 1] - cum_t[h : h + 1, :], 0.0)
            weights = jnp.where(mask, jnp.exp(gap) * scores, 0.0).astype(BF16)
            total = total + dot_nn(weights, jnp.where(lane == k, x_group, jnp.zeros_like(x_group)))
        y_ref[:, at] = total


def ssd_forward(act, dt, cum, cum_t, skip, onehot, heads):
    rows = act.shape[0]
    inner = onehot.shape[1]
    blocks = rows // CH
    col = inner // LANES
    wide = pl.BlockSpec((CH, LANES), lambda b: (b, 0))
    return pl.pallas_call(
        functools.partial(ssd_kernel, heads),
        name="ssd_forward",
        grid=(blocks,),
        in_specs=[
            pl.BlockSpec((CH, inner), lambda b: (b, 0)),
            pl.BlockSpec((CH, LANES), lambda b: (b, col)),
            pl.BlockSpec((CH, LANES), lambda b: (b, col + 1)),
            wide,
            wide,
            pl.BlockSpec((16, CH), lambda b: (0, b)),
            whole((1, inner)),
            whole((LANES, inner)),
        ],
        out_specs=[
            pl.BlockSpec((CH, inner), lambda b: (b, 0)),
            pl.BlockSpec((1, LANES, inner), lambda b: (b, 0, 0)),
            whole((LANES, inner)),
        ],
        out_shape=[
            jax.ShapeDtypeStruct((rows, inner), F32),
            jax.ShapeDtypeStruct((blocks, LANES, inner), F32),
            jax.ShapeDtypeStruct((LANES, inner), F32),
        ],
        scratch_shapes=[pltpu.VMEM((LANES, inner), F32)],
        compiler_params=params(),
        cost_estimate=cost(6 * rows * CH * inner, 12 * rows * inner, rows * CH * heads),
    )(act, act, act, dt, cum, cum_t, skip, onehot)


def gate_kernel(normed, grad, w_gate, w_out, y_in, cm, seq, state, gain, onehot, gate_ref, y_ref, gon_ref, stat_ref):
    gate = dot_nn(normed[...], w_gate[...])
    grad_on = dot_nn(grad[...], w_out[...])
    y = y_in[...] + by_heads(jnp.exp(seq[...]), onehot[...]) * dot_nn(cm[...], state[...])
    gated = y * (gate * sigmoid(gate))
    gate_ref[...] = gate
    y_ref[...] = y
    gon_ref[...] = grad_on
    square = jnp.sum(gated * gated, axis=1, keepdims=True)
    inner = jnp.sum(grad_on * gain[...] * gated, axis=1, keepdims=True)
    lane = lax.broadcasted_iota(jnp.int32, (gate.shape[0], LANES), 1)
    both = jnp.where(lane == 0, square, jnp.where(lane == 1, inner, 0.0))
    stat_ref[...] = jnp.transpose(both)[0:8, :]


def gate_stage(normed, grad, w_rest, y_in, act, seq, state, gain, onehot):
    rows, dim = normed.shape
    inner = onehot.shape[1]
    col = inner // LANES
    block = pl.BlockSpec((CH, inner), lambda b: (b, 0))
    full = jax.ShapeDtypeStruct((rows, inner), F32)
    return pl.pallas_call(
        gate_kernel,
        name="gate_stage",
        grid=(rows // CH,),
        in_specs=[
            pl.BlockSpec((CH, dim), lambda b: (b, 0)),
            pl.BlockSpec((CH, dim), lambda b: (b, 0)),
            pl.BlockSpec((dim, inner), lambda b: (0, 0)),
            pl.BlockSpec((dim, inner), lambda b: (0, 1)),
            block,
            pl.BlockSpec((CH, LANES), lambda b: (b, col + 1)),
            pl.BlockSpec((CH, LANES), lambda b: (b, 0)),
            whole((LANES, inner)),
            whole((1, inner)),
            whole((LANES, inner)),
        ],
        out_specs=[block, block, block, pl.BlockSpec((8, CH), lambda b: (0, b))],
        out_shape=[full, full, full, jax.ShapeDtypeStruct((8, rows), F32)],
        compiler_params=params(),
        cost_estimate=cost(4 * rows * dim * inner, 16 * rows * inner + 4 * rows * dim, rows * inner),
    )(normed, grad, w_rest, w_rest, y_in, act, seq, state, gain, onehot)


def back_order(i):
    return jnp.where(i < 2, 2 + i, 3 - i)


def norm_kernel(
    inner_all, place, gate_ref, y_ref, gon_ref, stat, w_out, cm, cum, seq, gain, onehot,
    send, keep, out_in_ref, gy_ref, ggate_ref, gog, gstart, gin, gin_sum,
):
    step = pl.program_id(0)

    @pl.when(step == 0)
    def _():
        gog[...] = jnp.zeros_like(gog)
        gin_sum[...] = jnp.zeros_like(gin_sum)

    columns = jnp.transpose(jnp.concatenate([stat[...]] * (LANES // 8), axis=0))
    scale = lax.rsqrt(columns[:, 0:1] * (1.0 / inner_all) + EPSILON)
    along = columns[:, 1:2] * (1.0 / inner_all)
    gate, y, grad_on = gate_ref[...], y_ref[...], gon_ref[...]
    sig = sigmoid(gate)
    silu = gate * sig
    gated = y * silu
    normed = gated * scale
    out_in = (normed * gain[...]).astype(BF16)
    out_in_ref[...] = out_in
    mixed = dot_nt(out_in, w_out[...]).astype(BF16)

    @pl.when(step < 2)
    def _():
        send[...] = mixed

    @pl.when(step >= 2)
    def _():
        keep[...] = mixed

    gog[...] += fold_rows(grad_on * normed)
    grad_gated = scale * (grad_on * gain[...]) - gated * (scale * scale * scale * along)
    grad_y = (grad_gated * silu).astype(BF16)
    gy_ref[...] = grad_y
    ggate_ref[...] = (grad_gated * y * (sig * (1.0 + gate * (1.0 - sig)))).astype(BF16)
    hot = onehot[...]
    scaled = (grad_y.astype(F32) * by_heads(jnp.exp(cum[...]), hot)).astype(BF16)
    grad_start = dot_tn(cm[...], scaled)
    gstart[0] = grad_start
    rows = gate.shape[0]
    ahead = seq[rows - 1 : rows, :] - cum[rows - 1 : rows, :]
    gin_sum[...] += row_of(jnp.exp(ahead), hot) * grad_start
    gin[...] = gin_sum[...].astype(BF16)


def norm_stage(place, gate, y, grad_on, stat, w_rest, act, cum, seq, gain, onehot, inner_all):
    rows, inner = gate.shape
    dim = w_rest.shape[0]
    col = inner // LANES
    blocks = rows // CH
    at = lambda i, q: back_order(i) ^ q[0]
    block = pl.BlockSpec((CH, inner), lambda i, q: (at(i, q), 0))
    wide = pl.BlockSpec((CH, LANES), lambda i, q: (at(i, q), 0))
    low = jax.ShapeDtypeStruct((rows, inner), BF16)
    half = jax.ShapeDtypeStruct((rows // 2, dim), BF16)
    return pl.pallas_call(
        functools.partial(norm_kernel, inner_all),
        name="norm_stage",
        grid_spec=pltpu.PrefetchScalarGridSpec(
            num_scalar_prefetch=1,
            grid=(blocks,),
            in_specs=[
                block,
                block,
                block,
                pl.BlockSpec((8, CH), lambda i, q: (0, at(i, q))),
                pl.BlockSpec((dim, inner), lambda i, q: (0, 1)),
                pl.BlockSpec((CH, LANES), lambda i, q: (at(i, q), col + 1)),
                wide,
                wide,
                whole((1, inner)),
                whole((LANES, inner)),
            ],
            out_specs=[
                pl.BlockSpec((CH, dim), lambda i, q: (jnp.minimum(i, 1), 0)),
                pl.BlockSpec((CH, dim), lambda i, q: (jnp.minimum(3 - i, 1), 0)),
                block,
                block,
                block,
                whole((8, inner)),
                pl.BlockSpec((1, LANES, inner), lambda i, q: (at(i, q), 0, 0)),
                whole((LANES, inner)),
            ],
            scratch_shapes=[pltpu.VMEM((LANES, inner), F32)],
        ),
        out_shape=[
            half,
            half,
            low,
            low,
            low,
            jax.ShapeDtypeStruct((8, inner), F32),
            jax.ShapeDtypeStruct((blocks, LANES, inner), F32),
            jax.ShapeDtypeStruct((LANES, inner), BF16),
        ],
        compiler_params=params(),
        cost_estimate=cost(2 * rows * dim * inner, 18 * rows * inner + 4 * rows * dim, rows * inner),
    )(place, gate, y, grad_on, stat, w_rest, act, cum, seq, gain, onehot)


def early_kernel(grad_t, out_in, normed_t, ggate, out):
    inner = out_in.shape[1]
    out[:, 0:inner] = dot_nn(grad_t[...], out_in[...]).astype(BF16)
    out[:, inner:] = dot_nn(normed_t[...], ggate[...]).astype(BF16)


def early_grads(grad_t, out_in, normed_t, ggate):
    dim, rows = grad_t.shape
    inner = out_in.shape[1]
    tile = dim // 4
    return pl.pallas_call(
        early_kernel,
        name="early_grads",
        grid=(4,),
        in_specs=[
            pl.BlockSpec((tile, rows), lambda i: (i, 0)),
            whole((rows, inner)),
            pl.BlockSpec((tile, rows), lambda i: (i, 0)),
            whole((rows, inner)),
        ],
        out_specs=pl.BlockSpec((tile, 2 * inner), lambda i: (i, 0)),
        out_shape=jax.ShapeDtypeStruct((dim, 2 * inner), BF16),
        compiler_params=params(),
        cost_estimate=cost(4 * rows * dim * inner, 4 * dim * (rows + inner) + 4 * rows * inner, 0),
    )(grad_t, out_in, normed_t, ggate)


def lower_decay(mask, cum, cum_t, h):
    gap = jnp.where(mask, cum[:, h : h + 1] - cum_t[h : h + 1, :], 0.0)
    return jnp.where(mask, jnp.exp(gap), 0.0)


def scores_back_kernel(
    heads, xa_ref, bm_ref, cm_ref, gy_ref, dt_ref, cum_ref, seq_ref, cum_t_ref, last_ref,
    start_ref, in_state, gstart, gin, onehot, gbm_ref, gcm_ref, after_ref, after,
):
    step = pl.program_id(0)
    blocks = gstart.shape[0]
    hot = onehot[...]

    @pl.when(step == 0)
    def _():
        decays = by_heads(jnp.exp(last_ref[...]), hot)
        running = gin[...].astype(F32)
        for b in reversed(range(blocks)):
            after[b] = running
            running = gstart[b] + decays[b : b + 1, :] * running

    cum, cum_t = cum_ref[...], cum_t_ref[...]
    bm, cm, gy = bm_ref[...], cm_ref[...], gy_ref[...]
    rows = cum.shape[0]
    last = cum[rows - 1 : rows, :]
    ahead = seq_ref[rows - 1 : rows, :] - last
    start = start_ref[0] + row_of(jnp.exp(ahead), hot) * in_state[...].astype(F32)
    grad_after = after[step]
    after_ref[0] = grad_after
    x_dt = xa_ref[...].astype(F32) * by_heads(dt_ref[...], hot)
    x_low = x_dt.astype(BF16)
    mask = lax.broadcasted_iota(jnp.int32, (rows, rows), 0) >= lax.broadcasted_iota(jnp.int32, (rows, rows), 1)
    width = x_low.shape[1] // heads
    per = LANES // width
    lane = lax.broadcasted_iota(jnp.int32, (rows, LANES), 1) // width
    grad_scores = jnp.zeros((rows, rows), F32)
    for group in range(heads // per):
        at = slice(group * LANES, (group + 1) * LANES)
        x_group, gy_group = x_low[:, at], gy[:, at]
        for k in range(per):
            decay = lower_decay(mask, cum, cum_t, group * per + k)
            gy_head = jnp.where(lane == k, gy_group, jnp.zeros_like(gy_group))
            grad_scores = grad_scores + dot_nt(gy_head, x_group) * decay
    to_end = (x_dt * by_heads(jnp.exp(last - cum), hot)).astype(BF16)
    gy_scaled = (gy.astype(F32) * by_heads(jnp.exp(cum), hot)).astype(BF16)
    scores_low = grad_scores.astype(BF16)
    gbm_ref[...] = (dot_tn(scores_low, cm) + dot_nt(to_end, grad_after.astype(BF16))).astype(BF16)
    gcm_ref[...] = (dot_nn(scores_low, bm) + dot_nt(gy_scaled, start.astype(BF16))).astype(BF16)


def scores_backward(act, gy, dt, cum, seq, cum_t, lasts, starts, in_state, gstart, gin, onehot, heads):
    rows, inner = gy.shape
    col = inner // LANES
    blocks = rows // CH
    block = pl.BlockSpec((CH, inner), lambda b: (b, 0))
    wide = pl.BlockSpec((CH, LANES), lambda b: (b, 0))
    state = pl.BlockSpec((1, LANES, inner), lambda b: (b, 0, 0))
    return pl.pallas_call(
        functools.partial(scores_back_kernel, heads),
        name="scores_backward",
        grid=(blocks,),
        in_specs=[
            block,
            pl.BlockSpec((CH, LANES), lambda b: (b, col)),
            pl.BlockSpec((CH, LANES), lambda b: (b, col + 1)),
            block,
            wide,
            wide,
            wide,
            pl.BlockSpec((16, CH), lambda b: (0, b)),
            whole((8, LANES)),
            state,
            whole((LANES, inner)),
            whole((blocks, LANES, inner)),
            whole((LANES, inner)),
            whole((LANES, inner)),
        ],
        out_specs=[wide, wide, state],
        out_shape=[
            jax.ShapeDtypeStruct((rows, LANES), BF16),
            jax.ShapeDtypeStruct((rows, LANES), BF16),
            jax.ShapeDtypeStruct((blocks, LANES, inner), F32),
        ],
        scratch_shapes=[pltpu.VMEM((blocks, LANES, inner), F32)],
        compiler_params=params(),
        cost_estimate=cost(6 * rows * CH * inner, 10 * rows * inner, rows * CH * heads),
    )(act, act, act, gy, dt, cum, seq, cum_t, lasts, starts, in_state, gstart, gin, onehot)


def ssd_back_kernel(
    heads, offset, xa_ref, bm_ref, cm_ref, gy_ref, y_ref, dt_ref, sig_ref, cum_ref, seq_ref, cum_t_ref,
    start_ref, in_state, after_ref, pre_ref, taps, rate, skip, onehot, *rest,
):
    gconv_ref, graw_ref, head_ref, rows_sum, heads_sum, gx = rest[-6:]
    step = pl.program_id(0)
    hot = onehot[...]

    @pl.when(step == 0)
    def _():
        rows_sum[...] = jnp.zeros_like(rows_sum)
        heads_sum[...] = jnp.zeros_like(heads_sum)

    cum, cum_t, dt = cum_ref[...], cum_t_ref[...], dt_ref[...]
    bm, cm = bm_ref[...], cm_ref[...]
    rows = cum.shape[0]
    last = cum[rows - 1 : rows, :]
    ahead = seq_ref[rows - 1 : rows, :] - last
    start = start_ref[0] + row_of(jnp.exp(ahead), hot) * in_state[...].astype(F32)
    grad_after = after_ref[0]

    gy = gy_ref[...]
    xa = xa_ref[...].astype(F32)
    dt_wide = by_heads(dt, hot)
    x_dt = xa * dt_wide
    x_low = x_dt.astype(BF16)
    scores = dot_nt(cm, bm)
    mask = lax.broadcasted_iota(jnp.int32, (rows, rows), 0) >= lax.broadcasted_iota(jnp.int32, (rows, rows), 1)
    width = xa.shape[1] // heads
    per = LANES // width
    lane = lax.broadcasted_iota(jnp.int32, (rows, LANES), 1) // width
    for group in range(heads // per):
        at = slice(group * LANES, (group + 1) * LANES)
        gy_group = gy[:, at]
        total = jnp.zeros((rows, LANES), F32)
        for k in range(per):
            weights = (lower_decay(mask, cum, cum_t, group * per + k) * scores).astype(BF16)
            total = total + dot_tn(weights, jnp.where(lane == k, gy_group, jnp.zeros_like(gy_group)))
        gx[:, at] = total

    end_wide = by_heads(jnp.exp(last - cum), hot)
    from_end = dot_nn(bm, grad_after.astype(BF16))
    to_end = (x_dt * end_wide).astype(BF16)
    gx_intra = gx[...]
    gx_all = gx_intra + end_wide * from_end
    end_term = to_end.astype(F32) * from_end
    gy_f = gy.astype(F32)
    grad_xa = dt_wide * gx_all + skip[...] * gy_f

    grad_dt = by_heads_t(xa * gx_all, hot)
    grad_cum = by_heads_t(
        gy_f * (y_ref[...] - skip[...] * xa) - x_low.astype(F32) * gx_intra - end_term, hot
    )
    end_rows = fold_rows(end_term)
    state_rows = fold_rows(grad_after * start) * row_of(jnp.exp(last), hot)
    grad_last = jnp.sum(by_heads_t(end_rows + state_rows, hot), axis=0, keepdims=True)
    upper = (
        lax.broadcasted_iota(jnp.int32, (rows, rows), 0) <= lax.broadcasted_iota(jnp.int32, (rows, rows), 1)
    ).astype(BF16)
    grad_a = jnp.broadcast_to(grad_last, grad_cum.shape)
    for part in exact_parts(grad_cum):
        grad_a = grad_a + dot_nn(upper, part)
    grad_raw = (grad_dt + rate[...] * grad_a) * sig_ref[...]
    graw_ref[...] = grad_raw.astype(BF16)
    heads_sum[0:8, :] += fold_rows(grad_raw)
    heads_sum[8:16, :] += fold_rows(grad_a * dt * rate[...])

    tap_count = 4
    first = HALO - tap_count + 1
    base = pl.multiple_of((step + offset) * rows, rows)
    window = pre_ref[pl.ds(base, rows + HALO), :]
    conv = taps[tap_count : tap_count + 1, :] + taps[0:1, :] * window[first : first + rows]
    for k in range(1, tap_count):
        conv = conv + taps[k : k + 1, :] * window[first + k : first + k + rows]
    sig = sigmoid(conv)
    gconv = grad_xa * (sig * (1.0 + conv * (1.0 - sig)))
    gconv_ref[...] = gconv

    @pl.when(step == 0)
    def _():
        head_ref[...] = gconv[0:HALO, :]

    for k in range(tap_count):
        rows_sum[8 * k : 8 * k + 8, :] += fold_rows(gconv * window[first + k : first + k + rows])
    rows_sum[8 * tap_count : 8 * tap_count + 8, :] += fold_rows(gconv)
    rows_sum[8 * tap_count + 8 : 8 * tap_count + 16, :] += fold_rows(gy_f * xa)


def ssd_backward(
    act, gy, y, dt, sig, cum, seq, cum_t, starts, in_state, after, pre, taps, rate, skip, onehot, heads,
    offset, count, into,
):
    rows, inner = gy.shape
    col = inner // LANES
    block = pl.BlockSpec((CH, inner), lambda b: (b + offset, 0))
    wide = pl.BlockSpec((CH, LANES), lambda b: (b + offset, 0))
    state = pl.BlockSpec((1, LANES, inner), lambda b: (b + offset, 0, 0))
    operands = [act, act, act, gy, y, dt, sig, cum, seq, cum_t, starts, in_state, after, pre, taps, rate, skip, onehot]
    specs = [
        block,
        pl.BlockSpec((CH, LANES), lambda b: (b + offset, col)),
        pl.BlockSpec((CH, LANES), lambda b: (b + offset, col + 1)),
        block,
        block,
        wide,
        wide,
        wide,
        wide,
        pl.BlockSpec((16, CH), lambda b: (0, b + offset)),
        state,
        whole((LANES, inner)),
        state,
        pl.BlockSpec((rows + HALO, inner), lambda b: (0, 0)),
        pl.BlockSpec((8, inner), lambda b: (0, 0)),
        whole((1, LANES)),
        whole((1, inner)),
        whole((LANES, inner)),
    ]
    aliases = {}
    if into is not None:
        aliases = {len(operands): 0, len(operands) + 1: 1}
        operands += list(into)
        specs += [pl.BlockSpec(memory_space=pl.ANY)] * 2
    part = CH * count
    return pl.pallas_call(
        functools.partial(ssd_back_kernel, heads, offset),
        name="ssd_backward",
        grid=(count,),
        in_specs=specs,
        out_specs=[block, wide, whole((HALO, inner)), whole((48, inner)), whole((16, LANES))],
        out_shape=[
            jax.ShapeDtypeStruct((rows, inner), F32),
            jax.ShapeDtypeStruct((rows, LANES), BF16),
            jax.ShapeDtypeStruct((HALO, inner), F32),
            jax.ShapeDtypeStruct((48, inner), F32),
            jax.ShapeDtypeStruct((16, LANES), F32),
        ],
        input_output_aliases=aliases,
        scratch_shapes=[pltpu.VMEM((CH, inner), F32)],
        compiler_params=params(),
        cost_estimate=cost(8 * part * CH * inner, 24 * part * inner, part * CH * heads),
    )(*operands)


def bc_kernel(side, grad, pre_ref, taps, gconv_ref, tap_sum):
    tap_count = 4
    rows = grad.shape[0]
    first = HALO - tap_count + 1
    conv = taps[tap_count : tap_count + 1, :] + taps[0:1, :] * pre_ref[first : first + rows, :]
    for k in range(1, tap_count):
        conv = conv + taps[k : k + 1, :] * pre_ref[first + k : first + k + rows, :]
    sig = sigmoid(conv)
    gconv = grad[...] * (sig * (1.0 + conv * (1.0 - sig)))
    gconv_ref[...] = gconv
    for k in range(tap_count):
        tap_sum[8 * k : 8 * k + 8, :] = fold_rows(gconv * pre_ref[first + k : first + k + rows, :])
    tap_sum[8 * tap_count : 8 * tap_count + 8, :] = fold_rows(gconv)


def bc_backward(side, grad, pre, taps, col):
    rows = grad.shape[0]
    return pl.pallas_call(
        bc_kernel,
        name="bc_backward",
        grid_spec=pltpu.PrefetchScalarGridSpec(
            num_scalar_prefetch=1,
            grid=(1,),
            in_specs=[
                pl.BlockSpec((rows, LANES), lambda i, s: (0, 0)),
                pl.BlockSpec((rows + HALO, LANES), lambda i, s: (0, col + s[0])),
                pl.BlockSpec((8, LANES), lambda i, s: (0, col + s[0])),
            ],
            out_specs=[
                pl.BlockSpec((rows, LANES), lambda i, s: (0, 0)),
                pl.BlockSpec((40, LANES), lambda i, s: (0, 0)),
            ],
        ),
        out_shape=[
            jax.ShapeDtypeStruct((rows, LANES), F32),
            jax.ShapeDtypeStruct((40, LANES), F32),
        ],
        compiler_params=params(),
        cost_estimate=cost(30 * rows * LANES, 16 * rows * LANES, rows * LANES),
    )(side, grad, pre, taps)


def conv_transpose(grad_ref, next_ref, halo_ref, taps, ext, at_end):
    tap_count = 4
    rows = grad_ref.shape[0]
    ext[0:rows, :] = grad_ref[...]
    ext[rows:, :] = jnp.where(at_end, halo_ref[...], next_ref[...])
    total = taps[tap_count - 1 : tap_count, :] * ext[0:rows, :]
    for k in range(tap_count - 1):
        ahead = tap_count - 1 - k
        total = total + taps[k : k + 1, :] * ext[ahead : ahead + rows, :]
    return total.astype(BF16)


def input_kernel(
    share, where, gx_ref, gx_next, gx_halo, gb_ref, gb_next, gb_halo, taps_x, taps_b, ggate, graw,
    w_gate, w_x, w_b, w_dt, send, keep, gcat_a, gcat_b, ext_x, ext_b,
):
    step = pl.program_id(0)
    at_end = (back_order(step) ^ where[0]) == pl.num_programs(0) - 1
    gpre_x = conv_transpose(gx_ref, gx_next, gx_halo, taps_x, ext_x, at_end)
    gpre_b = conv_transpose(gb_ref, gb_next, gb_halo, taps_b, ext_b, at_end)
    cut = gcat_a.shape[1]
    gcat_a[...] = gpre_x[:, :cut]
    rest = gpre_x.shape[1] - cut
    gcat_b[:, 0:rest] = gpre_x[:, cut:]
    gcat_b[:, rest:] = gpre_b
    total = dot_nt(ggate[...], w_gate[...]) + dot_nt(gpre_x, w_x[...])
    total = total + dot_nt(graw[...], w_dt[...]) + share * dot_nt(gpre_b, w_b[...])
    part = total.astype(BF16)

    @pl.when(step < 2)
    def _():
        send[...] = part

    @pl.when(step >= 2)
    def _():
        keep[...] = part


def input_stage(where, gx, gx_halo, gb, gb_halo, taps, ggate, graw, w_rest, w_first, share):
    rows, inner = gx.shape
    dim = w_rest.shape[0]
    col = inner // LANES
    per = CH // HALO
    top = rows // HALO - 1
    blocks = rows // CH
    at = lambda i, q: back_order(i) ^ q[0]
    nxt = lambda i, q: (jnp.minimum(per * (at(i, q) + 1), top), 0)
    cut = 4 * LANES
    half = jax.ShapeDtypeStruct((rows // 2, dim), BF16)
    return pl.pallas_call(
        functools.partial(input_kernel, share),
        name="input_stage",
        grid_spec=pltpu.PrefetchScalarGridSpec(
            num_scalar_prefetch=1,
            grid=(blocks,),
            in_specs=[
                pl.BlockSpec((CH, inner), lambda i, q: (at(i, q), 0)),
                pl.BlockSpec((HALO, inner), nxt),
                pl.BlockSpec((HALO, inner), lambda i, q: (0, 0)),
                pl.BlockSpec((CH, LANES), lambda i, q: (at(i, q), 0)),
                pl.BlockSpec((HALO, LANES), nxt),
                pl.BlockSpec((HALO, LANES), lambda i, q: (0, 0)),
                pl.BlockSpec((8, inner), lambda i, q: (0, 0)),
                pl.BlockSpec((8, LANES), lambda i, q: (0, col + q[1])),
                pl.BlockSpec((CH, inner), lambda i, q: (at(i, q), 0)),
                pl.BlockSpec((CH, LANES), lambda i, q: (at(i, q), 0)),
                pl.BlockSpec((dim, inner), lambda i, q: (0, 0)),
                pl.BlockSpec((dim, inner), lambda i, q: (0, 0)),
                pl.BlockSpec((dim, LANES), lambda i, q: (0, col + q[1])),
                pl.BlockSpec((dim, LANES), lambda i, q: (0, col + 2)),
            ],
            out_specs=[
                pl.BlockSpec((CH, dim), lambda i, q: (jnp.minimum(i, 1), 0)),
                pl.BlockSpec((CH, dim), lambda i, q: (jnp.minimum(3 - i, 1), 0)),
                pl.BlockSpec((CH, cut), lambda i, q: (at(i, q), 0)),
                pl.BlockSpec((CH, inner + LANES - cut), lambda i, q: (at(i, q), 0)),
            ],
            scratch_shapes=[pltpu.VMEM((CH + HALO, inner), F32), pltpu.VMEM((CH + HALO, LANES), F32)],
        ),
        out_shape=[
            half,
            half,
            jax.ShapeDtypeStruct((rows, cut), BF16),
            jax.ShapeDtypeStruct((rows, inner + LANES - cut), BF16),
        ],
        compiler_params=params(),
        cost_estimate=cost(4 * rows * dim * inner, 10 * rows * inner + 2 * rows * dim, 0),
    )(where, gx, gx, gx_halo, gb, gb, gb_halo, taps, taps, ggate, graw, w_rest, w_first, w_first, w_first)


def late_kernel(side, normed_t, gcat, keep, send):
    result = dot_nn(normed_t[...], gcat[...]).astype(BF16)
    rows = result.shape[0] // 2
    top, bottom = result[:rows], result[rows:]
    first = side[0] == 0
    keep[0] = jnp.where(first, top, bottom)
    send[0] = jnp.where(first, bottom, top)


def late_grads(side, normed_t, gcat, shards):
    dim, rows = normed_t.shape
    width = gcat.shape[1]
    tile = dim // shards
    half = pl.BlockSpec((1, tile // 2, width), lambda i, q: (i, 0, 0))
    shape = jax.ShapeDtypeStruct((shards, tile // 2, width), BF16)
    return pl.pallas_call(
        late_kernel,
        name="late_grads",
        grid_spec=pltpu.PrefetchScalarGridSpec(
            num_scalar_prefetch=1,
            grid=(shards,),
            in_specs=[
                pl.BlockSpec((tile, rows), lambda i, q: (i, 0)),
                pl.BlockSpec((rows, width), lambda i, q: (0, 0)),
            ],
            out_specs=[half, half],
        ),
        out_shape=[shape, shape],
        compiler_params=params(),
        cost_estimate=cost(2 * rows * dim * width, 2 * dim * (rows + width) + 2 * rows * width, 0),
    )(side, normed_t, gcat)


def on_device(
    hidden_in,
    norm_gain,
    w_in_zx,
    w_in_bc,
    w_in_dt,
    conv_x,
    conv_bc,
    dt_bias,
    a_log,
    d_skip,
    out_gain,
    w_out,
    cotangent,
):
    seq_count, rows, dim = hidden_in.shape
    inner = w_in_zx.shape[2]
    heads = w_in_dt.shape[1]
    head_dim = inner // heads
    tap_count = conv_x.shape[0] - 1
    tensor_size, shards, contexts = lax.axis_size("tensor"), lax.axis_size("shard"), lax.axis_size("context")
    inner_all = inner * tensor_size
    blocks = rows // CH
    assert seq_count == 1 and tensor_size == 4 and blocks == 4 and contexts == 2
    shard_rows = w_in_zx.shape[0]
    place = lax.axis_index("tensor")
    context = lax.axis_index("context")
    side_num = place % 2
    quarter = side_num * 2 + place // 2
    where = jnp.stack([quarter, side_num]).astype(jnp.int32)
    col = inner // LANES

    x_rows = hidden_in.reshape(rows, dim)
    g_rows = cotangent.reshape(rows, dim)

    pad_dt = jnp.zeros((shard_rows, LANES - heads), BF16)
    w_front = jnp.concatenate([w_in_zx[:, 1], w_in_bc, w_in_dt, pad_dt], axis=1)
    w_back = jnp.concatenate([w_in_zx[:, 0], w_out.T], axis=1)
    half_rows = shard_rows // contexts
    w_rest = lax.all_gather(
        lax.dynamic_slice_in_dim(w_back, context * half_rows, half_rows, 0), ("shard", "context"), axis=0, tiled=True
    )
    w_first = gather_weights(w_front)
    halo_rows = shifted(x_rows[rows - HALO :], "context", 1)

    def norm_of(values):
        wide = values.astype(F32)
        scale = lax.rsqrt(jnp.mean(wide * wide, axis=-1, keepdims=True) + EPSILON)
        return (wide * scale * norm_gain).astype(BF16)

    normed = norm_of(x_rows)
    halo = norm_of(halo_rows)
    normed_t = normed.T
    grad_t = g_rows.T

    pad_heads = lambda v: jnp.pad(v, (0, LANES - heads)).reshape(1, LANES)
    rate = pad_heads(-jnp.exp(a_log))
    bias = pad_heads(dt_bias)
    skip = jnp.repeat(d_skip, head_dim).reshape(1, inner)
    gain = out_gain.reshape(1, inner)
    taps = jnp.pad(jnp.concatenate([conv_x, conv_bc], axis=1), ((0, 8 - tap_count - 1), (0, 0)))
    onehot = (
        lax.broadcasted_iota(jnp.int32, (LANES, inner), 0)
        == lax.broadcasted_iota(jnp.int32, (LANES, inner), 1) // head_dim
    ).astype(BF16)

    dt, sig, cum, seq, cum_t = step_sizes(normed, w_first, bias, rate, col + 2)
    act, pre = conv_front(normed, halo, w_first, taps)
    y_local, starts, end_state = ssd_forward(act, dt, cum, cum_t, skip, onehot, heads)
    lasts = jnp.pad(cum.reshape(blocks, CH, LANES)[:, CH - 1], ((0, 8 - blocks), (0, 0)))
    in_state = shifted(end_state.astype(BF16), "context", 1)

    gate, y, grad_on, stat = gate_stage(normed, g_rows, w_rest, y_local, act, seq, in_state, gain, onehot)
    stat = butterfly(stat, "tensor")
    send, keep, out_in, gy, ggate, gog, gstart, gin_first = norm_stage(
        where, gate, y, grad_on, stat, w_rest, act, cum, seq, gain, onehot, inner_all
    )
    gin = shifted(gin_first, "context", -1)

    early = early_grads(grad_t, out_in, normed_t, ggate)
    early_share = lax.psum_scatter(early, ("shard", "context"), scatter_dimension=0, tiled=True).astype(F32)

    mixed_mine = reduce_mine(keep, send, tensor_size)
    own_rows = rows // 4
    x_mine = lax.dynamic_slice_in_dim(x_rows, quarter * own_rows, own_rows, 0).astype(F32)
    stream_mine = x_mine + mixed_mine
    square_sums = jnp.stack([jnp.sum(stream_mine * stream_mine), jnp.sum(mixed_mine * mixed_mine)])
    out = gather_quarters(stream_mine.astype(BF16), where, tensor_size, BF16)

    gy, gin, early = lax.optimization_barrier((gy, gin, early))
    gbm, gcm, after = scores_backward(
        act, gy, dt, cum, seq, cum_t, lasts, starts, in_state, gstart, gin, onehot, heads
    )
    core_send = jnp.where(side_num == 0, gcm, gbm)
    core_keep = jnp.where(side_num == 0, gbm, gcm)
    core_got = lax.ppermute(core_send, "tensor", swap_pairs(tensor_size, 1))
    state = (act, gy, y, dt, sig, cum, seq, cum_t, starts, in_state, after, pre, taps, rate, skip, onehot, heads)
    gconv, graw, head, rows_sum_a, heads_sum_a = ssd_backward(*state, 0, 2, None)
    gx_halo = shifted(head, "context", -1)
    core_got, gconv = lax.optimization_barrier((core_got, gconv))
    chip_low = (core_keep.astype(F32) + core_got.astype(F32)).astype(BF16)
    chip_got = lax.ppermute(chip_low, "tensor", swap_pairs(tensor_size, 2))
    gconv, chip_low = lax.optimization_barrier((gconv, chip_low))
    gconv, graw, _, rows_sum_b, heads_sum_b = ssd_backward(*state, 2, 2, (gconv, graw))
    bc_sum = chip_low.astype(F32) + chip_got.astype(F32)
    gconv_bc, tap_bc = bc_backward(where[1:], bc_sum, pre, taps, col)
    gb_halo = shifted(gconv_bc[:HALO], "context", -1)

    send, keep, gcat_a, gcat_b = input_stage(
        where, gconv, gx_halo, gconv_bc, gb_halo, taps, ggate, graw, w_rest, w_first, 2.0 / tensor_size
    )
    if shards <= 8:
        context_num = context.astype(jnp.int32).reshape(1)
        late_share = [
            scatter_grad(*late_grads(context_num, normed_t, piece, shards)) for piece in (gcat_a, gcat_b)
        ]
    else:
        late_share = [
            lax.psum_scatter(
                dot_nn(normed_t, piece).astype(BF16), ("shard", "context"), scatter_dimension=0, tiled=True
            ).astype(F32)
            for piece in (gcat_a, gcat_b)
        ]
    cut = inner - gcat_a.shape[1]

    grad_normed = reduce_mine(keep, send, tensor_size)
    scale_mine = lax.rsqrt(jnp.mean(x_mine * x_mine, axis=-1, keepdims=True) + EPSILON)
    g_mine = lax.dynamic_slice_in_dim(g_rows, quarter * own_rows, own_rows, 0).astype(F32)
    grad_ng = jnp.sum(grad_normed * x_mine * scale_mine, axis=0)
    grad_un = grad_normed * norm_gain
    grad_mine = (
        g_mine
        + scale_mine * grad_un
        - x_mine * scale_mine**3 * jnp.mean(grad_un * x_mine, axis=-1, keepdims=True)
    )
    grad_input = gather_quarters(grad_mine.astype(BF16), where, tensor_size, F32)

    grad_dt_t = dot_tn(graw[:, :16], normed)
    local = jnp.concatenate(
        [
            grad_dt_t.reshape(-1, inner),
            (rows_sum_a + rows_sum_b).reshape(6, 8, inner).sum(1),
            gog.sum(0, keepdims=True),
            jnp.pad((heads_sum_a + heads_sum_b).reshape(2, 8, LANES).sum(1), ((0, 0), (0, inner - LANES))),
        ],
        axis=0,
    )
    local = butterfly(butterfly(local, "context"), "shard")
    first = 16 * dim // inner
    grad_dt_all = local[:first].reshape(16, dim)
    local = local[first:]

    own_taps = jnp.pad(tap_bc.reshape(tap_count + 1, 8, LANES).sum(1), ((0, 3), (0, 0))) * (2.0 / tensor_size)
    nothing = jnp.zeros_like(own_taps)
    shared = jnp.concatenate(
        [
            grad_ng.reshape(-1, 2 * LANES),
            jnp.concatenate(
                [jnp.where(side_num == 0, own_taps, nothing), jnp.where(side_num == 0, nothing, own_taps)], axis=1
            ),
            jnp.pad(square_sums.reshape(1, 2), ((0, 7), (0, 2 * LANES - 2))),
        ],
        axis=0,
    )
    shared = butterfly(butterfly(butterfly(shared, "tensor"), "context"), "shard")
    ng_rows = dim // (2 * LANES)
    totals = shared[ng_rows + 8]
    entry_count = rows * dim * shards * contexts

    bc_mine = late_share[1][:, cut:]
    bc_other = lax.ppermute(bc_mine, "tensor", swap_pairs(tensor_size, 1))
    grad_wbc = jnp.concatenate(
        [jnp.where(side_num == 0, bc_mine, bc_other), jnp.where(side_num == 0, bc_other, bc_mine)], axis=1
    )
    own_features = (lax.axis_index("shard") * contexts + context) * half_rows
    return (
        out.reshape(hidden_in.shape),
        grad_input.reshape(hidden_in.shape),
        shared[:ng_rows].reshape(dim),
        jnp.stack(
            [early_share[:, inner:], jnp.concatenate([late_share[0], late_share[1][:, :cut]], axis=1)], axis=1
        ),
        grad_wbc,
        lax.dynamic_slice_in_dim(grad_dt_all, own_features, half_rows, 1)[:heads].T,
        local[: tap_count + 1],
        shared[ng_rows : ng_rows + tap_count + 1],
        local[tap_count + 3, :heads],
        local[tap_count + 4, :heads],
        local[tap_count + 1].reshape(heads, head_dim).sum(1),
        local[tap_count + 2],
        early_share[:, :inner].T,
        jnp.sqrt(totals[0] / entry_count),
        jnp.sqrt(totals[1] / entry_count),
    )


def solution(mesh):
    placed = (
        P("shard", "context", None),
        P(),
        P("shard", None, "tensor"),
        P("shard", None),
        P("shard", "tensor"),
        P(None, "tensor"),
        P(),
        P("tensor"),
        P("tensor"),
        P("tensor"),
        P("tensor"),
        P("tensor", "shard"),
        P("shard", "context", None),
    )
    return jax.shard_map(
        on_device,
        mesh=mesh,
        in_specs=placed,
        out_specs=(
            P("shard", "context", None),
            P("shard", "context", None),
            P(),
            P(("shard", "context"), None, "tensor"),
            P(("shard", "context"), None),
            P(("shard", "context"), "tensor"),
            P(None, "tensor"),
            P(),
            P("tensor"),
            P("tensor"),
            P("tensor"),
            P("tensor"),
            P("tensor", ("shard", "context")),
            P(),
            P(),
        ),
        check_vma=False,
    )
```

```python
import functools

import jax
import jax.numpy as jnp
from jax import lax
from jax.experimental import pallas as pl
from jax.experimental.pallas import tpu as pltpu
from jax.sharding import PartitionSpec as P

CH = 256
EPSILON = 1e-05
LANES = 128
HALO = 8
F32 = jnp.float32
BF16 = jnp.bfloat16


def swap_pairs(size, by):
    return [(i, i ^ by) for i in range(size)]


def butterfly(value, axis):
    size = lax.axis_size(axis)
    if size & (size - 1):
        return lax.psum(value, axis)
    by = 1
    while by < size:
        value = value + lax.ppermute(value, axis, swap_pairs(size, by))
        by *= 2
    return value


def shifted(array, axis, by):
    length = lax.axis_size(axis)
    pairs = [(i, i + by) for i in range(length) if 0 <= i + by < length]
    return lax.ppermute(array, axis, pairs)


def joint_pairs(size, context, sources, move):
    return [(i * context + c, move(i, c)[0] * context + move(i, c)[1]) for i in sources for c in range(context)]


class Gather:
    def __init__(self, local):
        self.shards, self.here, self.side = lax.axis_size("shard"), lax.axis_index("shard"), lax.axis_index("context")
        self.rows = local.shape[0] // 2
        self.local = local
        self.plus = self.minus = lax.dynamic_slice_in_dim(local, self.side * self.rows, self.rows, 0)
        self.k = 0
        self.pieces, self.places = [], []

    def step(self):
        self.k += 1
        size = self.shards
        self.plus = lax.ppermute(self.plus, "shard", [(i, i + 1) for i in range(self.k - 1, size - 1)])
        self.minus = lax.ppermute(self.minus, "shard", [(i, i - 1) for i in range(1, size - self.k + 1)])

    def add(self, piece, valid, source, side):
        self.pieces.append(piece)
        self.places.append(jnp.where(valid, source * 2 + side, -1))

    def cross(self):
        k, size = self.k, self.shards
        axes = ("shard", "context")
        across_plus = lax.ppermute(self.plus, axes, joint_pairs(size, 2, range(k, size), lambda i, c: (i, 1 - c)))
        across_minus = lax.ppermute(self.minus, axes, joint_pairs(size, 2, range(0, size - k), lambda i, c: (i, 1 - c)))
        for piece, side in ((self.plus, self.side), (across_plus, 1 - self.side)):
            self.add(piece, self.here >= k, self.here - k, side)
        for piece, side in ((self.minus, self.side), (across_minus, 1 - self.side)):
            self.add(piece, self.here + k < size, self.here + k, side)

    def full(self):
        place = jnp.stack([self.here * 2] + self.places).astype(jnp.int32)
        rows, cols = self.rows, self.local.shape[1]
        count = len(self.pieces)
        total = 2 * self.shards * rows
        return pl.pallas_call(
            layout_kernel,
            name="layout",
            grid_spec=pltpu.PrefetchScalarGridSpec(
                num_scalar_prefetch=1,
                grid=(1,),
                in_specs=[pl.BlockSpec((2 * rows, cols), lambda i, q: (0, 0))]
                + [pl.BlockSpec((rows, cols), lambda i, q: (0, 0))] * count,
                out_specs=pl.BlockSpec((total, cols), lambda i, q: (0, 0)),
            ),
            out_shape=jax.ShapeDtypeStruct((total, cols), self.local.dtype),
            compiler_params=params(),
            cost_estimate=cost(0, 2 * (2 * total + count * rows) * cols, 0),
        )(place, self.local, *self.pieces)


def layout_kernel(place, local, *rest):
    out = rest[-1]
    rows = rest[0].shape[0]
    out[pl.ds(pl.multiple_of(place[0] * rows, rows), 2 * rows), :] = local[...]
    for k, piece in enumerate(rest[:-1]):

        @pl.when(place[k + 1] >= 0)
        def _():
            out[pl.ds(pl.multiple_of(place[k + 1] * rows, rows), rows), :] = piece[...]


class LineSum:
    def __init__(self, keep, got):
        self.shards, self.here = lax.axis_size("shard"), lax.axis_index("shard")
        self.summed = (keep.astype(F32) + got.astype(F32)).astype(BF16)
        self.plus = self.minus = None
        self.k = 0

    def piece(self, at):
        return lax.dynamic_index_in_dim(self.summed, jnp.clip(at, 0, self.shards - 1), 0, False)

    def step(self):
        self.k += 1
        k, size = self.k, self.shards
        up, down = self.piece(self.here + size - k), self.piece(self.here - size + k)
        if self.plus is not None:
            up = (up.astype(F32) + self.plus.astype(F32)).astype(BF16)
            down = (down.astype(F32) + self.minus.astype(F32)).astype(BF16)
        self.plus = lax.ppermute(up, "shard", [(i, i + 1) for i in range(k)])
        self.minus = lax.ppermute(down, "shard", [(size - 1 - i, size - 2 - i) for i in range(k)])

    def result(self):
        return self.piece(self.here).astype(F32) + self.plus.astype(F32) + self.minus.astype(F32)


def together(*values):
    return lax.optimization_barrier(values)


def to_core(value):
    return lax.ppermute(value, "tensor", swap_pairs(lax.axis_size("tensor"), 1))


def to_chip(value):
    return lax.ppermute(value, "tensor", swap_pairs(lax.axis_size("tensor"), 2))


def add_low(a, b):
    return (a.astype(F32) + b.astype(F32)).astype(BF16)


def assemble_kernel(place, own, chip, core_a, core_b, out):
    r = pl.program_id(0)
    for k, ref in enumerate((own, chip, core_a, core_b)):

        @pl.when(r == k)
        def _():
            out[...] = ref[...].astype(out.dtype)


def assemble(mine, chip, core_a, core_b, place, dtype):
    rows, cols = mine.shape
    piece = pl.BlockSpec((rows, cols), lambda r, q: (0, 0))
    return pl.pallas_call(
        assemble_kernel,
        name="assemble",
        grid_spec=pltpu.PrefetchScalarGridSpec(
            num_scalar_prefetch=1,
            grid=(4,),
            in_specs=[piece] * 4,
            out_specs=pl.BlockSpec((rows, cols), lambda r, q: (r ^ q[0], 0)),
        ),
        out_shape=jax.ShapeDtypeStruct((4 * rows, cols), dtype),
        compiler_params=params(),
        cost_estimate=cost(0, 12 * rows * cols + 0, 0),
    )(place, mine, chip, core_a, core_b)


def dot_nn(a, b):
    return lax.dot_general(a, b, (((1,), (0,)), ((), ())), preferred_element_type=F32)


def dot_nt(a, b):
    return lax.dot_general(a, b, (((1,), (1,)), ((), ())), preferred_element_type=F32)


def dot_tn(a, b):
    return lax.dot_general(a, b, (((0,), (0,)), ((), ())), preferred_element_type=F32)


def by_heads(values, onehot):
    high = values.astype(BF16)
    low = (values - high.astype(F32)).astype(BF16)
    return dot_nn(high, onehot) + dot_nn(low, onehot)


def by_heads_t(values, onehot):
    high = values.astype(BF16)
    low = (values - high.astype(F32)).astype(BF16)
    return dot_nt(high, onehot) + dot_nt(low, onehot)


def row_of(values, onehot):
    return by_heads(jnp.broadcast_to(values, (8, values.shape[1])), onehot)[0:1]


def fold_rows(values):
    rows, cols = values.shape
    return jnp.sum(values.reshape(rows // 8, 8, cols), axis=0)


def exact_parts(values):
    high = values.astype(BF16)
    rest = values - high.astype(F32)
    mid = rest.astype(BF16)
    low = (rest - mid.astype(F32)).astype(BF16)
    return high, mid, low


def sigmoid(values):
    return 1.0 / (1.0 + jnp.exp(-values))


def whole(shape):
    zeros = (0,) * len(shape)
    return pl.BlockSpec(shape, lambda *_: zeros)


def params(semantics=("arbitrary",)):
    return pltpu.CompilerParams(dimension_semantics=semantics, vmem_limit_bytes=60 * 1024 * 1024)


def cost(flops, nbytes, exps=0):
    return pl.CostEstimate(flops=int(flops), bytes_accessed=int(nbytes), transcendentals=int(exps))


def conv_kernel(normed, halo, weight, taps, act, pre):
    rows = normed.shape[0]
    tap_count = 4
    w = weight[...]
    pre[0:HALO, :] = dot_nn(halo[...], w)
    pre[HALO:, :] = dot_nn(normed[...], w)
    first = HALO - tap_count + 1
    out = taps[tap_count : tap_count + 1, :] + taps[0:1, :] * pre[first : first + rows, :]
    for k in range(1, tap_count):
        out = out + taps[k : k + 1, :] * pre[first + k : first + k + rows, :]
    act[...] = (out * sigmoid(out)).astype(BF16)


def conv_front(normed, halo, weight, taps):
    rows, dim = normed.shape
    cols = taps.shape[1]
    tile = 256
    return pl.pallas_call(
        conv_kernel,
        name="conv_front",
        grid=(cols // tile,),
        in_specs=[
            whole((rows, dim)),
            whole((HALO, dim)),
            pl.BlockSpec((dim, tile), lambda j: (0, j)),
            pl.BlockSpec((8, tile), lambda j: (0, j)),
        ],
        out_specs=[
            pl.BlockSpec((rows, tile), lambda j: (0, j)),
            pl.BlockSpec((rows + HALO, tile), lambda j: (0, j)),
        ],
        out_shape=[
            jax.ShapeDtypeStruct((rows, cols), BF16),
            jax.ShapeDtypeStruct((rows + HALO, cols), F32),
        ],
        compiler_params=params(),
        cost_estimate=cost(2 * rows * dim * cols, 2 * (rows + cols) * dim + 6 * rows * cols, rows * cols),
    )(normed, halo, weight, taps)


def step_kernel(normed, weight, bias, rate, dt, sig, cum, seq, cum_t, before):
    @pl.when(pl.program_id(0) == 0)
    def _():
        before[...] = jnp.zeros_like(before)

    raw = dot_nn(normed[...], weight[...]) + bias[...]
    small = jnp.exp(-jnp.abs(raw))
    dt_val = jnp.maximum(raw, 0.0) + jnp.log1p(small)
    dt[...] = dt_val
    sig[...] = sigmoid(raw)
    rows = raw.shape[0]
    lower = (
        lax.broadcasted_iota(jnp.int32, (rows, rows), 0) >= lax.broadcasted_iota(jnp.int32, (rows, rows), 1)
    ).astype(BF16)
    total = jnp.zeros_like(raw)
    for part in exact_parts(dt_val * rate[...]):
        total = total + dot_nn(lower, part)
    cum[...] = total
    seq[...] = total + before[0:1, :]
    before[...] = before[...] + jnp.broadcast_to(total[rows - 1 : rows, :], before.shape)
    cum_t[...] = jnp.transpose(total)[0:16, :]


def step_sizes(normed, weight, bias, rate, col):
    rows, dim = normed.shape
    block = pl.BlockSpec((CH, LANES), lambda b: (b, 0))
    wide = jax.ShapeDtypeStruct((rows, LANES), F32)
    return pl.pallas_call(
        step_kernel,
        name="step_sizes",
        grid=(rows // CH,),
        in_specs=[
            pl.BlockSpec((CH, dim), lambda b: (b, 0)),
            pl.BlockSpec((dim, LANES), lambda b: (0, col)),
            whole((1, LANES)),
            whole((1, LANES)),
        ],
        out_specs=[block, block, block, block, pl.BlockSpec((16, CH), lambda b: (0, b))],
        out_shape=[wide, wide, wide, wide, jax.ShapeDtypeStruct((16, rows), F32)],
        scratch_shapes=[pltpu.VMEM((8, LANES), F32)],
        compiler_params=params(),
        cost_estimate=cost(2 * rows * dim * LANES, 2 * rows * dim + 20 * rows * LANES, 3 * rows * LANES),
    )(normed, weight, bias, rate)


def ssd_kernel(heads, xa_ref, bm_ref, cm_ref, dt_ref, cum_ref, cum_t_ref, skip, onehot, y_ref, start_ref, end_ref, state):
    @pl.when(pl.program_id(0) == 0)
    def _():
        state[...] = jnp.zeros_like(state)

    hot = onehot[...]
    xa = xa_ref[...].astype(F32)
    bm, cm, cum, cum_t = bm_ref[...], cm_ref[...], cum_ref[...], cum_t_ref[...]
    rows = cum.shape[0]
    last = cum[rows - 1 : rows, :]
    x_dt = xa * by_heads(dt_ref[...], hot)
    before = state[...]
    start_ref[0] = before
    y_ref[...] = by_heads(jnp.exp(cum), hot) * dot_nn(cm, before.astype(BF16)) + skip[...] * xa
    to_end = (x_dt * by_heads(jnp.exp(last - cum), hot)).astype(BF16)
    after = row_of(jnp.exp(last), hot) * before + dot_tn(bm, to_end)
    state[...] = after
    end_ref[...] = after
    x_low = x_dt.astype(BF16)
    scores = dot_nt(cm, bm)
    mask = lax.broadcasted_iota(jnp.int32, (rows, rows), 0) >= lax.broadcasted_iota(jnp.int32, (rows, rows), 1)
    width = xa.shape[1] // heads
    per = LANES // width
    lane = lax.broadcasted_iota(jnp.int32, (rows, LANES), 1) // width
    for group in range(heads // per):
        at = slice(group * LANES, (group + 1) * LANES)
        x_group = x_low[:, at]
        total = y_ref[:, at]
        for k in range(per):
            h = group * per + k
            gap = jnp.where(mask, cum[:, h : h + 1] - cum_t[h : h + 1, :], 0.0)
            weights = jnp.where(mask, jnp.exp(gap) * scores, 0.0).astype(BF16)
            total = total + dot_nn(weights, jnp.where(lane == k, x_group, jnp.zeros_like(x_group)))
        y_ref[:, at] = total


def ssd_forward(act, dt, cum, cum_t, skip, onehot, heads):
    rows = act.shape[0]
    inner = onehot.shape[1]
    blocks = rows // CH
    col = inner // LANES
    wide = pl.BlockSpec((CH, LANES), lambda b: (b, 0))
    return pl.pallas_call(
        functools.partial(ssd_kernel, heads),
        name="ssd_forward",
        grid=(blocks,),
        in_specs=[
            pl.BlockSpec((CH, inner), lambda b: (b, 0)),
            pl.BlockSpec((CH, LANES), lambda b: (b, col)),
            pl.BlockSpec((CH, LANES), lambda b: (b, col + 1)),
            wide,
            wide,
            pl.BlockSpec((16, CH), lambda b: (0, b)),
            whole((1, inner)),
            whole((LANES, inner)),
        ],
        out_specs=[
            pl.BlockSpec((CH, inner), lambda b: (b, 0)),
            pl.BlockSpec((1, LANES, inner), lambda b: (b, 0, 0)),
            whole((LANES, inner)),
        ],
        out_shape=[
            jax.ShapeDtypeStruct((rows, inner), F32),
            jax.ShapeDtypeStruct((blocks, LANES, inner), F32),
            jax.ShapeDtypeStruct((LANES, inner), F32),
        ],
        scratch_shapes=[pltpu.VMEM((LANES, inner), F32)],
        compiler_params=params(),
        cost_estimate=cost(6 * rows * CH * inner, 12 * rows * inner, rows * CH * heads),
    )(act, act, act, dt, cum, cum_t, skip, onehot)


def gate_kernel(normed, grad, w_gate, w_out, y_in, cm, seq, state, gain, onehot, gate_ref, y_ref, gon_ref, stat_ref):
    gate = dot_nn(normed[...], w_gate[...])
    grad_on = dot_nn(grad[...], w_out[...])
    y = y_in[...] + by_heads(jnp.exp(seq[...]), onehot[...]) * dot_nn(cm[...], state[...])
    gated = y * (gate * sigmoid(gate))
    gate_ref[...] = gate
    y_ref[...] = y
    gon_ref[...] = grad_on
    square = jnp.sum(gated * gated, axis=1, keepdims=True)
    inner = jnp.sum(grad_on * gain[...] * gated, axis=1, keepdims=True)
    lane = lax.broadcasted_iota(jnp.int32, (gate.shape[0], LANES), 1)
    both = jnp.where(lane == 0, square, jnp.where(lane == 1, inner, 0.0))
    stat_ref[...] = jnp.transpose(both)[0:8, :]


def gate_stage(normed, grad, w_rest, y_in, act, seq, state, gain, onehot):
    rows, dim = normed.shape
    inner = onehot.shape[1]
    col = inner // LANES
    block = pl.BlockSpec((CH, inner), lambda b: (b, 0))
    full = jax.ShapeDtypeStruct((rows, inner), F32)
    return pl.pallas_call(
        gate_kernel,
        name="gate_stage",
        grid=(rows // CH,),
        in_specs=[
            pl.BlockSpec((CH, dim), lambda b: (b, 0)),
            pl.BlockSpec((CH, dim), lambda b: (b, 0)),
            pl.BlockSpec((dim, inner), lambda b: (0, 0)),
            pl.BlockSpec((dim, inner), lambda b: (0, 1)),
            block,
            pl.BlockSpec((CH, LANES), lambda b: (b, col + 1)),
            pl.BlockSpec((CH, LANES), lambda b: (b, 0)),
            whole((LANES, inner)),
            whole((1, inner)),
            whole((LANES, inner)),
        ],
        out_specs=[block, block, block, pl.BlockSpec((8, CH), lambda b: (0, b))],
        out_shape=[full, full, full, jax.ShapeDtypeStruct((8, rows), F32)],
        compiler_params=params(),
        cost_estimate=cost(4 * rows * dim * inner, 16 * rows * inner + 4 * rows * dim, rows * inner),
    )(normed, grad, w_rest, w_rest, y_in, act, seq, state, gain, onehot)


def back_order(i):
    return jnp.where(i < 2, 2 + i, 3 - i)


def norm_kernel(
    inner_all, place, gate_ref, y_ref, gon_ref, stat, w_out, cm, cum, seq, gain, onehot,
    send, keep, out_in_ref, gy_ref, ggate_ref, gog, gstart, gin, gin_sum,
):
    step = pl.program_id(0)

    @pl.when(step == 0)
    def _():
        gog[...] = jnp.zeros_like(gog)
        gin_sum[...] = jnp.zeros_like(gin_sum)

    columns = jnp.transpose(jnp.concatenate([stat[...]] * (LANES // 8), axis=0))
    scale = lax.rsqrt(columns[:, 0:1] * (1.0 / inner_all) + EPSILON)
    along = columns[:, 1:2] * (1.0 / inner_all)
    gate, y, grad_on = gate_ref[...], y_ref[...], gon_ref[...]
    sig = sigmoid(gate)
    silu = gate * sig
    gated = y * silu
    normed = gated * scale
    out_in = (normed * gain[...]).astype(BF16)
    out_in_ref[...] = out_in
    mixed = dot_nt(out_in, w_out[...]).astype(BF16)

    @pl.when(step < 2)
    def _():
        send[...] = mixed

    @pl.when(step >= 2)
    def _():
        keep[...] = mixed

    gog[...] += fold_rows(grad_on * normed)
    grad_gated = scale * (grad_on * gain[...]) - gated * (scale * scale * scale * along)
    grad_y = (grad_gated * silu).astype(BF16)
    gy_ref[...] = grad_y
    ggate_ref[...] = (grad_gated * y * (sig * (1.0 + gate * (1.0 - sig)))).astype(BF16)
    hot = onehot[...]
    scaled = (grad_y.astype(F32) * by_heads(jnp.exp(cum[...]), hot)).astype(BF16)
    grad_start = dot_tn(cm[...], scaled)
    gstart[0] = grad_start
    rows = gate.shape[0]
    ahead = seq[rows - 1 : rows, :] - cum[rows - 1 : rows, :]
    gin_sum[...] += row_of(jnp.exp(ahead), hot) * grad_start
    gin[...] = gin_sum[...].astype(BF16)


def norm_stage(place, gate, y, grad_on, stat, w_rest, act, cum, seq, gain, onehot, inner_all, dim):
    rows, inner = gate.shape
    col = inner // LANES
    blocks = rows // CH
    at = lambda i, q: back_order(i) ^ q[0]
    block = pl.BlockSpec((CH, inner), lambda i, q: (at(i, q), 0))
    wide = pl.BlockSpec((CH, LANES), lambda i, q: (at(i, q), 0))
    low = jax.ShapeDtypeStruct((rows, inner), BF16)
    half = jax.ShapeDtypeStruct((rows // 2, dim), BF16)
    return pl.pallas_call(
        functools.partial(norm_kernel, inner_all),
        name="norm_stage",
        grid_spec=pltpu.PrefetchScalarGridSpec(
            num_scalar_prefetch=1,
            grid=(blocks,),
            in_specs=[
                block,
                block,
                block,
                pl.BlockSpec((8, CH), lambda i, q: (0, at(i, q))),
                pl.BlockSpec((dim, inner), lambda i, q: (0, 1)),
                pl.BlockSpec((CH, LANES), lambda i, q: (at(i, q), col + 1)),
                wide,
                wide,
                whole((1, inner)),
                whole((LANES, inner)),
            ],
            out_specs=[
                pl.BlockSpec((CH, dim), lambda i, q: (jnp.minimum(i, 1), 0)),
                pl.BlockSpec((CH, dim), lambda i, q: (jnp.minimum(3 - i, 1), 0)),
                block,
                block,
                block,
                whole((8, inner)),
                pl.BlockSpec((1, LANES, inner), lambda i, q: (at(i, q), 0, 0)),
                whole((LANES, inner)),
            ],
            scratch_shapes=[pltpu.VMEM((LANES, inner), F32)],
        ),
        out_shape=[
            half,
            half,
            low,
            low,
            low,
            jax.ShapeDtypeStruct((8, inner), F32),
            jax.ShapeDtypeStruct((blocks, LANES, inner), F32),
            jax.ShapeDtypeStruct((LANES, inner), BF16),
        ],
        compiler_params=params(),
        cost_estimate=cost(2 * rows * dim * inner, 18 * rows * inner + 4 * rows * dim, rows * inner),
    )(place, gate, y, grad_on, stat, w_rest, act, cum, seq, gain, onehot)


def early_kernel(grad_t, out_in, normed_t, ggate, out):
    inner = out_in.shape[1]
    out[:, 0:inner] = dot_nn(grad_t[...], out_in[...]).astype(BF16)
    out[:, inner:] = dot_nn(normed_t[...], ggate[...]).astype(BF16)


def early_grads(grad_t, out_in, normed_t, ggate):
    dim, rows = grad_t.shape
    inner = out_in.shape[1]
    tile = dim // 4
    return pl.pallas_call(
        early_kernel,
        name="early_grads",
        grid=(4,),
        in_specs=[
            pl.BlockSpec((tile, rows), lambda i: (i, 0)),
            whole((rows, inner)),
            pl.BlockSpec((tile, rows), lambda i: (i, 0)),
            whole((rows, inner)),
        ],
        out_specs=pl.BlockSpec((tile, 2 * inner), lambda i: (i, 0)),
        out_shape=jax.ShapeDtypeStruct((dim, 2 * inner), BF16),
        compiler_params=params(),
        cost_estimate=cost(4 * rows * dim * inner, 4 * dim * (rows + inner) + 4 * rows * inner, 0),
    )(grad_t, out_in, normed_t, ggate)


def lower_decay(mask, cum, cum_t, h):
    gap = jnp.where(mask, cum[:, h : h + 1] - cum_t[h : h + 1, :], 0.0)
    return jnp.where(mask, jnp.exp(gap), 0.0)


def scores_back_kernel(
    heads, xa_ref, bm_ref, cm_ref, gy_ref, dt_ref, cum_ref, seq_ref, cum_t_ref, last_ref,
    start_ref, in_state, gstart, gin, onehot, gbc_ref, after_ref, after,
):
    step = pl.program_id(0)
    blocks = gstart.shape[0]
    hot = onehot[...]

    @pl.when(step == 0)
    def _():
        decays = by_heads(jnp.exp(last_ref[...]), hot)
        running = gin[...].astype(F32)
        for b in reversed(range(blocks)):
            after[b] = running
            running = gstart[b] + decays[b : b + 1, :] * running

    cum, cum_t = cum_ref[...], cum_t_ref[...]
    bm, cm, gy = bm_ref[...], cm_ref[...], gy_ref[...]
    rows = cum.shape[0]
    last = cum[rows - 1 : rows, :]
    ahead = seq_ref[rows - 1 : rows, :] - last
    start = start_ref[0] + row_of(jnp.exp(ahead), hot) * in_state[...].astype(F32)
    grad_after = after[step]
    after_ref[0] = grad_after
    x_dt = xa_ref[...].astype(F32) * by_heads(dt_ref[...], hot)
    x_low = x_dt.astype(BF16)
    mask = lax.broadcasted_iota(jnp.int32, (rows, rows), 0) >= lax.broadcasted_iota(jnp.int32, (rows, rows), 1)
    width = x_low.shape[1] // heads
    per = LANES // width
    lane = lax.broadcasted_iota(jnp.int32, (rows, LANES), 1) // width
    grad_scores = jnp.zeros((rows, rows), F32)
    for group in range(heads // per):
        at = slice(group * LANES, (group + 1) * LANES)
        x_group, gy_group = x_low[:, at], gy[:, at]
        for k in range(per):
            decay = lower_decay(mask, cum, cum_t, group * per + k)
            gy_head = jnp.where(lane == k, gy_group, jnp.zeros_like(gy_group))
            grad_scores = grad_scores + dot_nt(gy_head, x_group) * decay
    to_end = (x_dt * by_heads(jnp.exp(last - cum), hot)).astype(BF16)
    gy_scaled = (gy.astype(F32) * by_heads(jnp.exp(cum), hot)).astype(BF16)
    scores_low = grad_scores.astype(BF16)
    gbc_ref[:, 0:LANES] = dot_tn(scores_low, cm) + dot_nt(to_end, grad_after.astype(BF16))
    gbc_ref[:, LANES:] = dot_nn(scores_low, bm) + dot_nt(gy_scaled, start.astype(BF16))


def scores_backward(act, gy, dt, cum, seq, cum_t, lasts, starts, in_state, gstart, gin, onehot, heads):
    rows, inner = gy.shape
    col = inner // LANES
    blocks = rows // CH
    block = pl.BlockSpec((CH, inner), lambda b: (b, 0))
    wide = pl.BlockSpec((CH, LANES), lambda b: (b, 0))
    state = pl.BlockSpec((1, LANES, inner), lambda b: (b, 0, 0))
    return pl.pallas_call(
        functools.partial(scores_back_kernel, heads),
        name="scores_backward",
        grid=(blocks,),
        in_specs=[
            block,
            pl.BlockSpec((CH, LANES), lambda b: (b, col)),
            pl.BlockSpec((CH, LANES), lambda b: (b, col + 1)),
            block,
            wide,
            wide,
            wide,
            pl.BlockSpec((16, CH), lambda b: (0, b)),
            whole((8, LANES)),
            state,
            whole((LANES, inner)),
            whole((blocks, LANES, inner)),
            whole((LANES, inner)),
            whole((LANES, inner)),
        ],
        out_specs=[pl.BlockSpec((CH, 2 * LANES), lambda b: (b, 0)), state],
        out_shape=[
            jax.ShapeDtypeStruct((rows, 2 * LANES), F32),
            jax.ShapeDtypeStruct((blocks, LANES, inner), F32),
        ],
        scratch_shapes=[pltpu.VMEM((blocks, LANES, inner), F32)],
        compiler_params=params(),
        cost_estimate=cost(6 * rows * CH * inner, 10 * rows * inner, rows * CH * heads),
    )(act, act, act, gy, dt, cum, seq, cum_t, lasts, starts, in_state, gstart, gin, onehot)


def ssd_back_kernel(
    heads, offset, xa_ref, bm_ref, cm_ref, gy_ref, y_ref, dt_ref, sig_ref, cum_ref, seq_ref, cum_t_ref,
    start_ref, in_state, after_ref, pre_ref, taps, rate, skip, onehot, *rest,
):
    gconv_ref, graw_ref, head_ref, rows_sum, heads_sum, gx = rest[-6:]
    step = pl.program_id(0)
    hot = onehot[...]

    @pl.when(step == 0)
    def _():
        rows_sum[...] = jnp.zeros_like(rows_sum)
        heads_sum[...] = jnp.zeros_like(heads_sum)

    cum, cum_t, dt = cum_ref[...], cum_t_ref[...], dt_ref[...]
    bm, cm = bm_ref[...], cm_ref[...]
    rows = cum.shape[0]
    last = cum[rows - 1 : rows, :]
    ahead = seq_ref[rows - 1 : rows, :] - last
    start = start_ref[0] + row_of(jnp.exp(ahead), hot) * in_state[...].astype(F32)
    grad_after = after_ref[0]

    gy = gy_ref[...]
    xa = xa_ref[...].astype(F32)
    dt_wide = by_heads(dt, hot)
    x_dt = xa * dt_wide
    x_low = x_dt.astype(BF16)
    scores = dot_nt(cm, bm)
    mask = lax.broadcasted_iota(jnp.int32, (rows, rows), 0) >= lax.broadcasted_iota(jnp.int32, (rows, rows), 1)
    width = xa.shape[1] // heads
    per = LANES // width
    lane = lax.broadcasted_iota(jnp.int32, (rows, LANES), 1) // width
    for group in range(heads // per):
        at = slice(group * LANES, (group + 1) * LANES)
        gy_group = gy[:, at]
        total = jnp.zeros((rows, LANES), F32)
        for k in range(per):
            weights = (lower_decay(mask, cum, cum_t, group * per + k) * scores).astype(BF16)
            total = total + dot_tn(weights, jnp.where(lane == k, gy_group, jnp.zeros_like(gy_group)))
        gx[:, at] = total

    end_wide = by_heads(jnp.exp(last - cum), hot)
    from_end = dot_nn(bm, grad_after.astype(BF16))
    to_end = (x_dt * end_wide).astype(BF16)
    gx_intra = gx[...]
    gx_all = gx_intra + end_wide * from_end
    end_term = to_end.astype(F32) * from_end
    gy_f = gy.astype(F32)
    grad_xa = dt_wide * gx_all + skip[...] * gy_f

    grad_dt = by_heads_t(xa * gx_all, hot)
    grad_cum = by_heads_t(
        gy_f * (y_ref[...] - skip[...] * xa) - x_low.astype(F32) * gx_intra - end_term, hot
    )
    end_rows = fold_rows(end_term)
    state_rows = fold_rows(grad_after * start) * row_of(jnp.exp(last), hot)
    grad_last = jnp.sum(by_heads_t(end_rows + state_rows, hot), axis=0, keepdims=True)
    upper = (
        lax.broadcasted_iota(jnp.int32, (rows, rows), 0) <= lax.broadcasted_iota(jnp.int32, (rows, rows), 1)
    ).astype(BF16)
    grad_a = jnp.broadcast_to(grad_last, grad_cum.shape)
    for part in exact_parts(grad_cum):
        grad_a = grad_a + dot_nn(upper, part)
    grad_raw = (grad_dt + rate[...] * grad_a) * sig_ref[...]
    graw_ref[...] = grad_raw.astype(BF16)
    heads_sum[0:8, :] += fold_rows(grad_raw)
    heads_sum[8:16, :] += fold_rows(grad_a * dt * rate[...])

    tap_count = 4
    first = HALO - tap_count + 1
    base = pl.multiple_of((step + offset) * rows, rows)
    window = pre_ref[pl.ds(base, rows + HALO), :]
    conv = taps[tap_count : tap_count + 1, :] + taps[0:1, :] * window[first : first + rows]
    for k in range(1, tap_count):
        conv = conv + taps[k : k + 1, :] * window[first + k : first + k + rows]
    sig = sigmoid(conv)
    gconv = grad_xa * (sig * (1.0 + conv * (1.0 - sig)))
    gconv_ref[...] = gconv

    @pl.when(step == 0)
    def _():
        head_ref[...] = gconv[0:HALO, :]

    for k in range(tap_count):
        rows_sum[8 * k : 8 * k + 8, :] += fold_rows(gconv * window[first + k : first + k + rows])
    rows_sum[8 * tap_count : 8 * tap_count + 8, :] += fold_rows(gconv)
    rows_sum[8 * tap_count + 8 : 8 * tap_count + 16, :] += fold_rows(gy_f * xa)


def ssd_backward(
    act, gy, y, dt, sig, cum, seq, cum_t, starts, in_state, after, pre, taps, rate, skip, onehot, heads,
    offset, count, into,
):
    rows, inner = gy.shape
    col = inner // LANES
    block = pl.BlockSpec((CH, inner), lambda b: (b + offset, 0))
    wide = pl.BlockSpec((CH, LANES), lambda b: (b + offset, 0))
    state = pl.BlockSpec((1, LANES, inner), lambda b: (b + offset, 0, 0))
    operands = [act, act, act, gy, y, dt, sig, cum, seq, cum_t, starts, in_state, after, pre, taps, rate, skip, onehot]
    specs = [
        block,
        pl.BlockSpec((CH, LANES), lambda b: (b + offset, col)),
        pl.BlockSpec((CH, LANES), lambda b: (b + offset, col + 1)),
        block,
        block,
        wide,
        wide,
        wide,
        wide,
        pl.BlockSpec((16, CH), lambda b: (0, b + offset)),
        state,
        whole((LANES, inner)),
        state,
        pl.BlockSpec((rows + HALO, inner), lambda b: (0, 0)),
        pl.BlockSpec((8, inner), lambda b: (0, 0)),
        whole((1, LANES)),
        whole((1, inner)),
        whole((LANES, inner)),
    ]
    aliases = {}
    if into is not None:
        aliases = {len(operands): 0, len(operands) + 1: 1}
        operands += list(into)
        specs += [pl.BlockSpec(memory_space=pl.ANY)] * 2
    part = CH * count
    return pl.pallas_call(
        functools.partial(ssd_back_kernel, heads, offset),
        name="ssd_backward",
        grid=(count,),
        in_specs=specs,
        out_specs=[block, wide, whole((HALO, inner)), whole((48, inner)), whole((16, LANES))],
        out_shape=[
            jax.ShapeDtypeStruct((rows, inner), F32),
            jax.ShapeDtypeStruct((rows, LANES), BF16),
            jax.ShapeDtypeStruct((HALO, inner), F32),
            jax.ShapeDtypeStruct((48, inner), F32),
            jax.ShapeDtypeStruct((16, LANES), F32),
        ],
        input_output_aliases=aliases,
        scratch_shapes=[pltpu.VMEM((CH, inner), F32)],
        compiler_params=params(),
        cost_estimate=cost(8 * part * CH * inner, 24 * part * inner, part * CH * heads),
    )(*operands)


def bc_kernel(grad, pre_ref, taps, gconv_ref, tap_sum):
    tap_count = 4
    rows = grad.shape[0]
    first = HALO - tap_count + 1
    conv = taps[tap_count : tap_count + 1, :] + taps[0:1, :] * pre_ref[first : first + rows, :]
    for k in range(1, tap_count):
        conv = conv + taps[k : k + 1, :] * pre_ref[first + k : first + k + rows, :]
    sig = sigmoid(conv)
    gconv = grad[...] * (sig * (1.0 + conv * (1.0 - sig)))
    gconv_ref[...] = gconv
    for k in range(tap_count):
        tap_sum[8 * k : 8 * k + 8, :] = fold_rows(gconv * pre_ref[first + k : first + k + rows, :])
    tap_sum[8 * tap_count : 8 * tap_count + 8, :] = fold_rows(gconv)


def bc_backward(grad, pre, taps):
    rows, wide = grad.shape
    col = pre.shape[1] // wide - 1
    return pl.pallas_call(
        bc_kernel,
        name="bc_backward",
        grid=(1,),
        in_specs=[
            whole((rows, wide)),
            pl.BlockSpec((rows + HALO, wide), lambda i: (0, col)),
            pl.BlockSpec((8, wide), lambda i: (0, col)),
        ],
        out_specs=[whole((rows, wide)), whole((40, wide))],
        out_shape=[jax.ShapeDtypeStruct((rows, wide), F32), jax.ShapeDtypeStruct((40, wide), F32)],
        compiler_params=params(),
        cost_estimate=cost(30 * rows * wide, 16 * rows * wide, rows * wide),
    )(grad, pre, taps)


def conv_transpose(grad_ref, next_ref, halo_ref, taps, ext, at_end):
    tap_count = 4
    rows = grad_ref.shape[0]
    ext[0:rows, :] = grad_ref[...]
    ext[rows:, :] = jnp.where(at_end, halo_ref[...], next_ref[...])
    total = taps[tap_count - 1 : tap_count, :] * ext[0:rows, :]
    for k in range(tap_count - 1):
        ahead = tap_count - 1 - k
        total = total + taps[k : k + 1, :] * ext[ahead : ahead + rows, :]
    return total.astype(BF16)


def input_kernel(
    where, gx_ref, gx_next, gx_halo, gb_ref, gb_next, gb_halo, taps_x, taps_b, ggate, graw, x_ref,
    w_gate, w_x, w_b, w_dt, send, keep, gcat, gain_sum, ext_x, ext_b,
):
    step = pl.program_id(0)

    @pl.when(step == 0)
    def _():
        gain_sum[...] = jnp.zeros_like(gain_sum)

    at_end = (back_order(step) ^ where[0]) == pl.num_programs(0) - 1
    gpre_x = conv_transpose(gx_ref, gx_next, gx_halo, taps_x, ext_x, at_end)
    gpre_b = conv_transpose(gb_ref, gb_next, gb_halo, taps_b, ext_b, at_end)
    shared = gpre_b.shape[1]
    gcat[:, 0:shared] = gpre_b
    gcat[:, shared:] = gpre_x
    total = dot_nt(ggate[...], w_gate[...]) + dot_nt(gpre_x, w_x[...])
    total = total + dot_nt(graw[...], w_dt[...]) + dot_nt(gpre_b, w_b[...])
    xf = x_ref[...].astype(F32)
    scale = lax.rsqrt(jnp.mean(xf * xf, axis=1, keepdims=True) + EPSILON)
    gain_sum[...] += fold_rows(total * (xf * scale))
    part = total.astype(BF16)

    @pl.when(step < 2)
    def _():
        send[...] = part

    @pl.when(step >= 2)
    def _():
        keep[...] = part


def input_stage(where, gx, gx_halo, gb, gb_halo, taps, ggate, graw, x, w_rest, w_first):
    rows, inner = gx.shape
    dim = x.shape[1]
    col = inner // LANES
    per = CH // HALO
    top = rows // HALO - 1
    blocks = rows // CH
    at = lambda i, q: back_order(i) ^ q[0]
    nxt = lambda i, q: (jnp.minimum(per * (at(i, q) + 1), top), 0)
    both = 2 * LANES
    half = jax.ShapeDtypeStruct((rows // 2, dim), BF16)
    return pl.pallas_call(
        input_kernel,
        name="input_stage",
        grid_spec=pltpu.PrefetchScalarGridSpec(
            num_scalar_prefetch=1,
            grid=(blocks,),
            in_specs=[
                pl.BlockSpec((CH, inner), lambda i, q: (at(i, q), 0)),
                pl.BlockSpec((HALO, inner), nxt),
                pl.BlockSpec((HALO, inner), lambda i, q: (0, 0)),
                pl.BlockSpec((CH, both), lambda i, q: (at(i, q), 0)),
                pl.BlockSpec((HALO, both), nxt),
                pl.BlockSpec((HALO, both), lambda i, q: (0, 0)),
                pl.BlockSpec((8, inner), lambda i, q: (0, 0)),
                pl.BlockSpec((8, both), lambda i, q: (0, inner // both)),
                pl.BlockSpec((CH, inner), lambda i, q: (at(i, q), 0)),
                pl.BlockSpec((CH, LANES), lambda i, q: (at(i, q), 0)),
                pl.BlockSpec((CH, dim), lambda i, q: (at(i, q), 0)),
                pl.BlockSpec((dim, inner), lambda i, q: (0, 0)),
                pl.BlockSpec((dim, inner), lambda i, q: (0, 0)),
                pl.BlockSpec((dim, both), lambda i, q: (0, inner // both)),
                pl.BlockSpec((dim, LANES), lambda i, q: (0, col + 2)),
            ],
            out_specs=[
                pl.BlockSpec((CH, dim), lambda i, q: (jnp.minimum(i, 1), 0)),
                pl.BlockSpec((CH, dim), lambda i, q: (jnp.minimum(3 - i, 1), 0)),
                pl.BlockSpec((CH, inner + both), lambda i, q: (at(i, q), 0)),
                pl.BlockSpec((8, dim), lambda i, q: (0, 0)),
            ],
            scratch_shapes=[pltpu.VMEM((CH + HALO, inner), F32), pltpu.VMEM((CH + HALO, both), F32)],
        ),
        out_shape=[
            half,
            half,
            jax.ShapeDtypeStruct((rows, inner + both), BF16),
            jax.ShapeDtypeStruct((8, dim), F32),
        ],
        compiler_params=params(),
        cost_estimate=cost(4 * rows * dim * inner, 10 * rows * inner + 2 * rows * dim, 0),
    )(where, gx, gx, gx_halo, gb, gb, gb_halo, taps, taps, ggate, graw, x, w_rest, w_first, w_first, w_first)


def late_kernel(side, normed_t, gcat, keep_a, send_a, keep_b, send_b):
    result = dot_nn(normed_t[...], gcat[...]).astype(BF16)
    rows = result.shape[0] // 2
    cut = keep_a.shape[2]
    top, bottom = result[:rows], result[rows:]
    first = side[0] == 0
    keep, send = jnp.where(first, top, bottom), jnp.where(first, bottom, top)
    keep_a[0], keep_b[0] = keep[:, :cut], keep[:, cut:]
    send_a[0], send_b[0] = send[:, :cut], send[:, cut:]


def late_grads(side, normed_t, gcat, shards):
    dim, rows = normed_t.shape
    width = gcat.shape[1]
    tile, cut = dim // shards, width // 2
    half = pl.BlockSpec((1, tile // 2, cut), lambda i, q: (i, 0, 0))
    return pl.pallas_call(
        late_kernel,
        name="late_grads",
        grid_spec=pltpu.PrefetchScalarGridSpec(
            num_scalar_prefetch=1,
            grid=(shards,),
            in_specs=[
                pl.BlockSpec((tile, rows), lambda i, q: (i, 0)),
                pl.BlockSpec((rows, width), lambda i, q: (0, 0)),
            ],
            out_specs=[half] * 4,
        ),
        out_shape=[jax.ShapeDtypeStruct((shards, tile // 2, cut), BF16)] * 4,
        compiler_params=params(),
        cost_estimate=cost(2 * rows * dim * width, 2 * dim * (rows + width) + 2 * rows * width, 0),
    )(side, normed_t, gcat)


def on_device(
    hidden_in,
    norm_gain,
    w_in_zx,
    w_in_bc,
    w_in_dt,
    conv_x,
    conv_bc,
    dt_bias,
    a_log,
    d_skip,
    out_gain,
    w_out,
    cotangent,
):
    seq_count, rows, dim = hidden_in.shape
    inner = w_in_zx.shape[2]
    heads = w_in_dt.shape[1]
    head_dim = inner // heads
    tap_count = conv_x.shape[0] - 1
    tensor_size, shards, contexts = lax.axis_size("tensor"), lax.axis_size("shard"), lax.axis_size("context")
    inner_all = inner * tensor_size
    blocks = rows // CH
    assert seq_count == 1 and tensor_size == 4 and blocks == 4 and contexts == 2
    shard_rows = w_in_zx.shape[0]
    place = lax.axis_index("tensor")
    context = lax.axis_index("context")
    side_num = place % 2
    quarter = side_num * 2 + place // 2
    where = jnp.stack([quarter, side_num]).astype(jnp.int32)
    col = inner // LANES

    x_rows = hidden_in.reshape(rows, dim)
    g_rows = cotangent.reshape(rows, dim)

    pad_dt = jnp.zeros((shard_rows, LANES - heads), BF16)
    w_front = jnp.concatenate([w_in_zx[:, 1], w_in_bc, w_in_dt, pad_dt], axis=1)
    w_front, w_gate_local, w_out_local = together(w_front, w_in_zx[:, 0], w_out)
    w_back = jnp.concatenate([w_gate_local, w_out_local.T], axis=1)
    half_rows = shard_rows // contexts
    line = shards == 4
    all_rows = ("shard", "context")
    own_half = lambda v: lax.dynamic_slice_in_dim(v, context * half_rows, half_rows, 0)
    w_rest = lax.all_gather(own_half(w_back), all_rows, axis=0, tiled=True)
    if line:
        front = Gather(w_front)
        front.step()
    halo_rows = shifted(x_rows[rows - HALO :], "context", 1)

    def norm_of(values):
        wide = values.astype(F32)
        scale = lax.rsqrt(jnp.mean(wide * wide, axis=-1, keepdims=True) + EPSILON)
        return (wide * scale * norm_gain).astype(BF16)

    normed = norm_of(x_rows)
    halo = norm_of(halo_rows)

    pad_heads = lambda v: jnp.pad(v, (0, LANES - heads)).reshape(1, LANES)
    rate = pad_heads(-jnp.exp(a_log))
    bias = pad_heads(dt_bias)
    skip = jnp.repeat(d_skip, head_dim).reshape(1, inner)
    gain = out_gain.reshape(1, inner)
    taps = jnp.pad(jnp.concatenate([conv_x, conv_bc], axis=1), ((0, 8 - tap_count - 1), (0, 0)))
    onehot = (
        lax.broadcasted_iota(jnp.int32, (LANES, inner), 0)
        == lax.broadcasted_iota(jnp.int32, (LANES, inner), 1) // head_dim
    ).astype(BF16)

    if line:
        front.plus, front.minus, normed = together(front.plus, front.minus, normed)
        front.cross()
        front.step()
        front.plus, front.minus, halo = together(front.plus, front.minus, halo)
        front.cross()
        front.step()
        front.plus, front.minus = together(front.plus, front.minus)
        front.cross()
        w_first = front.full()
    else:
        w_first = lax.all_gather(own_half(w_front), all_rows, axis=0, tiled=True)

    act, pre = conv_front(normed, halo, w_first, taps)
    dt, sig, cum, seq, cum_t = step_sizes(normed, w_first, bias, rate, col + 2)
    y_local, starts, end_state = ssd_forward(act, dt, cum, cum_t, skip, onehot, heads)
    in_state = shifted(end_state.astype(BF16), "context", 1)
    normed_low, g_low, y_local = together(normed, g_rows, y_local)
    normed_t, grad_t = normed_low.T, g_low.T
    in_state, normed_t, grad_t = together(in_state, normed_t, grad_t)
    lasts = jnp.pad(cum.reshape(blocks, CH, LANES)[:, CH - 1], ((0, 8 - blocks), (0, 0)))

    gate, y, grad_on, stat = gate_stage(normed, g_rows, w_rest, y_local, act, seq, in_state, gain, onehot)
    stat = butterfly(stat, "tensor")
    send, keep, out_in, gy, ggate, gog, gstart, gin_first = norm_stage(
        where, gate, y, grad_on, stat, w_rest, act, cum, seq, gain, onehot, inner_all, dim
    )

    own_rows = rows // 4
    gin = shifted(gin_first, "context", -1)
    got = to_core(send)
    early = early_grads(grad_t, out_in, normed_t, ggate)
    gy, gin, early, got = together(gy, gin, early, got)
    early_share = lax.psum_scatter(early, ("shard", "context"), scatter_dimension=0, tiled=True)
    got_mine = to_chip(add_low(keep[own_rows:], got[own_rows:]))
    gbc, after = scores_backward(act, gy, dt, cum, seq, cum_t, lasts, starts, in_state, gstart, gin, onehot, heads)
    gconv_bc, tap_bc = bc_backward(gbc, pre, taps)
    state = (act, gy, y, dt, sig, cum, seq, cum_t, starts, in_state, after, pre, taps, rate, skip, onehot, heads)
    gconv, graw, head, rows_sum_a, heads_sum_a = ssd_backward(*state, 0, 1, None)
    halo_out = jnp.concatenate([head, gconv_bc[:HALO]], axis=1)
    gconv, halo_out, got_mine = together(gconv, halo_out, got_mine)
    g_halo = shifted(halo_out, "context", -1)
    mixed_mine = keep[:own_rows].astype(F32) + got[:own_rows].astype(F32) + got_mine.astype(F32)
    x_mine = lax.dynamic_slice_in_dim(x_rows, quarter * own_rows, own_rows, 0).astype(F32)
    stream_mine = x_mine + mixed_mine
    out_mine = stream_mine.astype(BF16)
    out_chip = to_chip(out_mine)
    out_a = to_core(out_mine)
    gconv, graw, _, rows_sum_b, heads_sum_b = ssd_backward(*state, 1, blocks - 1, (gconv, graw))
    gconv, out_chip, out_a, g_halo = together(gconv, out_chip, out_a, g_halo)
    out_b = to_core(out_chip)
    gx_halo, gb_halo = g_halo[:, :inner], g_halo[:, inner:]

    send, keep, gcat, gain_sum = input_stage(
        where, gconv, gx_halo, gconv_bc, gb_halo, taps, ggate, graw, x_rows, w_rest, w_first
    )

    wide_bc = 2 * LANES
    send, keep, gcat, gain_sum, out_b = together(send, keep, gcat, gain_sum, out_b)
    got = to_core(send)
    if line:
        keep_a, send_a, keep_b, send_b = late_grads(context.astype(jnp.int32).reshape(1), normed_t, gcat, shards)
        got, keep_a, send_a, send_b = together(got, keep_a, send_a, send_b)
        x_got_a = lax.ppermute(send_a, "context", swap_pairs(2, 1))
    got_mine = to_chip(add_low(keep[own_rows:], got[own_rows:]))
    got, gain_sum, tap_bc, graw, gog, stream_late, mixed_late = together(
        got, gain_sum, tap_bc, graw, gog, stream_mine, mixed_mine
    )

    wide = dim // inner
    tap_rows = -(-5 * wide_bc // inner)
    taps_flat = jnp.pad(tap_bc.reshape(tap_count + 1, 8, wide_bc).sum(1).reshape(-1), (0, tap_rows * inner - 5 * wide_bc))
    shared = jnp.concatenate(
        [
            gain_sum.sum(0).reshape(wide, inner),
            taps_flat.reshape(tap_rows, inner),
            jnp.pad(
                jnp.stack([jnp.sum(stream_late * stream_late), jnp.sum(mixed_late * mixed_late)]).reshape(1, 2),
                ((0, 0), (0, inner - 2)),
            ),
        ],
        axis=0,
    )
    shared = jnp.pad(shared, ((0, -shared.shape[0] % 8), (0, 0)))
    shared_rows = shared.shape[0]
    grad_dt_t = dot_tn(graw[:, :16], normed)
    local = jnp.concatenate(
        [
            grad_dt_t.reshape(-1, inner),
            (rows_sum_a + rows_sum_b).reshape(6, 8, inner).sum(1),
            gog.sum(0, keepdims=True),
            jnp.pad((heads_sum_a + heads_sum_b).reshape(2, 8, LANES).sum(1), ((0, 0), (0, inner - LANES))),
        ],
        axis=0,
    )
    local = jnp.pad(local, ((0, -local.shape[0] % 8), (0, 0)))
    shared = shared + to_core(shared)
    if line:
        got_mine, local, shared, x_got_a, send_b, early_share = together(
            got_mine, local, shared, x_got_a, send_b, early_share
        )
        x_got_b = lax.ppermute(send_b, "context", swap_pairs(2, 1))
        sum_a = LineSum(keep_a, x_got_a)
        sum_a.step()

    grad_normed = keep[:own_rows].astype(F32) + got[:own_rows].astype(F32) + got_mine.astype(F32)
    scale_mine = lax.rsqrt(jnp.mean(x_mine * x_mine, axis=-1, keepdims=True) + EPSILON)
    g_mine = lax.dynamic_slice_in_dim(g_rows, quarter * own_rows, own_rows, 0).astype(F32)
    grad_un = grad_normed * norm_gain
    grad_mine = (
        g_mine
        + scale_mine * grad_un
        - x_mine * scale_mine**3 * jnp.mean(grad_un * x_mine, axis=-1, keepdims=True)
    ).astype(BF16)
    in_chip = to_chip(grad_mine)
    in_a = to_core(grad_mine)
    if line:
        grad_mine, sum_a.plus, sum_a.minus = together(grad_mine, sum_a.plus, sum_a.minus)
        sum_a.step()
        out = assemble(out_mine, out_chip, out_a, out_b, where, BF16)
        sum_a.plus, sum_a.minus, out, x_got_b = together(sum_a.plus, sum_a.minus, out, x_got_b)
        sum_a.step()
        sum_b = LineSum(keep_b, x_got_b)
        sum_b.step()
        sum_a.plus, sum_a.minus, sum_b.plus, sum_b.minus, in_chip = together(
            sum_a.plus, sum_a.minus, sum_b.plus, sum_b.minus, in_chip
        )
        in_b = to_core(in_chip)
        shared = shared + to_chip(shared)
        late_a = sum_a.result()
        sum_b.step()
        bc_sum = late_a[:, :wide_bc]
        bc_sum = bc_sum + to_core(bc_sum)
        local = jnp.concatenate([shared, local], axis=0)
        local = local + lax.ppermute(local, "context", swap_pairs(2, 1))
        sum_b.plus, sum_b.minus, local, bc_sum, in_b = together(sum_b.plus, sum_b.minus, local, bc_sum, in_b)
        sum_b.step()
        local = local + lax.ppermute(local, "shard", swap_pairs(shards, 1))
        grad_input = assemble(grad_mine, in_chip, in_a, in_b, where, F32)
        bc_sum = bc_sum + to_chip(bc_sum)
        sum_b.plus, sum_b.minus, local, bc_sum, grad_input = together(
            sum_b.plus, sum_b.minus, local, bc_sum, grad_input
        )
        local = local + lax.ppermute(local, "shard", swap_pairs(shards, 2))
        late_share = jnp.concatenate([late_a, sum_b.result()], axis=1)
    else:
        late = dot_nn(normed_t, gcat).astype(BF16)
        late_share = lax.psum_scatter(late, all_rows, scatter_dimension=0, tiled=True).astype(F32)
        local = jnp.concatenate([shared + to_chip(shared), local], axis=0)
        local = butterfly(butterfly(local, "context"), "shard")
        out = assemble(out_mine, out_chip, out_a, out_b, where, BF16)
        grad_input = assemble(grad_mine, in_chip, in_a, to_core(in_chip), where, F32)
        bc_sum = butterfly(late_share[:, :wide_bc], "tensor")
    early_share = early_share.astype(F32)

    shared, local = local[:shared_rows], local[shared_rows:]
    first = 16 * dim // inner
    grad_dt_all = local[:first].reshape(16, dim)
    local = local[first:]
    totals = shared[wide + tap_rows]
    entry_count = rows * dim * shards * contexts
    own_features = (lax.axis_index("shard") * contexts + context) * half_rows
    return (
        out.reshape(hidden_in.shape),
        grad_input.reshape(hidden_in.shape),
        shared[:wide].reshape(dim),
        jnp.stack([early_share[:, inner:], late_share[:, wide_bc:]], axis=1),
        bc_sum,
        lax.dynamic_slice_in_dim(grad_dt_all, own_features, half_rows, 1)[:heads].T,
        local[: tap_count + 1],
        shared[wide : wide + tap_rows].reshape(-1)[: 5 * wide_bc].reshape(5, wide_bc),
        local[tap_count + 3, :heads],
        local[tap_count + 4, :heads],
        local[tap_count + 1].reshape(heads, head_dim).sum(1),
        local[tap_count + 2],
        early_share[:, :inner].T,
        jnp.sqrt(totals[0] / entry_count),
        jnp.sqrt(totals[1] / entry_count),
    )


def solution(mesh):
    placed = (
        P("shard", "context", None),
        P(),
        P("shard", None, "tensor"),
        P("shard", None),
        P("shard", "tensor"),
        P(None, "tensor"),
        P(),
        P("tensor"),
        P("tensor"),
        P("tensor"),
        P("tensor"),
        P("tensor", "shard"),
        P("shard", "context", None),
    )
    return jax.shard_map(
        on_device,
        mesh=mesh,
        in_specs=placed,
        out_specs=(
            P("shard", "context", None),
            P("shard", "context", None),
            P(),
            P(("shard", "context"), None, "tensor"),
            P(("shard", "context"), None),
            P(("shard", "context"), "tensor"),
            P(None, "tensor"),
            P(),
            P("tensor"),
            P("tensor"),
            P("tensor"),
            P("tensor"),
            P("tensor", ("shard", "context")),
            P(),
            P(),
        ),
        check_vma=False,
    )
```

```python
import functools

import jax
import jax.numpy as jnp
from jax import lax
from jax.experimental import pallas as pl
from jax.experimental.pallas import tpu as pltpu
from jax.sharding import PartitionSpec as P

CH = 256
EPSILON = 1e-05
LANES = 128
HALO = 8
F32 = jnp.float32
BF16 = jnp.bfloat16


def swap_pairs(size, by):
    return [(i, i ^ by) for i in range(size)]


def butterfly(value, axis):
    size = lax.axis_size(axis)
    if size & (size - 1):
        return lax.psum(value, axis)
    by = 1
    while by < size:
        value = value + lax.ppermute(value, axis, swap_pairs(size, by))
        by *= 2
    return value


def shifted(array, axis, by):
    length = lax.axis_size(axis)
    pairs = [(i, i + by) for i in range(length) if 0 <= i + by < length]
    return lax.ppermute(array, axis, pairs)


def joint_pairs(size, context, sources, move):
    return [(i * context + c, move(i, c)[0] * context + move(i, c)[1]) for i in sources for c in range(context)]


class Gather:
    def __init__(self, local):
        self.shards, self.here, self.side = lax.axis_size("shard"), lax.axis_index("shard"), lax.axis_index("context")
        self.rows = local.shape[0] // 2
        self.local = local
        self.plus = self.minus = lax.dynamic_slice_in_dim(local, self.side * self.rows, self.rows, 0)
        self.k = 0
        self.pieces, self.places = [], []

    def step(self):
        self.k += 1
        size = self.shards
        self.plus = lax.ppermute(self.plus, "shard", [(i, i + 1) for i in range(self.k - 1, size - 1)])
        self.minus = lax.ppermute(self.minus, "shard", [(i, i - 1) for i in range(1, size - self.k + 1)])

    def add(self, piece, valid, source, side):
        self.pieces.append(piece)
        self.places.append(jnp.where(valid, source * 2 + side, -1))

    def cross(self):
        k, size = self.k, self.shards
        axes = ("shard", "context")
        across_plus = lax.ppermute(self.plus, axes, joint_pairs(size, 2, range(k, size), lambda i, c: (i, 1 - c)))
        across_minus = lax.ppermute(self.minus, axes, joint_pairs(size, 2, range(0, size - k), lambda i, c: (i, 1 - c)))
        for piece, side in ((self.plus, self.side), (across_plus, 1 - self.side)):
            self.add(piece, self.here >= k, self.here - k, side)
        for piece, side in ((self.minus, self.side), (across_minus, 1 - self.side)):
            self.add(piece, self.here + k < size, self.here + k, side)

    def full(self):
        place = jnp.stack([self.here * 2] + self.places).astype(jnp.int32)
        rows, cols = self.rows, self.local.shape[1]
        count = len(self.pieces)
        total = 2 * self.shards * rows
        return pl.pallas_call(
            layout_kernel,
            name="layout",
            grid_spec=pltpu.PrefetchScalarGridSpec(
                num_scalar_prefetch=1,
                grid=(1,),
                in_specs=[pl.BlockSpec((2 * rows, cols), lambda i, q: (0, 0))]
                + [pl.BlockSpec((rows, cols), lambda i, q: (0, 0))] * count,
                out_specs=pl.BlockSpec((total, cols), lambda i, q: (0, 0)),
            ),
            out_shape=jax.ShapeDtypeStruct((total, cols), self.local.dtype),
            compiler_params=params(),
            cost_estimate=cost(0, 2 * (2 * total + count * rows) * cols, 0),
        )(place, self.local, *self.pieces)


def layout_kernel(place, local, *rest):
    out = rest[-1]
    rows = rest[0].shape[0]
    out[pl.ds(pl.multiple_of(place[0] * rows, rows), 2 * rows), :] = local[...]
    for k, piece in enumerate(rest[:-1]):

        @pl.when(place[k + 1] >= 0)
        def _():
            out[pl.ds(pl.multiple_of(place[k + 1] * rows, rows), rows), :] = piece[...]


class LineSum:
    def __init__(self):
        self.size, self.here = lax.axis_size("shard"), lax.axis_index("shard")
        self.k = 0

    def piece(self, at):
        pieces = (self.outer[0], self.inner[0], self.inner[1], self.outer[1])
        return jnp.where(at == 0, pieces[0], jnp.where(at == 1, pieces[1], jnp.where(at == 2, pieces[2], pieces[3])))

    def send(self, up, down):
        self.k += 1
        self.plus = lax.ppermute(up, "shard", [(i, i + 1) for i in range(self.k)])
        self.minus = lax.ppermute(down, "shard", [(self.size - 1 - i, self.size - 2 - i) for i in range(self.k)])

    def first(self, keep, got):
        self.outer = add_low(keep, got)
        self.send(self.outer[1], self.outer[0])

    def second(self, keep, got):
        self.inner = add_low(keep, got)
        up = jnp.where(self.here == 0, self.inner[1], self.outer[1])
        down = jnp.where(self.here == 3, self.inner[0], self.outer[0])
        self.send(add_low(up, self.plus), add_low(down, self.minus))

    def third(self):
        self.send(add_low(self.piece(self.here + 1), self.plus), add_low(self.piece(self.here - 1), self.minus))

    def result(self):
        return self.piece(self.here).astype(F32) + self.plus.astype(F32) + self.minus.astype(F32)


def together(*values):
    return lax.optimization_barrier(values)


def to_core(value):
    return lax.ppermute(value, "tensor", swap_pairs(lax.axis_size("tensor"), 1))


def to_chip(value):
    return lax.ppermute(value, "tensor", swap_pairs(lax.axis_size("tensor"), 2))


def add_low(a, b):
    return (a.astype(F32) + b.astype(F32)).astype(BF16)


def assemble_kernel(place, own, chip, core_a, core_b, out):
    r = pl.program_id(0)
    for k, ref in enumerate((own, chip, core_a, core_b)):

        @pl.when(r == k)
        def _():
            out[...] = ref[...].astype(out.dtype)


def assemble(mine, chip, core_a, core_b, place, dtype):
    rows, cols = mine.shape
    piece = pl.BlockSpec((rows, cols), lambda r, q: (0, 0))
    return pl.pallas_call(
        assemble_kernel,
        name="assemble",
        grid_spec=pltpu.PrefetchScalarGridSpec(
            num_scalar_prefetch=1,
            grid=(4,),
            in_specs=[piece] * 4,
            out_specs=pl.BlockSpec((rows, cols), lambda r, q: (r ^ q[0], 0)),
        ),
        out_shape=jax.ShapeDtypeStruct((4 * rows, cols), dtype),
        compiler_params=params(),
        cost_estimate=cost(0, 12 * rows * cols + 0, 0),
    )(place, mine, chip, core_a, core_b)


def dot_nn(a, b):
    return lax.dot_general(a, b, (((1,), (0,)), ((), ())), preferred_element_type=F32)


def dot_nt(a, b):
    return lax.dot_general(a, b, (((1,), (1,)), ((), ())), preferred_element_type=F32)


def dot_tn(a, b):
    return lax.dot_general(a, b, (((0,), (0,)), ((), ())), preferred_element_type=F32)


def by_heads(values, onehot):
    high = values.astype(BF16)
    low = (values - high.astype(F32)).astype(BF16)
    return dot_nn(high, onehot) + dot_nn(low, onehot)


def by_heads_t(values, onehot):
    high = values.astype(BF16)
    low = (values - high.astype(F32)).astype(BF16)
    return dot_nt(high, onehot) + dot_nt(low, onehot)


def row_of(values, onehot):
    return by_heads(jnp.broadcast_to(values, (8, values.shape[1])), onehot)[0:1]


def fold_rows(values):
    rows, cols = values.shape
    return jnp.sum(values.reshape(rows // 8, 8, cols), axis=0)


def exact_parts(values):
    high = values.astype(BF16)
    rest = values - high.astype(F32)
    mid = rest.astype(BF16)
    low = (rest - mid.astype(F32)).astype(BF16)
    return high, mid, low


def sigmoid(values):
    return 1.0 / (1.0 + jnp.exp(-values))


def whole(shape):
    zeros = (0,) * len(shape)
    return pl.BlockSpec(shape, lambda *_: zeros)


def params(semantics=("arbitrary",)):
    return pltpu.CompilerParams(dimension_semantics=semantics, vmem_limit_bytes=60 * 1024 * 1024)


def cost(flops, nbytes, exps=0):
    return pl.CostEstimate(flops=int(flops), bytes_accessed=int(nbytes), transcendentals=int(exps))


def conv_kernel(normed, halo, weight, taps, act, pre):
    rows = normed.shape[0]
    tap_count = 4
    w = weight[...]
    pre[0:HALO, :] = dot_nn(halo[...], w)
    pre[HALO:, :] = dot_nn(normed[...], w)
    first = HALO - tap_count + 1
    out = taps[tap_count : tap_count + 1, :] + taps[0:1, :] * pre[first : first + rows, :]
    for k in range(1, tap_count):
        out = out + taps[k : k + 1, :] * pre[first + k : first + k + rows, :]
    act[...] = (out * sigmoid(out)).astype(BF16)


def conv_front(normed, halo, weight, taps):
    rows, dim = normed.shape
    cols = taps.shape[1]
    tile = 256
    return pl.pallas_call(
        conv_kernel,
        name="conv_front",
        grid=(cols // tile,),
        in_specs=[
            whole((rows, dim)),
            whole((HALO, dim)),
            pl.BlockSpec((dim, tile), lambda j: (0, j)),
            pl.BlockSpec((8, tile), lambda j: (0, j)),
        ],
        out_specs=[
            pl.BlockSpec((rows, tile), lambda j: (0, j)),
            pl.BlockSpec((rows + HALO, tile), lambda j: (0, j)),
        ],
        out_shape=[
            jax.ShapeDtypeStruct((rows, cols), BF16),
            jax.ShapeDtypeStruct((rows + HALO, cols), F32),
        ],
        compiler_params=params(),
        cost_estimate=cost(2 * rows * dim * cols, 2 * (rows + cols) * dim + 6 * rows * cols, rows * cols),
    )(normed, halo, weight, taps)


def step_kernel(normed, weight, bias, rate, dt, sig, cum, seq, cum_t, before):
    @pl.when(pl.program_id(0) == 0)
    def _():
        before[...] = jnp.zeros_like(before)

    raw = dot_nn(normed[...], weight[...]) + bias[...]
    small = jnp.exp(-jnp.abs(raw))
    dt_val = jnp.maximum(raw, 0.0) + jnp.log1p(small)
    dt[...] = dt_val
    sig[...] = sigmoid(raw)
    rows = raw.shape[0]
    lower = (
        lax.broadcasted_iota(jnp.int32, (rows, rows), 0) >= lax.broadcasted_iota(jnp.int32, (rows, rows), 1)
    ).astype(BF16)
    total = jnp.zeros_like(raw)
    for part in exact_parts(dt_val * rate[...]):
        total = total + dot_nn(lower, part)
    cum[...] = total
    seq[...] = total + before[0:1, :]
    before[...] = before[...] + jnp.broadcast_to(total[rows - 1 : rows, :], before.shape)
    cum_t[...] = jnp.transpose(total)[0:16, :]


def step_sizes(normed, weight, bias, rate, col):
    rows, dim = normed.shape
    block = pl.BlockSpec((CH, LANES), lambda b: (b, 0))
    wide = jax.ShapeDtypeStruct((rows, LANES), F32)
    return pl.pallas_call(
        step_kernel,
        name="step_sizes",
        grid=(rows // CH,),
        in_specs=[
            pl.BlockSpec((CH, dim), lambda b: (b, 0)),
            pl.BlockSpec((dim, LANES), lambda b: (0, col)),
            whole((1, LANES)),
            whole((1, LANES)),
        ],
        out_specs=[block, block, block, block, pl.BlockSpec((16, CH), lambda b: (0, b))],
        out_shape=[wide, wide, wide, wide, jax.ShapeDtypeStruct((16, rows), F32)],
        scratch_shapes=[pltpu.VMEM((8, LANES), F32)],
        compiler_params=params(),
        cost_estimate=cost(2 * rows * dim * LANES, 2 * rows * dim + 20 * rows * LANES, 3 * rows * LANES),
    )(normed, weight, bias, rate)


def ssd_kernel(heads, xa_ref, bm_ref, cm_ref, dt_ref, cum_ref, cum_t_ref, skip, onehot, y_ref, start_ref, end_ref, state):
    @pl.when(pl.program_id(0) == 0)
    def _():
        state[...] = jnp.zeros_like(state)

    hot = onehot[...]
    xa = xa_ref[...].astype(F32)
    bm, cm, cum, cum_t = bm_ref[...], cm_ref[...], cum_ref[...], cum_t_ref[...]
    rows = cum.shape[0]
    last = cum[rows - 1 : rows, :]
    x_dt = xa * by_heads(dt_ref[...], hot)
    before = state[...]
    start_ref[0] = before
    y_ref[...] = by_heads(jnp.exp(cum), hot) * dot_nn(cm, before.astype(BF16)) + skip[...] * xa
    to_end = (x_dt * by_heads(jnp.exp(last - cum), hot)).astype(BF16)
    after = row_of(jnp.exp(last), hot) * before + dot_tn(bm, to_end)
    state[...] = after
    end_ref[...] = after
    x_low = x_dt.astype(BF16)
    scores = dot_nt(cm, bm)
    mask = lax.broadcasted_iota(jnp.int32, (rows, rows), 0) >= lax.broadcasted_iota(jnp.int32, (rows, rows), 1)
    width = xa.shape[1] // heads
    per = LANES // width
    lane = lax.broadcasted_iota(jnp.int32, (rows, LANES), 1) // width
    for group in range(heads // per):
        at = slice(group * LANES, (group + 1) * LANES)
        x_group = x_low[:, at]
        total = y_ref[:, at]
        for k in range(per):
            h = group * per + k
            gap = jnp.where(mask, cum[:, h : h + 1] - cum_t[h : h + 1, :], 0.0)
            weights = jnp.where(mask, jnp.exp(gap) * scores, 0.0).astype(BF16)
            total = total + dot_nn(weights, jnp.where(lane == k, x_group, jnp.zeros_like(x_group)))
        y_ref[:, at] = total


def ssd_forward(act, dt, cum, cum_t, skip, onehot, heads):
    rows = act.shape[0]
    inner = onehot.shape[1]
    blocks = rows // CH
    col = inner // LANES
    wide = pl.BlockSpec((CH, LANES), lambda b: (b, 0))
    return pl.pallas_call(
        functools.partial(ssd_kernel, heads),
        name="ssd_forward",
        grid=(blocks,),
        in_specs=[
            pl.BlockSpec((CH, inner), lambda b: (b, 0)),
            pl.BlockSpec((CH, LANES), lambda b: (b, col)),
            pl.BlockSpec((CH, LANES), lambda b: (b, col + 1)),
            wide,
            wide,
            pl.BlockSpec((16, CH), lambda b: (0, b)),
            whole((1, inner)),
            whole((LANES, inner)),
        ],
        out_specs=[
            pl.BlockSpec((CH, inner), lambda b: (b, 0)),
            pl.BlockSpec((1, LANES, inner), lambda b: (b, 0, 0)),
            whole((LANES, inner)),
        ],
        out_shape=[
            jax.ShapeDtypeStruct((rows, inner), F32),
            jax.ShapeDtypeStruct((blocks, LANES, inner), F32),
            jax.ShapeDtypeStruct((LANES, inner), F32),
        ],
        scratch_shapes=[pltpu.VMEM((LANES, inner), F32)],
        compiler_params=params(),
        cost_estimate=cost(6 * rows * CH * inner, 12 * rows * inner, rows * CH * heads),
    )(act, act, act, dt, cum, cum_t, skip, onehot)


def gate_kernel(normed, grad, w_gate, w_out, y_in, cm, seq, state, gain, onehot, gate_ref, y_ref, gon_ref, stat_ref):
    gate = dot_nn(normed[...], w_gate[...])
    grad_on = dot_nn(grad[...], w_out[...])
    y = y_in[...] + by_heads(jnp.exp(seq[...]), onehot[...]) * dot_nn(cm[...], state[...])
    gated = y * (gate * sigmoid(gate))
    gate_ref[...] = gate
    y_ref[...] = y
    gon_ref[...] = grad_on
    square = jnp.sum(gated * gated, axis=1, keepdims=True)
    inner = jnp.sum(grad_on * gain[...] * gated, axis=1, keepdims=True)
    lane = lax.broadcasted_iota(jnp.int32, (gate.shape[0], LANES), 1)
    both = jnp.where(lane == 0, square, jnp.where(lane == 1, inner, 0.0))
    stat_ref[...] = jnp.transpose(both)[0:8, :]


def gate_stage(normed, grad, w_rest, y_in, act, seq, state, gain, onehot):
    rows, dim = normed.shape
    inner = onehot.shape[1]
    col = inner // LANES
    block = pl.BlockSpec((CH, inner), lambda b: (b, 0))
    full = jax.ShapeDtypeStruct((rows, inner), F32)
    return pl.pallas_call(
        gate_kernel,
        name="gate_stage",
        grid=(rows // CH,),
        in_specs=[
            pl.BlockSpec((CH, dim), lambda b: (b, 0)),
            pl.BlockSpec((CH, dim), lambda b: (b, 0)),
            pl.BlockSpec((dim, inner), lambda b: (0, 0)),
            pl.BlockSpec((dim, inner), lambda b: (0, 1)),
            block,
            pl.BlockSpec((CH, LANES), lambda b: (b, col + 1)),
            pl.BlockSpec((CH, LANES), lambda b: (b, 0)),
            whole((LANES, inner)),
            whole((1, inner)),
            whole((LANES, inner)),
        ],
        out_specs=[block, block, block, pl.BlockSpec((8, CH), lambda b: (0, b))],
        out_shape=[full, full, full, jax.ShapeDtypeStruct((8, rows), F32)],
        compiler_params=params(),
        cost_estimate=cost(4 * rows * dim * inner, 16 * rows * inner + 4 * rows * dim, rows * inner),
    )(normed, grad, w_rest, w_rest, y_in, act, seq, state, gain, onehot)


def back_order(i):
    return jnp.where(i < 2, 2 + i, 3 - i)


def norm_kernel(
    inner_all, place, gate_ref, y_ref, gon_ref, stat, w_out, cm, cum, seq, gain, onehot,
    send, keep, out_in_ref, gy_ref, ggate_ref, gog, gstart, gin, gin_sum,
):
    step = pl.program_id(0)

    @pl.when(step == 0)
    def _():
        gog[...] = jnp.zeros_like(gog)
        gin_sum[...] = jnp.zeros_like(gin_sum)

    columns = jnp.transpose(jnp.concatenate([stat[...]] * (LANES // 8), axis=0))
    scale = lax.rsqrt(columns[:, 0:1] * (1.0 / inner_all) + EPSILON)
    along = columns[:, 1:2] * (1.0 / inner_all)
    gate, y, grad_on = gate_ref[...], y_ref[...], gon_ref[...]
    sig = sigmoid(gate)
    silu = gate * sig
    gated = y * silu
    normed = gated * scale
    out_in = (normed * gain[...]).astype(BF16)
    out_in_ref[...] = out_in
    mixed = dot_nt(out_in, w_out[...]).astype(BF16)

    @pl.when(step < 2)
    def _():
        send[...] = mixed

    @pl.when(step >= 2)
    def _():
        keep[...] = mixed

    gog[...] += fold_rows(grad_on * normed)
    grad_gated = scale * (grad_on * gain[...]) - gated * (scale * scale * scale * along)
    grad_y = (grad_gated * silu).astype(BF16)
    gy_ref[...] = grad_y
    ggate_ref[...] = (grad_gated * y * (sig * (1.0 + gate * (1.0 - sig)))).astype(BF16)
    hot = onehot[...]
    scaled = (grad_y.astype(F32) * by_heads(jnp.exp(cum[...]), hot)).astype(BF16)
    grad_start = dot_tn(cm[...], scaled)
    gstart[0] = grad_start
    rows = gate.shape[0]
    ahead = seq[rows - 1 : rows, :] - cum[rows - 1 : rows, :]
    gin_sum[...] += row_of(jnp.exp(ahead), hot) * grad_start
    gin[...] = gin_sum[...].astype(BF16)


def norm_stage(place, gate, y, grad_on, stat, w_rest, act, cum, seq, gain, onehot, inner_all, dim):
    rows, inner = gate.shape
    col = inner // LANES
    blocks = rows // CH
    at = lambda i, q: back_order(i) ^ q[0]
    block = pl.BlockSpec((CH, inner), lambda i, q: (at(i, q), 0))
    wide = pl.BlockSpec((CH, LANES), lambda i, q: (at(i, q), 0))
    low = jax.ShapeDtypeStruct((rows, inner), BF16)
    half = jax.ShapeDtypeStruct((rows // 2, dim), BF16)
    return pl.pallas_call(
        functools.partial(norm_kernel, inner_all),
        name="norm_stage",
        grid_spec=pltpu.PrefetchScalarGridSpec(
            num_scalar_prefetch=1,
            grid=(blocks,),
            in_specs=[
                block,
                block,
                block,
                pl.BlockSpec((8, CH), lambda i, q: (0, at(i, q))),
                pl.BlockSpec((dim, inner), lambda i, q: (0, 1)),
                pl.BlockSpec((CH, LANES), lambda i, q: (at(i, q), col + 1)),
                wide,
                wide,
                whole((1, inner)),
                whole((LANES, inner)),
            ],
            out_specs=[
                pl.BlockSpec((CH, dim), lambda i, q: (jnp.minimum(i, 1), 0)),
                pl.BlockSpec((CH, dim), lambda i, q: (jnp.minimum(3 - i, 1), 0)),
                block,
                block,
                block,
                whole((8, inner)),
                pl.BlockSpec((1, LANES, inner), lambda i, q: (at(i, q), 0, 0)),
                whole((LANES, inner)),
            ],
            scratch_shapes=[pltpu.VMEM((LANES, inner), F32)],
        ),
        out_shape=[
            half,
            half,
            low,
            low,
            low,
            jax.ShapeDtypeStruct((8, inner), F32),
            jax.ShapeDtypeStruct((blocks, LANES, inner), F32),
            jax.ShapeDtypeStruct((LANES, inner), BF16),
        ],
        compiler_params=params(),
        cost_estimate=cost(2 * rows * dim * inner, 18 * rows * inner + 4 * rows * dim, rows * inner),
    )(place, gate, y, grad_on, stat, w_rest, act, cum, seq, gain, onehot)


def early_kernel(grad_t, out_in, normed_t, ggate, out):
    inner = out_in.shape[1]
    out[:, 0:inner] = dot_nn(grad_t[...], out_in[...]).astype(BF16)
    out[:, inner:] = dot_nn(normed_t[...], ggate[...]).astype(BF16)


def early_grads(grad_t, out_in, normed_t, ggate):
    dim, rows = grad_t.shape
    inner = out_in.shape[1]
    tile = dim // 4
    return pl.pallas_call(
        early_kernel,
        name="early_grads",
        grid=(4,),
        in_specs=[
            pl.BlockSpec((tile, rows), lambda i: (i, 0)),
            whole((rows, inner)),
            pl.BlockSpec((tile, rows), lambda i: (i, 0)),
            whole((rows, inner)),
        ],
        out_specs=pl.BlockSpec((tile, 2 * inner), lambda i: (i, 0)),
        out_shape=jax.ShapeDtypeStruct((dim, 2 * inner), BF16),
        compiler_params=params(),
        cost_estimate=cost(4 * rows * dim * inner, 4 * dim * (rows + inner) + 4 * rows * inner, 0),
    )(grad_t, out_in, normed_t, ggate)


def lower_decay(mask, cum, cum_t, h):
    gap = jnp.where(mask, cum[:, h : h + 1] - cum_t[h : h + 1, :], 0.0)
    return jnp.where(mask, jnp.exp(gap), 0.0)


def ssd_back_kernel(
    heads, xa_ref, bm_ref, cm_ref, gy_ref, y_ref, dt_ref, sig_ref, cum_ref, seq_ref, cum_t_ref,
    start_ref, in_state, gstart_ref, gin, pre_ref, taps, rate, skip, onehot,
    gcat_ref, graw_ref, head_ref, tail_ref, rows_sum, heads_sum, gx, after, ext,
):
    step = pl.program_id(0)
    hot = onehot[...]

    @pl.when(step == 0)
    def _():
        rows_sum[...] = jnp.zeros_like(rows_sum)
        heads_sum[...] = jnp.zeros_like(heads_sum)
        after[...] = gin[...].astype(F32)
        ext[0:HALO, :] = jnp.zeros((HALO, ext.shape[1]), F32)

    cum, cum_t, dt = cum_ref[...], cum_t_ref[...], dt_ref[...]
    bm, cm = bm_ref[...], cm_ref[...]
    rows = cum.shape[0]
    last = cum[rows - 1 : rows, :]
    ahead = seq_ref[rows - 1 : rows, :] - last
    start = start_ref[0] + row_of(jnp.exp(ahead), hot) * in_state[...].astype(F32)
    grad_after = after[...]

    gy = gy_ref[...]
    xa = xa_ref[...].astype(F32)
    inner = xa.shape[1]
    dt_wide = by_heads(dt, hot)
    x_dt = xa * dt_wide
    x_low = x_dt.astype(BF16)
    scores = dot_nt(cm, bm)
    mask = lax.broadcasted_iota(jnp.int32, (rows, rows), 0) >= lax.broadcasted_iota(jnp.int32, (rows, rows), 1)
    width = inner // heads
    per = LANES // width
    lane = lax.broadcasted_iota(jnp.int32, (rows, LANES), 1) // width
    grad_scores = jnp.zeros((rows, rows), F32)
    for group in range(heads // per):
        at = slice(group * LANES, (group + 1) * LANES)
        gy_group, x_group = gy[:, at], x_low[:, at]
        total = jnp.zeros((rows, LANES), F32)
        for k in range(per):
            decay = lower_decay(mask, cum, cum_t, group * per + k)
            gy_head = jnp.where(lane == k, gy_group, jnp.zeros_like(gy_group))
            total = total + dot_tn((decay * scores).astype(BF16), gy_head)
            grad_scores = grad_scores + dot_nt(gy_head, x_group) * decay
        gx[:, at] = total

    end_wide = by_heads(jnp.exp(last - cum), hot)
    after_low = grad_after.astype(BF16)
    from_end = dot_nn(bm, after_low)
    to_end = (x_dt * end_wide).astype(BF16)
    gx_intra = gx[...]
    gx_all = gx_intra + end_wide * from_end
    end_term = to_end.astype(F32) * from_end
    gy_f = gy.astype(F32)
    grad_xa = dt_wide * gx_all + skip[...] * gy_f
    scores_low = grad_scores.astype(BF16)
    gy_scaled = (gy_f * by_heads(jnp.exp(cum), hot)).astype(BF16)
    grad_bm = dot_tn(scores_low, cm) + dot_nt(to_end, after_low)
    grad_cm = dot_nn(scores_low, bm) + dot_nt(gy_scaled, start.astype(BF16))

    grad_dt = by_heads_t(xa * gx_all, hot)
    grad_cum = by_heads_t(
        gy_f * (y_ref[...] - skip[...] * xa) - x_low.astype(F32) * gx_intra - end_term, hot
    )
    decay_row = row_of(jnp.exp(last), hot)
    end_rows = fold_rows(end_term)
    state_rows = fold_rows(grad_after * start) * decay_row
    grad_last = jnp.sum(by_heads_t(end_rows + state_rows, hot), axis=0, keepdims=True)
    upper = (
        lax.broadcasted_iota(jnp.int32, (rows, rows), 0) <= lax.broadcasted_iota(jnp.int32, (rows, rows), 1)
    ).astype(BF16)
    grad_a = jnp.broadcast_to(grad_last, grad_cum.shape)
    for part in exact_parts(grad_cum):
        grad_a = grad_a + dot_nn(upper, part)
    grad_raw = (grad_dt + rate[...] * grad_a) * sig_ref[...]
    graw_ref[...] = grad_raw.astype(BF16)
    heads_sum[0:8, :] += fold_rows(grad_raw)
    heads_sum[8:16, :] += fold_rows(grad_a * dt * rate[...])
    after[...] = gstart_ref[0] + decay_row * grad_after

    tap_count = 4
    first = HALO - tap_count + 1
    base = pl.multiple_of((pl.num_programs(0) - 1 - step) * rows, rows)
    ext[rows : rows + HALO, :] = ext[0:HALO, :]
    rows_sum[8 * tap_count + 8 : 8 * tap_count + 16, 0:inner] += fold_rows(gy_f * xa)
    for at, grad in (
        (slice(0, inner), grad_xa),
        (slice(inner, inner + 2 * LANES), jnp.concatenate([grad_bm, grad_cm], axis=1)),
    ):
        window = pre_ref[pl.ds(base, rows + HALO), at]
        conv = taps[tap_count : tap_count + 1, at] + taps[0:1, at] * window[first : first + rows]
        for k in range(1, tap_count):
            conv = conv + taps[k : k + 1, at] * window[first + k : first + k + rows]
        sig = sigmoid(conv)
        gconv = grad * (sig * (1.0 + conv * (1.0 - sig)))
        ext[0:rows, at] = gconv
        for k in range(tap_count):
            rows_sum[8 * k : 8 * k + 8, at] += fold_rows(gconv * window[first + k : first + k + rows])
        rows_sum[8 * tap_count : 8 * tap_count + 8, at] += fold_rows(gconv)
        gpre = taps[tap_count - 1 : tap_count, at] * gconv
        for k in range(tap_count - 1):
            ahead_by = tap_count - 1 - k
            gpre = gpre + taps[k : k + 1, at] * ext[ahead_by : ahead_by + rows, at]
        gcat_ref[:, at] = gpre.astype(BF16)

        @pl.when(step == 0)
        def _():
            tail_ref[:, at] = gpre[rows - 2 * HALO :, :]

    head_ref[...] = ext[0:HALO, :]


def ssd_backward(act, gy, y, dt, sig, cum, seq, cum_t, starts, in_state, gstart, gin, pre, taps, rate, skip, onehot, heads):
    rows, inner = gy.shape
    col = inner // LANES
    blocks = rows // CH
    total = pre.shape[1]
    top = blocks - 1
    block = pl.BlockSpec((CH, inner), lambda i: (top - i, 0))
    wide = pl.BlockSpec((CH, LANES), lambda i: (top - i, 0))
    state = pl.BlockSpec((1, LANES, inner), lambda i: (top - i, 0, 0))
    return pl.pallas_call(
        functools.partial(ssd_back_kernel, heads),
        name="ssd_backward",
        grid=(blocks,),
        in_specs=[
            block,
            pl.BlockSpec((CH, LANES), lambda i: (top - i, col)),
            pl.BlockSpec((CH, LANES), lambda i: (top - i, col + 1)),
            block,
            block,
            wide,
            wide,
            wide,
            wide,
            pl.BlockSpec((16, CH), lambda i: (0, top - i)),
            state,
            whole((LANES, inner)),
            state,
            whole((LANES, inner)),
            whole((rows + HALO, total)),
            whole((8, total)),
            whole((1, LANES)),
            whole((1, inner)),
            whole((LANES, inner)),
        ],
        out_specs=[
            pl.BlockSpec((CH, total), lambda i: (top - i, 0)),
            wide,
            whole((HALO, total)),
            whole((2 * HALO, total)),
            whole((48, total)),
            whole((16, LANES)),
        ],
        out_shape=[
            jax.ShapeDtypeStruct((rows, total), BF16),
            jax.ShapeDtypeStruct((rows, LANES), BF16),
            jax.ShapeDtypeStruct((HALO, total), F32),
            jax.ShapeDtypeStruct((2 * HALO, total), F32),
            jax.ShapeDtypeStruct((48, total), F32),
            jax.ShapeDtypeStruct((16, LANES), F32),
        ],
        scratch_shapes=[
            pltpu.VMEM((CH, inner), F32),
            pltpu.VMEM((LANES, inner), F32),
            pltpu.VMEM((CH + HALO, total), F32),
        ],
        compiler_params=params(),
        cost_estimate=cost(12 * rows * CH * inner, 24 * rows * inner, rows * CH * heads),
    )(act, act, act, gy, y, dt, sig, cum, seq, cum_t, starts, in_state, gstart, gin, pre, taps, rate, skip, onehot)


def input_kernel(where, gcat, ggate, graw, x_ref, w_gate, w_cat, w_dt, send, keep, gain_sum):
    step = pl.program_id(0)

    @pl.when(step == 0)
    def _():
        gain_sum[...] = jnp.zeros_like(gain_sum)

    total = dot_nt(ggate[...], w_gate[...]) + dot_nt(gcat[...], w_cat[...]) + dot_nt(graw[...], w_dt[...])
    xf = x_ref[...].astype(F32)
    scale = lax.rsqrt(jnp.mean(xf * xf, axis=1, keepdims=True) + EPSILON)
    gain_sum[...] += fold_rows(total * (xf * scale))
    part = total.astype(BF16)

    @pl.when(step < 2)
    def _():
        send[...] = part

    @pl.when(step >= 2)
    def _():
        keep[...] = part


def input_stage(where, gcat, ggate, graw, x, w_rest, w_first):
    rows, dim = x.shape
    inner, total = ggate.shape[1], gcat.shape[1]
    blocks = rows // CH
    at = lambda i, q: (back_order(i) ^ q[0], 0)
    half = jax.ShapeDtypeStruct((rows // 2, dim), BF16)
    return pl.pallas_call(
        input_kernel,
        name="input_stage",
        grid_spec=pltpu.PrefetchScalarGridSpec(
            num_scalar_prefetch=1,
            grid=(blocks,),
            in_specs=[
                pl.BlockSpec((CH, total), at),
                pl.BlockSpec((CH, inner), at),
                pl.BlockSpec((CH, LANES), at),
                pl.BlockSpec((CH, dim), at),
                pl.BlockSpec((dim, inner), lambda i, q: (0, 0)),
                pl.BlockSpec((dim, total), lambda i, q: (0, 0)),
                pl.BlockSpec((dim, LANES), lambda i, q: (0, total // LANES)),
            ],
            out_specs=[
                pl.BlockSpec((CH, dim), lambda i, q: (jnp.minimum(i, 1), 0)),
                pl.BlockSpec((CH, dim), lambda i, q: (jnp.minimum(3 - i, 1), 0)),
                pl.BlockSpec((8, dim), lambda i, q: (0, 0)),
            ],
        ),
        out_shape=[half, half, jax.ShapeDtypeStruct((8, dim), F32)],
        compiler_params=params(),
        cost_estimate=cost(4 * rows * dim * inner, 10 * rows * inner + 2 * rows * dim, 0),
    )(where, gcat, ggate, graw, x, w_rest, w_first, w_first)


def late_kernel(side, normed_t, gcat, keep_a, send_a, keep_b, send_b):
    step = pl.program_id(0)
    result = dot_nn(normed_t[...], gcat[...]).astype(BF16)
    rows = result.shape[0] // 2
    top, bottom = result[:rows], result[rows:]
    mine = side[0] == 0
    keep, send = jnp.where(mine, top, bottom), jnp.where(mine, bottom, top)

    @pl.when(step < 2)
    def _():
        keep_a[0], send_a[0] = keep, send

    @pl.when(step >= 2)
    def _():
        keep_b[0], send_b[0] = keep, send


def late_grads(side, normed_t, gcat):
    dim, rows = normed_t.shape
    width = gcat.shape[1]
    tile = dim // 4
    outer = pl.BlockSpec((1, tile // 2, width), lambda i, q: (jnp.minimum(i, 1), 0, 0))
    inner = pl.BlockSpec((1, tile // 2, width), lambda i, q: (jnp.maximum(i - 2, 0), 0, 0))
    return pl.pallas_call(
        late_kernel,
        name="late_grads",
        grid_spec=pltpu.PrefetchScalarGridSpec(
            num_scalar_prefetch=1,
            grid=(4,),
            in_specs=[
                pl.BlockSpec((tile, rows), lambda i, q: (jnp.where(i < 2, 3 * i, i - 1), 0)),
                pl.BlockSpec((rows, width), lambda i, q: (0, 0)),
            ],
            out_specs=[outer, outer, inner, inner],
        ),
        out_shape=[jax.ShapeDtypeStruct((2, tile // 2, width), BF16)] * 4,
        compiler_params=params(),
        cost_estimate=cost(2 * rows * dim * width, 2 * dim * (rows + width) + 2 * rows * width, 0),
    )(side, normed_t, gcat)


def on_device(
    hidden_in,
    norm_gain,
    w_in_zx,
    w_in_bc,
    w_in_dt,
    conv_x,
    conv_bc,
    dt_bias,
    a_log,
    d_skip,
    out_gain,
    w_out,
    cotangent,
):
    seq_count, rows, dim = hidden_in.shape
    inner = w_in_zx.shape[2]
    heads = w_in_dt.shape[1]
    head_dim = inner // heads
    tap_count = conv_x.shape[0] - 1
    tensor_size, shards, contexts = lax.axis_size("tensor"), lax.axis_size("shard"), lax.axis_size("context")
    inner_all = inner * tensor_size
    blocks = rows // CH
    assert seq_count == 1 and tensor_size == 4 and blocks == 4 and contexts == 2
    shard_rows = w_in_zx.shape[0]
    place = lax.axis_index("tensor")
    context = lax.axis_index("context")
    side_num = place % 2
    quarter = side_num * 2 + place // 2
    where = jnp.stack([quarter, side_num]).astype(jnp.int32)
    col = inner // LANES

    x_rows = hidden_in.reshape(rows, dim)
    g_rows = cotangent.reshape(rows, dim)

    pad_dt = jnp.zeros((shard_rows, LANES - heads), BF16)
    w_front = jnp.concatenate([w_in_zx[:, 1], w_in_bc, w_in_dt, pad_dt], axis=1)
    w_front, w_gate_local, w_out_local = together(w_front, w_in_zx[:, 0], w_out)
    w_back = jnp.concatenate([w_gate_local, w_out_local.T], axis=1)
    half_rows = shard_rows // contexts
    line = shards == 4
    all_rows = ("shard", "context")
    own_half = lambda v: lax.dynamic_slice_in_dim(v, context * half_rows, half_rows, 0)
    w_rest = lax.all_gather(own_half(w_back), all_rows, axis=0, tiled=True)
    if line:
        front = Gather(w_front)
        front.step()
    halo_rows = shifted(x_rows[rows - HALO :], "context", 1)

    def norm_of(values):
        wide = values.astype(F32)
        scale = lax.rsqrt(jnp.mean(wide * wide, axis=-1, keepdims=True) + EPSILON)
        return (wide * scale * norm_gain).astype(BF16)

    normed = norm_of(x_rows)
    halo = norm_of(halo_rows)

    pad_heads = lambda v: jnp.pad(v, (0, LANES - heads)).reshape(1, LANES)
    rate = pad_heads(-jnp.exp(a_log))
    bias = pad_heads(dt_bias)
    skip = jnp.repeat(d_skip, head_dim).reshape(1, inner)
    gain = out_gain.reshape(1, inner)
    taps = jnp.pad(jnp.concatenate([conv_x, conv_bc], axis=1), ((0, 8 - tap_count - 1), (0, 0)))
    onehot = (
        lax.broadcasted_iota(jnp.int32, (LANES, inner), 0)
        == lax.broadcasted_iota(jnp.int32, (LANES, inner), 1) // head_dim
    ).astype(BF16)

    if line:
        front.plus, front.minus, normed = together(front.plus, front.minus, normed)
        front.cross()
        front.step()
        front.plus, front.minus, halo = together(front.plus, front.minus, halo)
        front.cross()
        front.step()
        front.plus, front.minus = together(front.plus, front.minus)
        front.cross()
        w_first = front.full()
    else:
        w_first = lax.all_gather(own_half(w_front), all_rows, axis=0, tiled=True)

    act, pre = conv_front(normed, halo, w_first, taps)
    dt, sig, cum, seq, cum_t = step_sizes(normed, w_first, bias, rate, col + 2)
    y_local, starts, end_state = ssd_forward(act, dt, cum, cum_t, skip, onehot, heads)
    in_state = shifted(end_state.astype(BF16), "context", 1)
    normed_low, g_low, y_local = together(normed, g_rows, y_local)
    normed_t, grad_t = normed_low.T, g_low.T
    in_state, normed_t, grad_t = together(in_state, normed_t, grad_t)
    gate, y, grad_on, stat = gate_stage(normed, g_rows, w_rest, y_local, act, seq, in_state, gain, onehot)
    stat = butterfly(stat, "tensor")
    send, keep, out_in, gy, ggate, gog, gstart, gin_first = norm_stage(
        where, gate, y, grad_on, stat, w_rest, act, cum, seq, gain, onehot, inner_all, dim
    )

    own_rows = rows // 4
    gin = shifted(gin_first, "context", -1)
    got = to_core(send)
    early = early_grads(grad_t, out_in, normed_t, ggate)
    gy, gin, early, got = together(gy, gin, early, got)
    early_share = lax.psum_scatter(early, ("shard", "context"), scatter_dimension=0, tiled=True)
    got_mine = to_chip(add_low(keep[own_rows:], got[own_rows:]))
    gcat, graw, head, end_rows, rows_sum, heads_sum = ssd_backward(
        act, gy, y, dt, sig, cum, seq, cum_t, starts, in_state, gstart, gin, pre, taps, rate, skip, onehot, heads
    )
    gcat, head, got_mine = together(gcat, head, got_mine)
    halo_in = shifted(head, "context", -1)
    mixed_mine = keep[:own_rows].astype(F32) + got[:own_rows].astype(F32) + got_mine.astype(F32)
    x_mine = lax.dynamic_slice_in_dim(x_rows, quarter * own_rows, own_rows, 0).astype(F32)
    stream_mine = x_mine + mixed_mine
    out_mine = stream_mine.astype(BF16)
    out_chip = to_chip(out_mine)
    out_a = to_core(out_mine)
    halo_in, out_mine = together(halo_in, out_mine)
    beyond = jnp.concatenate([jnp.zeros((2 * HALO, halo_in.shape[1]), F32), halo_in], axis=0)
    for k in range(tap_count - 1):
        ahead = tap_count - 1 - k
        end_rows = end_rows + taps[k : k + 1] * beyond[ahead : ahead + 2 * HALO]
    gcat = lax.dynamic_update_slice_in_dim(gcat, end_rows.astype(BF16), rows - 2 * HALO, 0)
    wide_bc = 2 * LANES
    if line:
        keep_a, send_a, keep_b, send_b = late_grads(context.astype(jnp.int32).reshape(1), normed_t, gcat)
        gcat, keep_a, send_a, send_b = together(gcat, keep_a, send_a, send_b)
        x_got_a = lax.ppermute(send_a, "context", swap_pairs(2, 1))
    send, keep, gain_sum = input_stage(where, gcat, ggate, graw, x_rows, w_rest, w_first)

    send, keep, gain_sum, out_chip, out_a, rows_sum, graw, gog, stream_late, mixed_late = together(
        send, keep, gain_sum, out_chip, out_a, rows_sum, graw, gog, stream_mine, mixed_mine
    )
    if line:
        send, gain_sum, x_got_a, send_b = together(send, gain_sum, x_got_a, send_b)
        x_got_b = lax.ppermute(send_b, "context", swap_pairs(2, 1))
        late_sum = LineSum()
        late_sum.first(keep_a, x_got_a)
    got = to_core(send)
    out_b = to_core(out_chip)

    wide = dim // inner
    tap_rows = -(-5 * wide_bc // inner)
    tap_sums = rows_sum.reshape(6, 8, -1).sum(1)
    taps_flat = jnp.pad(tap_sums[:5, inner:].reshape(-1), (0, tap_rows * inner - 5 * wide_bc))
    shared = jnp.concatenate(
        [
            gain_sum.sum(0).reshape(wide, inner),
            taps_flat.reshape(tap_rows, inner),
            jnp.pad(
                jnp.stack([jnp.sum(stream_late * stream_late), jnp.sum(mixed_late * mixed_late)]).reshape(1, 2),
                ((0, 0), (0, inner - 2)),
            ),
        ],
        axis=0,
    )
    shared = jnp.pad(shared, ((0, -shared.shape[0] % 8), (0, 0)))
    shared_rows = shared.shape[0]
    grad_dt_t = dot_tn(graw[:, :16], normed)
    local = jnp.concatenate(
        [
            grad_dt_t.reshape(-1, inner),
            tap_sums[:, :inner],
            gog.sum(0, keepdims=True),
            jnp.pad(heads_sum.reshape(2, 8, LANES).sum(1), ((0, 0), (0, inner - LANES))),
        ],
        axis=0,
    )
    local = jnp.pad(local, ((0, -local.shape[0] % 8), (0, 0)))
    local = jnp.concatenate([shared, local], axis=0)
    if line:
        got, local, out_b, late_sum.plus, late_sum.minus = together(got, local, out_b, late_sum.plus, late_sum.minus)
    got_mine = to_chip(add_low(keep[own_rows:], got[own_rows:]))
    out = assemble(out_mine, out_chip, out_a, out_b, where, BF16)
    if line:
        local = local + lax.ppermute(local, "shard", swap_pairs(shards, 1))
        x_got_b, out, local = together(x_got_b, out, local)
        late_sum.second(keep_b, x_got_b)
        local = local + lax.ppermute(local, "shard", swap_pairs(shards, 2))
        got_mine, late_sum.inner = together(got_mine, late_sum.inner)

    grad_normed = keep[:own_rows].astype(F32) + got[:own_rows].astype(F32) + got_mine.astype(F32)
    scale_mine = lax.rsqrt(jnp.mean(x_mine * x_mine, axis=-1, keepdims=True) + EPSILON)
    g_mine = lax.dynamic_slice_in_dim(g_rows, quarter * own_rows, own_rows, 0).astype(F32)
    grad_un = grad_normed * norm_gain
    grad_mine = (
        g_mine
        + scale_mine * grad_un
        - x_mine * scale_mine**3 * jnp.mean(grad_un * x_mine, axis=-1, keepdims=True)
    ).astype(BF16)
    in_chip = to_chip(grad_mine)
    in_a = to_core(grad_mine)
    if line:
        late_sum.plus, late_sum.minus, local, grad_mine = together(late_sum.plus, late_sum.minus, local, grad_mine)
        late_sum.third()
        local = local + lax.ppermute(local, "context", swap_pairs(2, 1))
        late_sum.plus, late_sum.minus, local, in_chip, in_a, early_share = together(
            late_sum.plus, late_sum.minus, local, in_chip, in_a, early_share
        )
        in_b = to_core(in_chip)
        late_share = late_sum.result()
    else:
        late = dot_nn(normed_t, gcat).astype(BF16)
        late_share = lax.psum_scatter(late, all_rows, scatter_dimension=0, tiled=True).astype(F32)
        local = butterfly(butterfly(local, "context"), "shard")
        in_b = to_core(in_chip)
    early_share = early_share.astype(F32)

    shared, local = local[:shared_rows], local[shared_rows:]
    sums = jnp.concatenate([late_share[:, inner:], shared.reshape(-1, wide_bc)], axis=0)
    sums = sums + to_core(sums)
    sums, in_b = together(sums, in_b)
    sums = sums + to_chip(sums)
    grad_input = assemble(grad_mine, in_chip, in_a, in_b, where, F32)
    bc_sum, shared = sums[:half_rows], sums[half_rows:].reshape(shared_rows, inner)
    first = 16 * dim // inner
    grad_dt_all = local[:first].reshape(16, dim)
    local = local[first:]
    totals = shared[wide + tap_rows]
    entry_count = rows * dim * shards * contexts
    own_features = (lax.axis_index("shard") * contexts + context) * half_rows
    return (
        out.reshape(hidden_in.shape),
        grad_input.reshape(hidden_in.shape),
        shared[:wide].reshape(dim),
        jnp.stack([early_share[:, inner:], late_share[:, :inner]], axis=1),
        bc_sum,
        lax.dynamic_slice_in_dim(grad_dt_all, own_features, half_rows, 1)[:heads].T,
        local[: tap_count + 1],
        shared[wide : wide + tap_rows].reshape(-1)[: 5 * wide_bc].reshape(5, wide_bc),
        local[tap_count + 3, :heads],
        local[tap_count + 4, :heads],
        local[tap_count + 1].reshape(heads, head_dim).sum(1),
        local[tap_count + 2],
        early_share[:, :inner].T,
        jnp.sqrt(totals[0] / entry_count),
        jnp.sqrt(totals[1] / entry_count),
    )


def solution(mesh):
    placed = (
        P("shard", "context", None),
        P(),
        P("shard", None, "tensor"),
        P("shard", None),
        P("shard", "tensor"),
        P(None, "tensor"),
        P(),
        P("tensor"),
        P("tensor"),
        P("tensor"),
        P("tensor"),
        P("tensor", "shard"),
        P("shard", "context", None),
    )
    return jax.shard_map(
        on_device,
        mesh=mesh,
        in_specs=placed,
        out_specs=(
            P("shard", "context", None),
            P("shard", "context", None),
            P(),
            P(("shard", "context"), None, "tensor"),
            P(("shard", "context"), None),
            P(("shard", "context"), "tensor"),
            P(None, "tensor"),
            P(),
            P("tensor"),
            P("tensor"),
            P("tensor"),
            P("tensor"),
            P("tensor", ("shard", "context")),
            P(),
            P(),
        ),
        check_vma=False,
    )
```

```python
import functools

import jax
import jax.numpy as jnp
from jax import lax
from jax.experimental import pallas as pl
from jax.experimental.pallas import tpu as pltpu
from jax.sharding import PartitionSpec as P

CH = 256
EPSILON = 1e-05
LANES = 128
HALO = 8
F32 = jnp.float32
BF16 = jnp.bfloat16


def swap_pairs(size, by):
    return [(i, i ^ by) for i in range(size)]


def butterfly(value, axis):
    size = lax.axis_size(axis)
    if size & (size - 1):
        return lax.psum(value, axis)
    by = 1
    while by < size:
        value = value + lax.ppermute(value, axis, swap_pairs(size, by))
        by *= 2
    return value


def shifted(array, axis, by):
    length = lax.axis_size(axis)
    pairs = [(i, i + by) for i in range(length) if 0 <= i + by < length]
    return lax.ppermute(array, axis, pairs)


def joint_pairs(size, context, sources, move):
    return [(i * context + c, move(i, c)[0] * context + move(i, c)[1]) for i in sources for c in range(context)]


class Gather:
    def __init__(self, local):
        self.shards, self.here, self.side = lax.axis_size("shard"), lax.axis_index("shard"), lax.axis_index("context")
        self.rows = local.shape[0] // 2
        self.local = local
        self.plus = self.minus = lax.dynamic_slice_in_dim(local, self.side * self.rows, self.rows, 0)
        self.k = 0
        self.pieces, self.places = [], []

    def step(self):
        self.k += 1
        size = self.shards
        self.plus = lax.ppermute(self.plus, "shard", [(i, i + 1) for i in range(self.k - 1, size - 1)])
        self.minus = lax.ppermute(self.minus, "shard", [(i, i - 1) for i in range(1, size - self.k + 1)])

    def add(self, piece, valid, source, side):
        self.pieces.append(piece)
        self.places.append(jnp.where(valid, source * 2 + side, -1))

    def cross(self):
        k, size = self.k, self.shards
        axes = ("shard", "context")
        across_plus = lax.ppermute(self.plus, axes, joint_pairs(size, 2, range(k, size), lambda i, c: (i, 1 - c)))
        across_minus = lax.ppermute(self.minus, axes, joint_pairs(size, 2, range(0, size - k), lambda i, c: (i, 1 - c)))
        for piece, side in ((self.plus, self.side), (across_plus, 1 - self.side)):
            self.add(piece, self.here >= k, self.here - k, side)
        for piece, side in ((self.minus, self.side), (across_minus, 1 - self.side)):
            self.add(piece, self.here + k < size, self.here + k, side)

    def full(self):
        place = jnp.stack([self.here * 2] + self.places).astype(jnp.int32)
        rows, cols = self.rows, self.local.shape[1]
        count = len(self.pieces)
        total = 2 * self.shards * rows
        return pl.pallas_call(
            layout_kernel,
            name="layout",
            grid_spec=pltpu.PrefetchScalarGridSpec(
                num_scalar_prefetch=1,
                grid=(1,),
                in_specs=[pl.BlockSpec((2 * rows, cols), lambda i, q: (0, 0))]
                + [pl.BlockSpec((rows, cols), lambda i, q: (0, 0))] * count,
                out_specs=pl.BlockSpec((total, cols), lambda i, q: (0, 0)),
            ),
            out_shape=jax.ShapeDtypeStruct((total, cols), self.local.dtype),
            compiler_params=params(),
            cost_estimate=cost(0, 2 * (2 * total + count * rows) * cols, 0),
        )(place, self.local, *self.pieces)


def layout_kernel(place, local, *rest):
    out = rest[-1]
    rows = rest[0].shape[0]
    out[pl.ds(pl.multiple_of(place[0] * rows, rows), 2 * rows), :] = local[...]
    for k, piece in enumerate(rest[:-1]):

        @pl.when(place[k + 1] >= 0)
        def _():
            out[pl.ds(pl.multiple_of(place[k + 1] * rows, rows), rows), :] = piece[...]


class LineSum:
    def __init__(self):
        self.size, self.here = lax.axis_size("shard"), lax.axis_index("shard")
        self.k = 0

    def piece(self, at):
        pieces = (self.outer[0], self.inner[0], self.inner[1], self.outer[1])
        return jnp.where(at == 0, pieces[0], jnp.where(at == 1, pieces[1], jnp.where(at == 2, pieces[2], pieces[3])))

    def send(self, up, down):
        self.k += 1
        self.plus = lax.ppermute(up, "shard", [(i, i + 1) for i in range(self.k)])
        self.minus = lax.ppermute(down, "shard", [(self.size - 1 - i, self.size - 2 - i) for i in range(self.k)])

    def first(self, keep, got):
        self.outer = add_low(keep, got)
        self.send(self.outer[1], self.outer[0])

    def second(self, keep, got):
        self.inner = add_low(keep, got)
        up = jnp.where(self.here == 0, self.inner[1], self.outer[1])
        down = jnp.where(self.here == 3, self.inner[0], self.outer[0])
        self.send(add_low(up, self.plus), add_low(down, self.minus))

    def third(self):
        self.send(add_low(self.piece(self.here + 1), self.plus), add_low(self.piece(self.here - 1), self.minus))

    def result(self):
        return self.piece(self.here).astype(F32) + self.plus.astype(F32) + self.minus.astype(F32)


def together(*values):
    return lax.optimization_barrier(values)


def to_core(value):
    return lax.ppermute(value, "tensor", swap_pairs(lax.axis_size("tensor"), 1))


def to_chip(value):
    return lax.ppermute(value, "tensor", swap_pairs(lax.axis_size("tensor"), 2))


def add_low(a, b):
    return (a.astype(F32) + b.astype(F32)).astype(BF16)


def assemble_kernel(place, own, chip, core_a, core_b, out):
    r = pl.program_id(0)
    for k, ref in enumerate((own, chip, core_a, core_b)):

        @pl.when(r == k)
        def _():
            out[...] = ref[...].astype(out.dtype)


def assemble(mine, chip, core_a, core_b, place, dtype):
    rows, cols = mine.shape
    piece = pl.BlockSpec((rows, cols), lambda r, q: (0, 0))
    return pl.pallas_call(
        assemble_kernel,
        name="assemble",
        grid_spec=pltpu.PrefetchScalarGridSpec(
            num_scalar_prefetch=1,
            grid=(4,),
            in_specs=[piece] * 4,
            out_specs=pl.BlockSpec((rows, cols), lambda r, q: (r ^ q[0], 0)),
        ),
        out_shape=jax.ShapeDtypeStruct((4 * rows, cols), dtype),
        compiler_params=params(),
        cost_estimate=cost(0, 12 * rows * cols + 0, 0),
    )(place, mine, chip, core_a, core_b)


def dot_nn(a, b):
    return lax.dot_general(a, b, (((1,), (0,)), ((), ())), preferred_element_type=F32)


def dot_nt(a, b):
    return lax.dot_general(a, b, (((1,), (1,)), ((), ())), preferred_element_type=F32)


def dot_tn(a, b):
    return lax.dot_general(a, b, (((0,), (0,)), ((), ())), preferred_element_type=F32)


def by_heads(values, onehot):
    high = values.astype(BF16)
    low = (values - high.astype(F32)).astype(BF16)
    return dot_nn(high, onehot) + dot_nn(low, onehot)


def by_heads_t(values, onehot):
    high = values.astype(BF16)
    low = (values - high.astype(F32)).astype(BF16)
    return dot_nt(high, onehot) + dot_nt(low, onehot)


def row_of(values, onehot):
    return by_heads(jnp.broadcast_to(values, (8, values.shape[1])), onehot)[0:1]


def fold_rows(values):
    rows, cols = values.shape
    return jnp.sum(values.reshape(rows // 8, 8, cols), axis=0)


def exact_parts(values):
    high = values.astype(BF16)
    rest = values - high.astype(F32)
    mid = rest.astype(BF16)
    low = (rest - mid.astype(F32)).astype(BF16)
    return high, mid, low


def sigmoid(values):
    return 1.0 / (1.0 + jnp.exp(-values))


def whole(shape):
    zeros = (0,) * len(shape)
    return pl.BlockSpec(shape, lambda *_: zeros)


def params(semantics=("arbitrary",)):
    return pltpu.CompilerParams(dimension_semantics=semantics, vmem_limit_bytes=60 * 1024 * 1024)


def cost(flops, nbytes, exps=0):
    return pl.CostEstimate(flops=int(flops), bytes_accessed=int(nbytes), transcendentals=int(exps))


def conv_kernel(normed, halo, weight, taps, act, pre):
    rows = normed.shape[0]
    tap_count = 4
    w = weight[...]
    pre[0:HALO, :] = dot_nn(halo[...], w)
    pre[HALO:, :] = dot_nn(normed[...], w)
    first = HALO - tap_count + 1
    out = taps[tap_count : tap_count + 1, :] + taps[0:1, :] * pre[first : first + rows, :]
    for k in range(1, tap_count):
        out = out + taps[k : k + 1, :] * pre[first + k : first + k + rows, :]
    act[...] = (out * sigmoid(out)).astype(BF16)


def conv_front(normed, halo, weight, taps):
    rows, dim = normed.shape
    cols = taps.shape[1]
    tile = 256
    return pl.pallas_call(
        conv_kernel,
        name="conv_front",
        grid=(cols // tile,),
        in_specs=[
            whole((rows, dim)),
            whole((HALO, dim)),
            pl.BlockSpec((dim, tile), lambda j: (0, j)),
            pl.BlockSpec((8, tile), lambda j: (0, j)),
        ],
        out_specs=[
            pl.BlockSpec((rows, tile), lambda j: (0, j)),
            pl.BlockSpec((rows + HALO, tile), lambda j: (0, j)),
        ],
        out_shape=[
            jax.ShapeDtypeStruct((rows, cols), BF16),
            jax.ShapeDtypeStruct((rows + HALO, cols), F32),
        ],
        compiler_params=params(),
        cost_estimate=cost(2 * rows * dim * cols, 2 * (rows + cols) * dim + 6 * rows * cols, rows * cols),
    )(normed, halo, weight, taps)


def step_kernel(normed, weight, bias, rate, dt, sig, cum, seq, cum_t, before):
    @pl.when(pl.program_id(0) == 0)
    def _():
        before[...] = jnp.zeros_like(before)

    raw = dot_nn(normed[...], weight[...]) + bias[...]
    small = jnp.exp(-jnp.abs(raw))
    dt_val = jnp.maximum(raw, 0.0) + jnp.log1p(small)
    dt[...] = dt_val
    sig[...] = sigmoid(raw)
    rows = raw.shape[0]
    lower = (
        lax.broadcasted_iota(jnp.int32, (rows, rows), 0) >= lax.broadcasted_iota(jnp.int32, (rows, rows), 1)
    ).astype(BF16)
    total = jnp.zeros_like(raw)
    for part in exact_parts(dt_val * rate[...]):
        total = total + dot_nn(lower, part)
    cum[...] = total
    seq[...] = total + before[0:1, :]
    before[...] = before[...] + jnp.broadcast_to(total[rows - 1 : rows, :], before.shape)
    cum_t[...] = jnp.transpose(total)[0:16, :]


def step_sizes(normed, weight, bias, rate, col):
    rows, dim = normed.shape
    block = pl.BlockSpec((CH, LANES), lambda b: (b, 0))
    wide = jax.ShapeDtypeStruct((rows, LANES), F32)
    return pl.pallas_call(
        step_kernel,
        name="step_sizes",
        grid=(rows // CH,),
        in_specs=[
            pl.BlockSpec((CH, dim), lambda b: (b, 0)),
            pl.BlockSpec((dim, LANES), lambda b: (0, col)),
            whole((1, LANES)),
            whole((1, LANES)),
        ],
        out_specs=[block, block, block, block, pl.BlockSpec((16, CH), lambda b: (0, b))],
        out_shape=[wide, wide, wide, wide, jax.ShapeDtypeStruct((16, rows), F32)],
        scratch_shapes=[pltpu.VMEM((8, LANES), F32)],
        compiler_params=params(),
        cost_estimate=cost(2 * rows * dim * LANES, 2 * rows * dim + 20 * rows * LANES, 3 * rows * LANES),
    )(normed, weight, bias, rate)


def ssd_kernel(heads, xa_ref, bm_ref, cm_ref, dt_ref, cum_ref, cum_t_ref, skip, onehot, y_ref, start_ref, end_ref, state):
    @pl.when(pl.program_id(0) == 0)
    def _():
        state[...] = jnp.zeros_like(state)

    hot = onehot[...]
    xa = xa_ref[...].astype(F32)
    bm, cm, cum, cum_t = bm_ref[...], cm_ref[...], cum_ref[...], cum_t_ref[...]
    rows = cum.shape[0]
    last = cum[rows - 1 : rows, :]
    x_dt = xa * by_heads(dt_ref[...], hot)
    before = state[...]
    start_ref[0] = before
    y_ref[...] = by_heads(jnp.exp(cum), hot) * dot_nn(cm, before.astype(BF16)) + skip[...] * xa
    to_end = (x_dt * by_heads(jnp.exp(last - cum), hot)).astype(BF16)
    after = row_of(jnp.exp(last), hot) * before + dot_tn(bm, to_end)
    state[...] = after
    end_ref[...] = after
    x_low = x_dt.astype(BF16)
    scores = dot_nt(cm, bm)
    mask = lax.broadcasted_iota(jnp.int32, (rows, rows), 0) >= lax.broadcasted_iota(jnp.int32, (rows, rows), 1)
    width = xa.shape[1] // heads
    per = LANES // width
    lane = lax.broadcasted_iota(jnp.int32, (rows, LANES), 1) // width
    for group in range(heads // per):
        at = slice(group * LANES, (group + 1) * LANES)
        x_group = x_low[:, at]
        total = y_ref[:, at]
        for k in range(per):
            h = group * per + k
            gap = jnp.where(mask, cum[:, h : h + 1] - cum_t[h : h + 1, :], 0.0)
            weights = jnp.where(mask, jnp.exp(gap) * scores, 0.0).astype(BF16)
            total = total + dot_nn(weights, jnp.where(lane == k, x_group, jnp.zeros_like(x_group)))
        y_ref[:, at] = total


def ssd_forward(act, dt, cum, cum_t, skip, onehot, heads):
    rows = act.shape[0]
    inner = onehot.shape[1]
    blocks = rows // CH
    col = inner // LANES
    wide = pl.BlockSpec((CH, LANES), lambda b: (b, 0))
    return pl.pallas_call(
        functools.partial(ssd_kernel, heads),
        name="ssd_forward",
        grid=(blocks,),
        in_specs=[
            pl.BlockSpec((CH, inner), lambda b: (b, 0)),
            pl.BlockSpec((CH, LANES), lambda b: (b, col)),
            pl.BlockSpec((CH, LANES), lambda b: (b, col + 1)),
            wide,
            wide,
            pl.BlockSpec((16, CH), lambda b: (0, b)),
            whole((1, inner)),
            whole((LANES, inner)),
        ],
        out_specs=[
            pl.BlockSpec((CH, inner), lambda b: (b, 0)),
            pl.BlockSpec((1, LANES, inner), lambda b: (b, 0, 0)),
            whole((LANES, inner)),
        ],
        out_shape=[
            jax.ShapeDtypeStruct((rows, inner), F32),
            jax.ShapeDtypeStruct((blocks, LANES, inner), F32),
            jax.ShapeDtypeStruct((LANES, inner), F32),
        ],
        scratch_shapes=[pltpu.VMEM((LANES, inner), F32)],
        compiler_params=params(),
        cost_estimate=cost(6 * rows * CH * inner, 12 * rows * inner, rows * CH * heads),
    )(act, act, act, dt, cum, cum_t, skip, onehot)


def gate_kernel(normed, grad, w_gate, w_out, y_in, cm, seq, state, gain, onehot, gate_ref, y_ref, gon_ref, stat_ref):
    gate = dot_nn(normed[...], w_gate[...])
    grad_on = dot_nn(grad[...], w_out[...])
    y = y_in[...] + by_heads(jnp.exp(seq[...]), onehot[...]) * dot_nn(cm[...], state[...])
    gated = y * (gate * sigmoid(gate))
    gate_ref[...] = gate
    y_ref[...] = y
    gon_ref[...] = grad_on
    square = jnp.sum(gated * gated, axis=1, keepdims=True)
    inner = jnp.sum(grad_on * gain[...] * gated, axis=1, keepdims=True)
    lane = lax.broadcasted_iota(jnp.int32, (gate.shape[0], LANES), 1)
    both = jnp.where(lane == 0, square, jnp.where(lane == 1, inner, 0.0))
    stat_ref[...] = jnp.transpose(both)[0:8, :]


def gate_stage(normed, grad, w_rest, y_in, act, seq, state, gain, onehot):
    rows, dim = normed.shape
    inner = onehot.shape[1]
    col = inner // LANES
    block = pl.BlockSpec((CH, inner), lambda b: (b, 0))
    full = jax.ShapeDtypeStruct((rows, inner), F32)
    return pl.pallas_call(
        gate_kernel,
        name="gate_stage",
        grid=(rows // CH,),
        in_specs=[
            pl.BlockSpec((CH, dim), lambda b: (b, 0)),
            pl.BlockSpec((CH, dim), lambda b: (b, 0)),
            pl.BlockSpec((dim, inner), lambda b: (0, 0)),
            pl.BlockSpec((dim, inner), lambda b: (0, 1)),
            block,
            pl.BlockSpec((CH, LANES), lambda b: (b, col + 1)),
            pl.BlockSpec((CH, LANES), lambda b: (b, 0)),
            whole((LANES, inner)),
            whole((1, inner)),
            whole((LANES, inner)),
        ],
        out_specs=[block, block, block, pl.BlockSpec((8, CH), lambda b: (0, b))],
        out_shape=[full, full, full, jax.ShapeDtypeStruct((8, rows), F32)],
        compiler_params=params(),
        cost_estimate=cost(4 * rows * dim * inner, 16 * rows * inner + 4 * rows * dim, rows * inner),
    )(normed, grad, w_rest, w_rest, y_in, act, seq, state, gain, onehot)


def back_order(i):
    return jnp.where(i < 2, 2 + i, 3 - i)


def norm_kernel(inner_all, gate_ref, y_ref, gon_ref, stat, gain, out_in_ref, gy_ref, ggate_ref, gog):
    @pl.when(pl.program_id(0) == 0)
    def _():
        gog[...] = jnp.zeros_like(gog)

    columns = jnp.transpose(jnp.concatenate([stat[...]] * (LANES // 8), axis=0))
    scale = lax.rsqrt(columns[:, 0:1] * (1.0 / inner_all) + EPSILON)
    along = columns[:, 1:2] * (1.0 / inner_all)
    gate, y, grad_on = gate_ref[...], y_ref[...], gon_ref[...]
    sig = sigmoid(gate)
    silu = gate * sig
    gated = y * silu
    normed = gated * scale
    out_in_ref[...] = (normed * gain[...]).astype(BF16)
    gog[...] += fold_rows(grad_on * normed)
    grad_gated = scale * (grad_on * gain[...]) - gated * (scale * scale * scale * along)
    gy_ref[...] = (grad_gated * silu).astype(BF16)
    ggate_ref[...] = (grad_gated * y * (sig * (1.0 + gate * (1.0 - sig)))).astype(BF16)


def norm_stage(gate, y, grad_on, stat, gain, inner_all):
    rows, inner = gate.shape
    block = pl.BlockSpec((CH, inner), lambda i: (i, 0))
    low = jax.ShapeDtypeStruct((rows, inner), BF16)
    return pl.pallas_call(
        functools.partial(norm_kernel, inner_all),
        name="norm_stage",
        grid=(rows // CH,),
        in_specs=[block, block, block, pl.BlockSpec((8, CH), lambda i: (0, i)), whole((1, inner))],
        out_specs=[block, block, block, whole((8, inner))],
        out_shape=[low, low, low, jax.ShapeDtypeStruct((8, inner), F32)],
        compiler_params=params(),
        cost_estimate=cost(30 * rows * inner, 18 * rows * inner, rows * inner),
    )(gate, y, grad_on, stat, gain)


def mix_kernel(place, out_in, gy_ref, w_out, cm, cum, seq, onehot, send, keep, gstart, gin, gin_sum):
    step = pl.program_id(0)

    @pl.when(step == 0)
    def _():
        gin_sum[...] = jnp.zeros_like(gin_sum)

    mixed = dot_nt(out_in[...], w_out[...]).astype(BF16)

    @pl.when(step < 2)
    def _():
        send[...] = mixed

    @pl.when(step >= 2)
    def _():
        keep[...] = mixed

    hot = onehot[...]
    scaled = (gy_ref[...].astype(F32) * by_heads(jnp.exp(cum[...]), hot)).astype(BF16)
    grad_start = dot_tn(cm[...], scaled)
    gstart[0] = grad_start
    rows = cum.shape[0]
    ahead = seq[rows - 1 : rows, :] - cum[rows - 1 : rows, :]
    gin_sum[...] += row_of(jnp.exp(ahead), hot) * grad_start
    gin[...] = gin_sum[...].astype(BF16)


def mix_stage(place, out_in, gy, w_rest, act, cum, seq, onehot, dim):
    rows, inner = gy.shape
    col = inner // LANES
    blocks = rows // CH
    at = lambda i, q: back_order(i) ^ q[0]
    block = pl.BlockSpec((CH, inner), lambda i, q: (at(i, q), 0))
    wide = pl.BlockSpec((CH, LANES), lambda i, q: (at(i, q), 0))
    half = jax.ShapeDtypeStruct((rows // 2, dim), BF16)
    return pl.pallas_call(
        mix_kernel,
        name="mix_stage",
        grid_spec=pltpu.PrefetchScalarGridSpec(
            num_scalar_prefetch=1,
            grid=(blocks,),
            in_specs=[
                block,
                block,
                pl.BlockSpec((dim, inner), lambda i, q: (0, 1)),
                pl.BlockSpec((CH, LANES), lambda i, q: (at(i, q), col + 1)),
                wide,
                wide,
                whole((LANES, inner)),
            ],
            out_specs=[
                pl.BlockSpec((CH, dim), lambda i, q: (jnp.minimum(i, 1), 0)),
                pl.BlockSpec((CH, dim), lambda i, q: (jnp.minimum(3 - i, 1), 0)),
                pl.BlockSpec((1, LANES, inner), lambda i, q: (at(i, q), 0, 0)),
                whole((LANES, inner)),
            ],
            scratch_shapes=[pltpu.VMEM((LANES, inner), F32)],
        ),
        out_shape=[
            half,
            half,
            jax.ShapeDtypeStruct((blocks, LANES, inner), F32),
            jax.ShapeDtypeStruct((LANES, inner), BF16),
        ],
        compiler_params=params(),
        cost_estimate=cost(2 * rows * dim * inner, 6 * rows * inner + 4 * rows * dim, rows * LANES),
    )(place, out_in, gy, w_rest, act, cum, seq, onehot)


def early_kernel(grad_t, out_in, normed_t, ggate, out):
    inner = out_in.shape[1]
    out[:, 0:inner] = dot_nn(grad_t[...], out_in[...]).astype(BF16)
    out[:, inner:] = dot_nn(normed_t[...], ggate[...]).astype(BF16)


def early_grads(grad_t, out_in, normed_t, ggate):
    dim, rows = grad_t.shape
    inner = out_in.shape[1]
    tile = dim // 4
    return pl.pallas_call(
        early_kernel,
        name="early_grads",
        grid=(4,),
        in_specs=[
            pl.BlockSpec((tile, rows), lambda i: (i, 0)),
            whole((rows, inner)),
            pl.BlockSpec((tile, rows), lambda i: (i, 0)),
            whole((rows, inner)),
        ],
        out_specs=pl.BlockSpec((tile, 2 * inner), lambda i: (i, 0)),
        out_shape=jax.ShapeDtypeStruct((dim, 2 * inner), BF16),
        compiler_params=params(),
        cost_estimate=cost(4 * rows * dim * inner, 4 * dim * (rows + inner) + 4 * rows * inner, 0),
    )(grad_t, out_in, normed_t, ggate)


def lower_decay(mask, cum, cum_t, h):
    gap = jnp.where(mask, cum[:, h : h + 1] - cum_t[h : h + 1, :], 0.0)
    return jnp.where(mask, jnp.exp(gap), 0.0)


def ssd_back_kernel(
    heads, xa_ref, bm_ref, cm_ref, gy_ref, y_ref, dt_ref, sig_ref, cum_ref, seq_ref, cum_t_ref,
    start_ref, in_state, gstart_ref, gin, pre_ref, taps, rate, skip, onehot,
    gcat_ref, graw_ref, head_ref, tail_ref, rows_sum, heads_sum, gx, after, ext,
):
    step = pl.program_id(0)
    hot = onehot[...]

    @pl.when(step == 0)
    def _():
        rows_sum[...] = jnp.zeros_like(rows_sum)
        heads_sum[...] = jnp.zeros_like(heads_sum)
        after[...] = gin[...].astype(F32)
        ext[0:HALO, :] = jnp.zeros((HALO, ext.shape[1]), F32)

    cum, cum_t, dt = cum_ref[...], cum_t_ref[...], dt_ref[...]
    bm, cm = bm_ref[...], cm_ref[...]
    rows = cum.shape[0]
    last = cum[rows - 1 : rows, :]
    ahead = seq_ref[rows - 1 : rows, :] - last
    start = start_ref[0] + row_of(jnp.exp(ahead), hot) * in_state[...].astype(F32)
    grad_after = after[...]

    gy = gy_ref[...]
    xa = xa_ref[...].astype(F32)
    inner = xa.shape[1]
    dt_wide = by_heads(dt, hot)
    x_dt = xa * dt_wide
    x_low = x_dt.astype(BF16)
    scores = dot_nt(cm, bm)
    mask = lax.broadcasted_iota(jnp.int32, (rows, rows), 0) >= lax.broadcasted_iota(jnp.int32, (rows, rows), 1)
    width = inner // heads
    per = LANES // width
    lane = lax.broadcasted_iota(jnp.int32, (rows, LANES), 1) // width
    grad_scores = jnp.zeros((rows, rows), F32)
    for group in range(heads // per):
        at = slice(group * LANES, (group + 1) * LANES)
        gy_group, x_group = gy[:, at], x_low[:, at]
        total = jnp.zeros((rows, LANES), F32)
        for k in range(per):
            decay = lower_decay(mask, cum, cum_t, group * per + k)
            gy_head = jnp.where(lane == k, gy_group, jnp.zeros_like(gy_group))
            total = total + dot_tn((decay * scores).astype(BF16), gy_head)
            grad_scores = grad_scores + dot_nt(gy_head, x_group) * decay
        gx[:, at] = total

    end_wide = by_heads(jnp.exp(last - cum), hot)
    after_low = grad_after.astype(BF16)
    from_end = dot_nn(bm, after_low)
    to_end = (x_dt * end_wide).astype(BF16)
    gx_intra = gx[...]
    gx_all = gx_intra + end_wide * from_end
    end_term = to_end.astype(F32) * from_end
    gy_f = gy.astype(F32)
    grad_xa = dt_wide * gx_all + skip[...] * gy_f
    scores_low = grad_scores.astype(BF16)
    gy_scaled = (gy_f * by_heads(jnp.exp(cum), hot)).astype(BF16)
    grad_bm = dot_tn(scores_low, cm) + dot_nt(to_end, after_low)
    grad_cm = dot_nn(scores_low, bm) + dot_nt(gy_scaled, start.astype(BF16))

    grad_dt = by_heads_t(xa * gx_all, hot)
    grad_cum = by_heads_t(
        gy_f * (y_ref[...] - skip[...] * xa) - x_low.astype(F32) * gx_intra - end_term, hot
    )
    decay_row = row_of(jnp.exp(last), hot)
    end_rows = fold_rows(end_term)
    state_rows = fold_rows(grad_after * start) * decay_row
    grad_last = jnp.sum(by_heads_t(end_rows + state_rows, hot), axis=0, keepdims=True)
    upper = (
        lax.broadcasted_iota(jnp.int32, (rows, rows), 0) <= lax.broadcasted_iota(jnp.int32, (rows, rows), 1)
    ).astype(BF16)
    grad_a = jnp.broadcast_to(grad_last, grad_cum.shape)
    for part in exact_parts(grad_cum):
        grad_a = grad_a + dot_nn(upper, part)
    grad_raw = (grad_dt + rate[...] * grad_a) * sig_ref[...]
    graw_ref[...] = grad_raw.astype(BF16)
    heads_sum[0:8, :] += fold_rows(grad_raw)
    heads_sum[8:16, :] += fold_rows(grad_a * dt * rate[...])
    after[...] = gstart_ref[0] + decay_row * grad_after

    tap_count = 4
    first = HALO - tap_count + 1
    base = pl.multiple_of((pl.num_programs(0) - 1 - step) * rows, rows)
    ext[rows : rows + HALO, :] = ext[0:HALO, :]
    rows_sum[8 * tap_count + 8 : 8 * tap_count + 16, 0:inner] += fold_rows(gy_f * xa)
    for at, grad in (
        (slice(0, inner), grad_xa),
        (slice(inner, inner + 2 * LANES), jnp.concatenate([grad_bm, grad_cm], axis=1)),
    ):
        window = pre_ref[pl.ds(base, rows + HALO), at]
        conv = taps[tap_count : tap_count + 1, at] + taps[0:1, at] * window[first : first + rows]
        for k in range(1, tap_count):
            conv = conv + taps[k : k + 1, at] * window[first + k : first + k + rows]
        sig = sigmoid(conv)
        gconv = grad * (sig * (1.0 + conv * (1.0 - sig)))
        ext[0:rows, at] = gconv
        for k in range(tap_count):
            rows_sum[8 * k : 8 * k + 8, at] += fold_rows(gconv * window[first + k : first + k + rows])
        rows_sum[8 * tap_count : 8 * tap_count + 8, at] += fold_rows(gconv)
        gpre = taps[tap_count - 1 : tap_count, at] * gconv
        for k in range(tap_count - 1):
            ahead_by = tap_count - 1 - k
            gpre = gpre + taps[k : k + 1, at] * ext[ahead_by : ahead_by + rows, at]
        gcat_ref[:, at] = gpre.astype(BF16)

        @pl.when(step == 0)
        def _():
            tail_ref[:, at] = gpre[rows - 2 * HALO :, :]

    head_ref[...] = ext[0:HALO, :]


def ssd_backward(act, gy, y, dt, sig, cum, seq, cum_t, starts, in_state, gstart, gin, pre, taps, rate, skip, onehot, heads):
    rows, inner = gy.shape
    col = inner // LANES
    blocks = rows // CH
    total = pre.shape[1]
    top = blocks - 1
    block = pl.BlockSpec((CH, inner), lambda i: (top - i, 0))
    wide = pl.BlockSpec((CH, LANES), lambda i: (top - i, 0))
    state = pl.BlockSpec((1, LANES, inner), lambda i: (top - i, 0, 0))
    return pl.pallas_call(
        functools.partial(ssd_back_kernel, heads),
        name="ssd_backward",
        grid=(blocks,),
        in_specs=[
            block,
            pl.BlockSpec((CH, LANES), lambda i: (top - i, col)),
            pl.BlockSpec((CH, LANES), lambda i: (top - i, col + 1)),
            block,
            block,
            wide,
            wide,
            wide,
            wide,
            pl.BlockSpec((16, CH), lambda i: (0, top - i)),
            state,
            whole((LANES, inner)),
            state,
            whole((LANES, inner)),
            whole((rows + HALO, total)),
            whole((8, total)),
            whole((1, LANES)),
            whole((1, inner)),
            whole((LANES, inner)),
        ],
        out_specs=[
            pl.BlockSpec((CH, total), lambda i: (top - i, 0)),
            wide,
            whole((HALO, total)),
            whole((2 * HALO, total)),
            whole((48, total)),
            whole((16, LANES)),
        ],
        out_shape=[
            jax.ShapeDtypeStruct((rows, total), BF16),
            jax.ShapeDtypeStruct((rows, LANES), BF16),
            jax.ShapeDtypeStruct((HALO, total), F32),
            jax.ShapeDtypeStruct((2 * HALO, total), F32),
            jax.ShapeDtypeStruct((48, total), F32),
            jax.ShapeDtypeStruct((16, LANES), F32),
        ],
        scratch_shapes=[
            pltpu.VMEM((CH, inner), F32),
            pltpu.VMEM((LANES, inner), F32),
            pltpu.VMEM((CH + HALO, total), F32),
        ],
        compiler_params=params(),
        cost_estimate=cost(12 * rows * CH * inner, 24 * rows * inner, rows * CH * heads),
    )(act, act, act, gy, y, dt, sig, cum, seq, cum_t, starts, in_state, gstart, gin, pre, taps, rate, skip, onehot)


def input_kernel(where, gcat, ggate, graw, x_ref, w_gate, w_cat, w_dt, send, keep, gain_sum):
    step = pl.program_id(0)

    @pl.when(step == 0)
    def _():
        gain_sum[...] = jnp.zeros_like(gain_sum)

    total = dot_nt(ggate[...], w_gate[...]) + dot_nt(gcat[...], w_cat[...]) + dot_nt(graw[...], w_dt[...])
    xf = x_ref[...].astype(F32)
    scale = lax.rsqrt(jnp.mean(xf * xf, axis=1, keepdims=True) + EPSILON)
    gain_sum[...] += fold_rows(total * (xf * scale))
    part = total.astype(BF16)

    @pl.when(step < 2)
    def _():
        send[...] = part

    @pl.when(step >= 2)
    def _():
        keep[...] = part


def input_stage(where, gcat, ggate, graw, x, w_rest, w_first):
    rows, dim = x.shape
    inner, total = ggate.shape[1], gcat.shape[1]
    blocks = rows // CH
    at = lambda i, q: (back_order(i) ^ q[0], 0)
    half = jax.ShapeDtypeStruct((rows // 2, dim), BF16)
    return pl.pallas_call(
        input_kernel,
        name="input_stage",
        grid_spec=pltpu.PrefetchScalarGridSpec(
            num_scalar_prefetch=1,
            grid=(blocks,),
            in_specs=[
                pl.BlockSpec((CH, total), at),
                pl.BlockSpec((CH, inner), at),
                pl.BlockSpec((CH, LANES), at),
                pl.BlockSpec((CH, dim), at),
                pl.BlockSpec((dim, inner), lambda i, q: (0, 0)),
                pl.BlockSpec((dim, total), lambda i, q: (0, 0)),
                pl.BlockSpec((dim, LANES), lambda i, q: (0, total // LANES)),
            ],
            out_specs=[
                pl.BlockSpec((CH, dim), lambda i, q: (jnp.minimum(i, 1), 0)),
                pl.BlockSpec((CH, dim), lambda i, q: (jnp.minimum(3 - i, 1), 0)),
                pl.BlockSpec((8, dim), lambda i, q: (0, 0)),
            ],
        ),
        out_shape=[half, half, jax.ShapeDtypeStruct((8, dim), F32)],
        compiler_params=params(),
        cost_estimate=cost(4 * rows * dim * inner, 10 * rows * inner + 2 * rows * dim, 0),
    )(where, gcat, ggate, graw, x, w_rest, w_first, w_first)


def late_kernel(side, normed_t, gcat, keep_a, send_a, keep_b, send_b):
    step = pl.program_id(0)
    result = dot_nn(normed_t[...], gcat[...]).astype(BF16)
    rows = result.shape[0] // 2
    top, bottom = result[:rows], result[rows:]
    mine = side[0] == 0
    keep, send = jnp.where(mine, top, bottom), jnp.where(mine, bottom, top)

    @pl.when(step < 2)
    def _():
        keep_a[0], send_a[0] = keep, send

    @pl.when(step >= 2)
    def _():
        keep_b[0], send_b[0] = keep, send


def late_grads(side, normed_t, gcat):
    dim, rows = normed_t.shape
    width = gcat.shape[1]
    tile = dim // 4
    outer = pl.BlockSpec((1, tile // 2, width), lambda i, q: (jnp.minimum(i, 1), 0, 0))
    inner = pl.BlockSpec((1, tile // 2, width), lambda i, q: (jnp.maximum(i - 2, 0), 0, 0))
    return pl.pallas_call(
        late_kernel,
        name="late_grads",
        grid_spec=pltpu.PrefetchScalarGridSpec(
            num_scalar_prefetch=1,
            grid=(4,),
            in_specs=[
                pl.BlockSpec((tile, rows), lambda i, q: (jnp.where(i < 2, 3 * i, i - 1), 0)),
                pl.BlockSpec((rows, width), lambda i, q: (0, 0)),
            ],
            out_specs=[outer, outer, inner, inner],
        ),
        out_shape=[jax.ShapeDtypeStruct((2, tile // 2, width), BF16)] * 4,
        compiler_params=params(),
        cost_estimate=cost(2 * rows * dim * width, 2 * dim * (rows + width) + 2 * rows * width, 0),
    )(side, normed_t, gcat)


def on_device(
    hidden_in,
    norm_gain,
    w_in_zx,
    w_in_bc,
    w_in_dt,
    conv_x,
    conv_bc,
    dt_bias,
    a_log,
    d_skip,
    out_gain,
    w_out,
    cotangent,
):
    seq_count, rows, dim = hidden_in.shape
    inner = w_in_zx.shape[2]
    heads = w_in_dt.shape[1]
    head_dim = inner // heads
    tap_count = conv_x.shape[0] - 1
    tensor_size, shards, contexts = lax.axis_size("tensor"), lax.axis_size("shard"), lax.axis_size("context")
    inner_all = inner * tensor_size
    blocks = rows // CH
    assert seq_count == 1 and tensor_size == 4 and blocks == 4 and contexts == 2
    shard_rows = w_in_zx.shape[0]
    place = lax.axis_index("tensor")
    context = lax.axis_index("context")
    side_num = place % 2
    quarter = side_num * 2 + place // 2
    where = jnp.stack([quarter, side_num]).astype(jnp.int32)
    col = inner // LANES

    x_rows = hidden_in.reshape(rows, dim)
    g_rows = cotangent.reshape(rows, dim)

    pad_dt = jnp.zeros((shard_rows, LANES - heads), BF16)
    w_front = jnp.concatenate([w_in_zx[:, 1], w_in_bc, w_in_dt, pad_dt], axis=1)
    w_front, w_gate_local, w_out_local = together(w_front, w_in_zx[:, 0], w_out)
    w_back = jnp.concatenate([w_gate_local, w_out_local.T], axis=1)
    half_rows = shard_rows // contexts
    line = shards == 4
    all_rows = ("shard", "context")
    own_half = lambda v: lax.dynamic_slice_in_dim(v, context * half_rows, half_rows, 0)
    w_rest = lax.all_gather(own_half(w_back), all_rows, axis=0, tiled=True)
    if line:
        front = Gather(w_front)
        front.step()
    halo_rows = shifted(x_rows[rows - HALO :], "context", 1)

    def norm_of(values):
        wide = values.astype(F32)
        scale = lax.rsqrt(jnp.mean(wide * wide, axis=-1, keepdims=True) + EPSILON)
        return (wide * scale * norm_gain).astype(BF16)

    normed = norm_of(x_rows)
    halo = norm_of(halo_rows)

    pad_heads = lambda v: jnp.pad(v, (0, LANES - heads)).reshape(1, LANES)
    rate = pad_heads(-jnp.exp(a_log))
    bias = pad_heads(dt_bias)
    skip = jnp.repeat(d_skip, head_dim).reshape(1, inner)
    gain = out_gain.reshape(1, inner)
    taps = jnp.pad(jnp.concatenate([conv_x, conv_bc], axis=1), ((0, 8 - tap_count - 1), (0, 0)))
    onehot = (
        lax.broadcasted_iota(jnp.int32, (LANES, inner), 0)
        == lax.broadcasted_iota(jnp.int32, (LANES, inner), 1) // head_dim
    ).astype(BF16)

    if line:
        front.plus, front.minus, normed = together(front.plus, front.minus, normed)
        front.cross()
        front.step()
        front.plus, front.minus, halo = together(front.plus, front.minus, halo)
        front.cross()
        front.step()
        front.plus, front.minus = together(front.plus, front.minus)
        front.cross()
        w_first = front.full()
    else:
        w_first = lax.all_gather(own_half(w_front), all_rows, axis=0, tiled=True)

    act, pre = conv_front(normed, halo, w_first, taps)
    dt, sig, cum, seq, cum_t = step_sizes(normed, w_first, bias, rate, col + 2)
    y_local, starts, end_state = ssd_forward(act, dt, cum, cum_t, skip, onehot, heads)
    in_state = shifted(end_state.astype(BF16), "context", 1)
    normed_low, g_low, y_local = together(normed, g_rows, y_local)
    normed_t, grad_t = normed_low.T, g_low.T
    in_state, normed_t, grad_t = together(in_state, normed_t, grad_t)
    gate, y, grad_on, stat = gate_stage(normed, g_rows, w_rest, y_local, act, seq, in_state, gain, onehot)
    stat = butterfly(stat, "tensor")
    out_in, gy, ggate, gog = norm_stage(gate, y, grad_on, stat, gain, inner_all)
    early = early_grads(grad_t, out_in, normed_t, ggate)
    out_in, gy, early = together(out_in, gy, early)
    early_share = lax.psum_scatter(early, all_rows, scatter_dimension=0, tiled=True)

    own_rows = rows // 4
    send, keep, gstart, gin_first = mix_stage(where, out_in, gy, w_rest, act, cum, seq, onehot, dim)
    gin = shifted(gin_first, "context", -1)
    got = to_core(send)
    gy, gin, got = together(gy, gin, got)
    got_mine = to_chip(add_low(keep[own_rows:], got[own_rows:]))
    gcat, graw, head, end_rows, rows_sum, heads_sum = ssd_backward(
        act, gy, y, dt, sig, cum, seq, cum_t, starts, in_state, gstart, gin, pre, taps, rate, skip, onehot, heads
    )
    gcat, head, got_mine = together(gcat, head, got_mine)
    halo_in = shifted(head, "context", -1)
    mixed_mine = keep[:own_rows].astype(F32) + got[:own_rows].astype(F32) + got_mine.astype(F32)
    x_mine = lax.dynamic_slice_in_dim(x_rows, quarter * own_rows, own_rows, 0).astype(F32)
    stream_mine = x_mine + mixed_mine
    out_mine = stream_mine.astype(BF16)
    out_chip = to_chip(out_mine)
    out_a = to_core(out_mine)
    halo_in, out_mine = together(halo_in, out_mine)
    beyond = jnp.concatenate([jnp.zeros((2 * HALO, halo_in.shape[1]), F32), halo_in], axis=0)
    for k in range(tap_count - 1):
        ahead = tap_count - 1 - k
        end_rows = end_rows + taps[k : k + 1] * beyond[ahead : ahead + 2 * HALO]
    gcat = lax.dynamic_update_slice_in_dim(gcat, end_rows.astype(BF16), rows - 2 * HALO, 0)
    wide_bc = 2 * LANES
    if line:
        keep_a, send_a, keep_b, send_b = late_grads(context.astype(jnp.int32).reshape(1), normed_t, gcat)
        gcat, keep_a, send_a, send_b = together(gcat, keep_a, send_a, send_b)
        x_got_a = lax.ppermute(send_a, "context", swap_pairs(2, 1))
    send, keep, gain_sum = input_stage(where, gcat, ggate, graw, x_rows, w_rest, w_first)

    send, keep, gain_sum, out_chip, out_a, rows_sum, graw, gog, stream_late, mixed_late = together(
        send, keep, gain_sum, out_chip, out_a, rows_sum, graw, gog, stream_mine, mixed_mine
    )
    if line:
        send, gain_sum, x_got_a, send_b = together(send, gain_sum, x_got_a, send_b)
        x_got_b = lax.ppermute(send_b, "context", swap_pairs(2, 1))
        late_sum = LineSum()
        late_sum.first(keep_a, x_got_a)
    got = to_core(send)
    out_b = to_core(out_chip)

    wide = dim // inner
    tap_rows = -(-5 * wide_bc // inner)
    tap_sums = rows_sum.reshape(6, 8, -1).sum(1)
    taps_flat = jnp.pad(tap_sums[:5, inner:].reshape(-1), (0, tap_rows * inner - 5 * wide_bc))
    shared = jnp.concatenate(
        [
            gain_sum.sum(0).reshape(wide, inner),
            taps_flat.reshape(tap_rows, inner),
            jnp.pad(
                jnp.stack([jnp.sum(stream_late * stream_late), jnp.sum(mixed_late * mixed_late)]).reshape(1, 2),
                ((0, 0), (0, inner - 2)),
            ),
        ],
        axis=0,
    )
    shared = jnp.pad(shared, ((0, -shared.shape[0] % 8), (0, 0)))
    shared_rows = shared.shape[0]
    grad_dt_t = dot_tn(graw[:, :16], normed)
    local = jnp.concatenate(
        [
            grad_dt_t.reshape(-1, inner),
            tap_sums[:, :inner],
            gog.sum(0, keepdims=True),
            jnp.pad(heads_sum.reshape(2, 8, LANES).sum(1), ((0, 0), (0, inner - LANES))),
        ],
        axis=0,
    )
    local = jnp.pad(local, ((0, -local.shape[0] % 8), (0, 0)))
    local = jnp.concatenate([shared, local], axis=0)
    if line:
        got, local, out_b, late_sum.plus, late_sum.minus = together(got, local, out_b, late_sum.plus, late_sum.minus)
    got_mine = to_chip(add_low(keep[own_rows:], got[own_rows:]))
    out = assemble(out_mine, out_chip, out_a, out_b, where, BF16)
    if line:
        local = local + lax.ppermute(local, "shard", swap_pairs(shards, 1))
        x_got_b, out, local, early_share = together(x_got_b, out, local, early_share)
        late_sum.second(keep_b, x_got_b)
        local = local + lax.ppermute(local, "shard", swap_pairs(shards, 2))
        got_mine, late_sum.inner = together(got_mine, late_sum.inner)

    grad_normed = keep[:own_rows].astype(F32) + got[:own_rows].astype(F32) + got_mine.astype(F32)
    scale_mine = lax.rsqrt(jnp.mean(x_mine * x_mine, axis=-1, keepdims=True) + EPSILON)
    g_mine = lax.dynamic_slice_in_dim(g_rows, quarter * own_rows, own_rows, 0).astype(F32)
    grad_un = grad_normed * norm_gain
    grad_mine = (
        g_mine
        + scale_mine * grad_un
        - x_mine * scale_mine**3 * jnp.mean(grad_un * x_mine, axis=-1, keepdims=True)
    ).astype(BF16)
    in_chip = to_chip(grad_mine)
    in_a = to_core(grad_mine)
    if line:
        late_sum.plus, late_sum.minus, local, grad_mine = together(late_sum.plus, late_sum.minus, local, grad_mine)
        late_sum.third()
        local = local + lax.ppermute(local, "context", swap_pairs(2, 1))
        late_sum.plus, late_sum.minus, local, in_chip, in_a = together(
            late_sum.plus, late_sum.minus, local, in_chip, in_a
        )
        in_b = to_core(in_chip)
        late_share = late_sum.result()
    else:
        late = dot_nn(normed_t, gcat).astype(BF16)
        late_share = lax.psum_scatter(late, all_rows, scatter_dimension=0, tiled=True).astype(F32)
        local = butterfly(butterfly(local, "context"), "shard")
        in_b = to_core(in_chip)
    early_share = early_share.astype(F32)

    shared, local = local[:shared_rows], local[shared_rows:]
    sums = jnp.concatenate([late_share[:, inner:], shared.reshape(-1, wide_bc)], axis=0)
    sums = sums + to_core(sums)
    sums, in_b = together(sums, in_b)
    sums = sums + to_chip(sums)
    grad_input = assemble(grad_mine, in_chip, in_a, in_b, where, F32)
    bc_sum, shared = sums[:half_rows], sums[half_rows:].reshape(shared_rows, inner)
    first = 16 * dim // inner
    grad_dt_all = local[:first].reshape(16, dim)
    local = local[first:]
    totals = shared[wide + tap_rows]
    entry_count = rows * dim * shards * contexts
    own_features = (lax.axis_index("shard") * contexts + context) * half_rows
    return (
        out.reshape(hidden_in.shape),
        grad_input.reshape(hidden_in.shape),
        shared[:wide].reshape(dim),
        jnp.stack([early_share[:, inner:], late_share[:, :inner]], axis=1),
        bc_sum,
        lax.dynamic_slice_in_dim(grad_dt_all, own_features, half_rows, 1)[:heads].T,
        local[: tap_count + 1],
        shared[wide : wide + tap_rows].reshape(-1)[: 5 * wide_bc].reshape(5, wide_bc),
        local[tap_count + 3, :heads],
        local[tap_count + 4, :heads],
        local[tap_count + 1].reshape(heads, head_dim).sum(1),
        local[tap_count + 2],
        early_share[:, :inner].T,
        jnp.sqrt(totals[0] / entry_count),
        jnp.sqrt(totals[1] / entry_count),
    )


def solution(mesh):
    placed = (
        P("shard", "context", None),
        P(),
        P("shard", None, "tensor"),
        P("shard", None),
        P("shard", "tensor"),
        P(None, "tensor"),
        P(),
        P("tensor"),
        P("tensor"),
        P("tensor"),
        P("tensor"),
        P("tensor", "shard"),
        P("shard", "context", None),
    )
    return jax.shard_map(
        on_device,
        mesh=mesh,
        in_specs=placed,
        out_specs=(
            P("shard", "context", None),
            P("shard", "context", None),
            P(),
            P(("shard", "context"), None, "tensor"),
            P(("shard", "context"), None),
            P(("shard", "context"), "tensor"),
            P(None, "tensor"),
            P(),
            P("tensor"),
            P("tensor"),
            P("tensor"),
            P("tensor"),
            P("tensor", ("shard", "context")),
            P(),
            P(),
        ),
        check_vma=False,
    )
```

```python
import functools

import jax
import jax.numpy as jnp
from jax import lax
from jax.experimental import pallas as pl
from jax.experimental.pallas import tpu as pltpu
from jax.sharding import PartitionSpec as P

CH = 256
EPSILON = 1e-05
LANES = 128
HALO = 8
F32 = jnp.float32
BF16 = jnp.bfloat16


def swap_pairs(size, by):
    return [(i, i ^ by) for i in range(size)]


def butterfly(value, axis):
    size = lax.axis_size(axis)
    if size & (size - 1):
        return lax.psum(value, axis)
    by = 1
    while by < size:
        value = value + lax.ppermute(value, axis, swap_pairs(size, by))
        by *= 2
    return value


def shifted(array, axis, by):
    length = lax.axis_size(axis)
    pairs = [(i, i + by) for i in range(length) if 0 <= i + by < length]
    return lax.ppermute(array, axis, pairs)


def joint_pairs(size, context, sources, move):
    return [(i * context + c, move(i, c)[0] * context + move(i, c)[1]) for i in sources for c in range(context)]


class Gather:
    def __init__(self, local):
        self.shards, self.here, self.side = lax.axis_size("shard"), lax.axis_index("shard"), lax.axis_index("context")
        self.rows = local.shape[0] // 2
        self.local = local
        self.plus = self.minus = lax.dynamic_slice_in_dim(local, self.side * self.rows, self.rows, 0)
        self.k = 0
        self.pieces, self.places = [], []

    def step(self):
        self.k += 1
        size = self.shards
        self.plus = lax.ppermute(self.plus, "shard", [(i, i + 1) for i in range(self.k - 1, size - 1)])
        self.minus = lax.ppermute(self.minus, "shard", [(i, i - 1) for i in range(1, size - self.k + 1)])

    def add(self, piece, valid, source, side):
        self.pieces.append(piece)
        self.places.append(jnp.where(valid, source * 2 + side, -1))

    def cross(self):
        k, size = self.k, self.shards
        axes = ("shard", "context")
        across_plus = lax.ppermute(self.plus, axes, joint_pairs(size, 2, range(k, size), lambda i, c: (i, 1 - c)))
        across_minus = lax.ppermute(self.minus, axes, joint_pairs(size, 2, range(0, size - k), lambda i, c: (i, 1 - c)))
        for piece, side in ((self.plus, self.side), (across_plus, 1 - self.side)):
            self.add(piece, self.here >= k, self.here - k, side)
        for piece, side in ((self.minus, self.side), (across_minus, 1 - self.side)):
            self.add(piece, self.here + k < size, self.here + k, side)

    def full(self):
        place = jnp.stack([self.here * 2] + self.places).astype(jnp.int32)
        rows, cols = self.rows, self.local.shape[1]
        count = len(self.pieces)
        total = 2 * self.shards * rows
        return pl.pallas_call(
            layout_kernel,
            name="layout",
            grid_spec=pltpu.PrefetchScalarGridSpec(
                num_scalar_prefetch=1,
                grid=(1,),
                in_specs=[pl.BlockSpec((2 * rows, cols), lambda i, q: (0, 0))]
                + [pl.BlockSpec((rows, cols), lambda i, q: (0, 0))] * count,
                out_specs=pl.BlockSpec((total, cols), lambda i, q: (0, 0)),
            ),
            out_shape=jax.ShapeDtypeStruct((total, cols), self.local.dtype),
            compiler_params=params(),
            cost_estimate=cost(0, 2 * (2 * total + count * rows) * cols, 0),
        )(place, self.local, *self.pieces)


def layout_kernel(place, local, *rest):
    out = rest[-1]
    rows = rest[0].shape[0]
    out[pl.ds(pl.multiple_of(place[0] * rows, rows), 2 * rows), :] = local[...]
    for k, piece in enumerate(rest[:-1]):

        @pl.when(place[k + 1] >= 0)
        def _():
            out[pl.ds(pl.multiple_of(place[k + 1] * rows, rows), rows), :] = piece[...]


class LineSum:
    def __init__(self):
        self.size, self.here = lax.axis_size("shard"), lax.axis_index("shard")
        self.k = 0

    def piece(self, at):
        pieces = (self.outer[0], self.inner[0], self.inner[1], self.outer[1])
        return jnp.where(at == 0, pieces[0], jnp.where(at == 1, pieces[1], jnp.where(at == 2, pieces[2], pieces[3])))

    def send(self, up, down):
        self.k += 1
        self.plus = lax.ppermute(up, "shard", [(i, i + 1) for i in range(self.k)])
        self.minus = lax.ppermute(down, "shard", [(self.size - 1 - i, self.size - 2 - i) for i in range(self.k)])

    def first(self, keep, got):
        self.outer = add_low(keep, got)
        self.send(self.outer[1], self.outer[0])

    def second(self, keep, got):
        self.inner = add_low(keep, got)
        up = jnp.where(self.here == 0, self.inner[1], self.outer[1])
        down = jnp.where(self.here == 3, self.inner[0], self.outer[0])
        self.send(add_low(up, self.plus), add_low(down, self.minus))

    def third(self):
        self.send(add_low(self.piece(self.here + 1), self.plus), add_low(self.piece(self.here - 1), self.minus))

    def result(self):
        return self.piece(self.here).astype(F32) + self.plus.astype(F32) + self.minus.astype(F32)


def together(*values):
    return lax.optimization_barrier(values)


def to_core(value):
    return lax.ppermute(value, "tensor", swap_pairs(lax.axis_size("tensor"), 1))


def to_chip(value):
    return lax.ppermute(value, "tensor", swap_pairs(lax.axis_size("tensor"), 2))


def add_low(a, b):
    return (a.astype(F32) + b.astype(F32)).astype(BF16)


def assemble_kernel(place, own, chip, core_a, core_b, out):
    r = pl.program_id(0)
    for k, ref in enumerate((own, chip, core_a, core_b)):

        @pl.when(r == k)
        def _():
            out[...] = ref[...].astype(out.dtype)


def assemble(mine, chip, core_a, core_b, place, dtype):
    rows, cols = mine.shape
    piece = pl.BlockSpec((rows, cols), lambda r, q: (0, 0))
    return pl.pallas_call(
        assemble_kernel,
        name="assemble",
        grid_spec=pltpu.PrefetchScalarGridSpec(
            num_scalar_prefetch=1,
            grid=(4,),
            in_specs=[piece] * 4,
            out_specs=pl.BlockSpec((rows, cols), lambda r, q: (r ^ q[0], 0)),
        ),
        out_shape=jax.ShapeDtypeStruct((4 * rows, cols), dtype),
        compiler_params=params(),
        cost_estimate=cost(0, 12 * rows * cols + 0, 0),
    )(place, mine, chip, core_a, core_b)


def dot_nn(a, b):
    return lax.dot_general(a, b, (((1,), (0,)), ((), ())), preferred_element_type=F32)


def dot_nt(a, b):
    return lax.dot_general(a, b, (((1,), (1,)), ((), ())), preferred_element_type=F32)


def dot_tn(a, b):
    return lax.dot_general(a, b, (((0,), (0,)), ((), ())), preferred_element_type=F32)


def by_heads(values, onehot):
    high = values.astype(BF16)
    low = (values - high.astype(F32)).astype(BF16)
    return dot_nn(high, onehot) + dot_nn(low, onehot)


def by_heads_t(values, onehot):
    high = values.astype(BF16)
    low = (values - high.astype(F32)).astype(BF16)
    return dot_nt(high, onehot) + dot_nt(low, onehot)


def row_of(values, onehot):
    return by_heads(jnp.broadcast_to(values, (8, values.shape[1])), onehot)[0:1]


def fold_rows(values):
    rows, cols = values.shape
    return jnp.sum(values.reshape(rows // 8, 8, cols), axis=0)


def exact_parts(values):
    high = values.astype(BF16)
    rest = values - high.astype(F32)
    mid = rest.astype(BF16)
    low = (rest - mid.astype(F32)).astype(BF16)
    return high, mid, low


def sigmoid(values):
    return 1.0 / (1.0 + jnp.exp(-values))


def whole(shape):
    zeros = (0,) * len(shape)
    return pl.BlockSpec(shape, lambda *_: zeros)


def params(semantics=("arbitrary",)):
    return pltpu.CompilerParams(dimension_semantics=semantics, vmem_limit_bytes=60 * 1024 * 1024)


def cost(flops, nbytes, exps=0):
    return pl.CostEstimate(flops=int(flops), bytes_accessed=int(nbytes), transcendentals=int(exps))


def conv_kernel(normed, halo, weight, taps, act, pre):
    rows = normed.shape[0]
    tap_count = 4
    w = weight[...]
    pre[0:HALO, :] = dot_nn(halo[...], w)
    pre[HALO:, :] = dot_nn(normed[...], w)
    first = HALO - tap_count + 1
    out = taps[tap_count : tap_count + 1, :] + taps[0:1, :] * pre[first : first + rows, :]
    for k in range(1, tap_count):
        out = out + taps[k : k + 1, :] * pre[first + k : first + k + rows, :]
    act[...] = (out * sigmoid(out)).astype(BF16)


def conv_front(normed, halo, weight, taps):
    rows, dim = normed.shape
    cols = taps.shape[1]
    tile = 256
    return pl.pallas_call(
        conv_kernel,
        name="conv_front",
        grid=(cols // tile,),
        in_specs=[
            whole((rows, dim)),
            whole((HALO, dim)),
            pl.BlockSpec((dim, tile), lambda j: (0, j)),
            pl.BlockSpec((8, tile), lambda j: (0, j)),
        ],
        out_specs=[
            pl.BlockSpec((rows, tile), lambda j: (0, j)),
            pl.BlockSpec((rows + HALO, tile), lambda j: (0, j)),
        ],
        out_shape=[
            jax.ShapeDtypeStruct((rows, cols), BF16),
            jax.ShapeDtypeStruct((rows + HALO, cols), F32),
        ],
        compiler_params=params(),
        cost_estimate=cost(2 * rows * dim * cols, 2 * (rows + cols) * dim + 6 * rows * cols, rows * cols),
    )(normed, halo, weight, taps)


def step_kernel(normed, weight, bias, rate, dt, sig, cum, seq, cum_t, before):
    @pl.when(pl.program_id(0) == 0)
    def _():
        before[...] = jnp.zeros_like(before)

    raw = dot_nn(normed[...], weight[...]) + bias[...]
    small = jnp.exp(-jnp.abs(raw))
    dt_val = jnp.maximum(raw, 0.0) + jnp.log1p(small)
    dt[...] = dt_val
    sig[...] = sigmoid(raw)
    rows = raw.shape[0]
    lower = (
        lax.broadcasted_iota(jnp.int32, (rows, rows), 0) >= lax.broadcasted_iota(jnp.int32, (rows, rows), 1)
    ).astype(BF16)
    total = jnp.zeros_like(raw)
    for part in exact_parts(dt_val * rate[...]):
        total = total + dot_nn(lower, part)
    cum[...] = total
    seq[...] = total + before[0:1, :]
    before[...] = before[...] + jnp.broadcast_to(total[rows - 1 : rows, :], before.shape)
    cum_t[...] = jnp.transpose(total)[0:16, :]


def step_sizes(normed, weight, bias, rate, col):
    rows, dim = normed.shape
    block = pl.BlockSpec((CH, LANES), lambda b: (b, 0))
    wide = jax.ShapeDtypeStruct((rows, LANES), F32)
    return pl.pallas_call(
        step_kernel,
        name="step_sizes",
        grid=(rows // CH,),
        in_specs=[
            pl.BlockSpec((CH, dim), lambda b: (b, 0)),
            pl.BlockSpec((dim, LANES), lambda b: (0, col)),
            whole((1, LANES)),
            whole((1, LANES)),
        ],
        out_specs=[block, block, block, block, pl.BlockSpec((16, CH), lambda b: (0, b))],
        out_shape=[wide, wide, wide, wide, jax.ShapeDtypeStruct((16, rows), F32)],
        scratch_shapes=[pltpu.VMEM((8, LANES), F32)],
        compiler_params=params(),
        cost_estimate=cost(2 * rows * dim * LANES, 2 * rows * dim + 20 * rows * LANES, 3 * rows * LANES),
    )(normed, weight, bias, rate)


def ssd_kernel(heads, xa_ref, bm_ref, cm_ref, dt_ref, cum_ref, cum_t_ref, skip, onehot, y_ref, start_ref, end_ref, state):
    @pl.when(pl.program_id(0) == 0)
    def _():
        state[...] = jnp.zeros_like(state)

    hot = onehot[...]
    xa = xa_ref[...].astype(F32)
    bm, cm, cum, cum_t = bm_ref[...], cm_ref[...], cum_ref[...], cum_t_ref[...]
    rows = cum.shape[0]
    last = cum[rows - 1 : rows, :]
    x_dt = xa * by_heads(dt_ref[...], hot)
    before = state[...]
    start_ref[0] = before
    y_ref[...] = by_heads(jnp.exp(cum), hot) * dot_nn(cm, before.astype(BF16)) + skip[...] * xa
    to_end = (x_dt * by_heads(jnp.exp(last - cum), hot)).astype(BF16)
    after = row_of(jnp.exp(last), hot) * before + dot_tn(bm, to_end)
    state[...] = after
    end_ref[...] = after
    x_low = x_dt.astype(BF16)
    scores = dot_nt(cm, bm)
    mask = lax.broadcasted_iota(jnp.int32, (rows, rows), 0) >= lax.broadcasted_iota(jnp.int32, (rows, rows), 1)
    width = xa.shape[1] // heads
    per = LANES // width
    lane = lax.broadcasted_iota(jnp.int32, (rows, LANES), 1) // width
    for group in range(heads // per):
        at = slice(group * LANES, (group + 1) * LANES)
        x_group = x_low[:, at]
        total = y_ref[:, at]
        for k in range(per):
            h = group * per + k
            gap = jnp.where(mask, cum[:, h : h + 1] - cum_t[h : h + 1, :], 0.0)
            weights = jnp.where(mask, jnp.exp(gap) * scores, 0.0).astype(BF16)
            total = total + dot_nn(weights, jnp.where(lane == k, x_group, jnp.zeros_like(x_group)))
        y_ref[:, at] = total


def ssd_forward(act, dt, cum, cum_t, skip, onehot, heads):
    rows = act.shape[0]
    inner = onehot.shape[1]
    blocks = rows // CH
    col = inner // LANES
    wide = pl.BlockSpec((CH, LANES), lambda b: (b, 0))
    return pl.pallas_call(
        functools.partial(ssd_kernel, heads),
        name="ssd_forward",
        grid=(blocks,),
        in_specs=[
            pl.BlockSpec((CH, inner), lambda b: (b, 0)),
            pl.BlockSpec((CH, LANES), lambda b: (b, col)),
            pl.BlockSpec((CH, LANES), lambda b: (b, col + 1)),
            wide,
            wide,
            pl.BlockSpec((16, CH), lambda b: (0, b)),
            whole((1, inner)),
            whole((LANES, inner)),
        ],
        out_specs=[
            pl.BlockSpec((CH, inner), lambda b: (b, 0)),
            pl.BlockSpec((1, LANES, inner), lambda b: (b, 0, 0)),
            whole((LANES, inner)),
        ],
        out_shape=[
            jax.ShapeDtypeStruct((rows, inner), F32),
            jax.ShapeDtypeStruct((blocks, LANES, inner), F32),
            jax.ShapeDtypeStruct((LANES, inner), F32),
        ],
        scratch_shapes=[pltpu.VMEM((LANES, inner), F32)],
        compiler_params=params(),
        cost_estimate=cost(6 * rows * CH * inner, 12 * rows * inner, rows * CH * heads),
    )(act, act, act, dt, cum, cum_t, skip, onehot)


def gate_kernel(normed, grad, w_gate, w_out, y_in, cm, seq, state, gain, onehot, gate_ref, y_ref, gon_ref, stat_ref):
    gate = dot_nn(normed[...], w_gate[...])
    grad_on = dot_nn(grad[...], w_out[...])
    y = y_in[...] + by_heads(jnp.exp(seq[...]), onehot[...]) * dot_nn(cm[...], state[...])
    gated = y * (gate * sigmoid(gate))
    gate_ref[...] = gate
    y_ref[...] = y
    gon_ref[...] = grad_on
    square = jnp.sum(gated * gated, axis=1, keepdims=True)
    inner = jnp.sum(grad_on * gain[...] * gated, axis=1, keepdims=True)
    lane = lax.broadcasted_iota(jnp.int32, (gate.shape[0], LANES), 1)
    both = jnp.where(lane == 0, square, jnp.where(lane == 1, inner, 0.0))
    stat_ref[...] = jnp.transpose(both)[0:8, :]


def gate_stage(normed, grad, w_rest, y_in, act, seq, state, gain, onehot):
    rows, dim = normed.shape
    inner = onehot.shape[1]
    col = inner // LANES
    block = pl.BlockSpec((CH, inner), lambda b: (b, 0))
    full = jax.ShapeDtypeStruct((rows, inner), F32)
    return pl.pallas_call(
        gate_kernel,
        name="gate_stage",
        grid=(rows // CH,),
        in_specs=[
            pl.BlockSpec((CH, dim), lambda b: (b, 0)),
            pl.BlockSpec((CH, dim), lambda b: (b, 0)),
            pl.BlockSpec((dim, inner), lambda b: (0, 0)),
            pl.BlockSpec((dim, inner), lambda b: (0, 1)),
            block,
            pl.BlockSpec((CH, LANES), lambda b: (b, col + 1)),
            pl.BlockSpec((CH, LANES), lambda b: (b, 0)),
            whole((LANES, inner)),
            whole((1, inner)),
            whole((LANES, inner)),
        ],
        out_specs=[block, block, block, pl.BlockSpec((8, CH), lambda b: (0, b))],
        out_shape=[full, full, full, jax.ShapeDtypeStruct((8, rows), F32)],
        compiler_params=params(),
        cost_estimate=cost(4 * rows * dim * inner, 16 * rows * inner + 4 * rows * dim, rows * inner),
    )(normed, grad, w_rest, w_rest, y_in, act, seq, state, gain, onehot)


def back_order(i):
    return jnp.where(i < 2, 2 + i, 3 - i)


def norm_kernel(
    inner_all, gate_ref, y_ref, gon_ref, stat, gain, cm, cum, seq, onehot,
    out_in_ref, gy_ref, ggate_ref, gog, gstart, gin, gin_sum,
):
    @pl.when(pl.program_id(0) == 0)
    def _():
        gog[...] = jnp.zeros_like(gog)
        gin_sum[...] = jnp.zeros_like(gin_sum)

    columns = jnp.transpose(jnp.concatenate([stat[...]] * (LANES // 8), axis=0))
    scale = lax.rsqrt(columns[:, 0:1] * (1.0 / inner_all) + EPSILON)
    along = columns[:, 1:2] * (1.0 / inner_all)
    gate, y, grad_on = gate_ref[...], y_ref[...], gon_ref[...]
    sig = sigmoid(gate)
    silu = gate * sig
    gated = y * silu
    normed = gated * scale
    out_in_ref[...] = (normed * gain[...]).astype(BF16)
    gog[...] += fold_rows(grad_on * normed)
    grad_gated = scale * (grad_on * gain[...]) - gated * (scale * scale * scale * along)
    grad_y = (grad_gated * silu).astype(BF16)
    gy_ref[...] = grad_y
    ggate_ref[...] = (grad_gated * y * (sig * (1.0 + gate * (1.0 - sig)))).astype(BF16)
    hot = onehot[...]
    scaled = (grad_y.astype(F32) * by_heads(jnp.exp(cum[...]), hot)).astype(BF16)
    grad_start = dot_tn(cm[...], scaled)
    gstart[0] = grad_start
    rows = gate.shape[0]
    ahead = seq[rows - 1 : rows, :] - cum[rows - 1 : rows, :]
    gin_sum[...] += row_of(jnp.exp(ahead), hot) * grad_start
    gin[...] = gin_sum[...].astype(BF16)


def norm_stage(gate, y, grad_on, stat, act, cum, seq, gain, onehot, inner_all):
    rows, inner = gate.shape
    col = inner // LANES
    blocks = rows // CH
    block = pl.BlockSpec((CH, inner), lambda i: (i, 0))
    wide = pl.BlockSpec((CH, LANES), lambda i: (i, 0))
    low = jax.ShapeDtypeStruct((rows, inner), BF16)
    return pl.pallas_call(
        functools.partial(norm_kernel, inner_all),
        name="norm_stage",
        grid=(blocks,),
        in_specs=[
            block,
            block,
            block,
            pl.BlockSpec((8, CH), lambda i: (0, i)),
            whole((1, inner)),
            pl.BlockSpec((CH, LANES), lambda i: (i, col + 1)),
            wide,
            wide,
            whole((LANES, inner)),
        ],
        out_specs=[
            block,
            block,
            block,
            whole((8, inner)),
            pl.BlockSpec((1, LANES, inner), lambda i: (i, 0, 0)),
            whole((LANES, inner)),
        ],
        out_shape=[
            low,
            low,
            low,
            jax.ShapeDtypeStruct((8, inner), F32),
            jax.ShapeDtypeStruct((blocks, LANES, inner), F32),
            jax.ShapeDtypeStruct((LANES, inner), BF16),
        ],
        scratch_shapes=[pltpu.VMEM((LANES, inner), F32)],
        compiler_params=params(),
        cost_estimate=cost(600 * rows * inner, 18 * rows * inner, rows * inner),
    )(gate, y, grad_on, stat, gain, act, cum, seq, onehot)


def mix_kernel(place, out_in, w_out, send, keep):
    step = pl.program_id(0)
    mixed = dot_nt(out_in[...], w_out[...]).astype(BF16)

    @pl.when(step < 2)
    def _():
        send[...] = mixed

    @pl.when(step >= 2)
    def _():
        keep[...] = mixed


def mix_stage(place, out_in, w_rest, dim):
    rows, inner = out_in.shape
    half = jax.ShapeDtypeStruct((rows // 2, dim), BF16)
    return pl.pallas_call(
        mix_kernel,
        name="mix_stage",
        grid_spec=pltpu.PrefetchScalarGridSpec(
            num_scalar_prefetch=1,
            grid=(rows // CH,),
            in_specs=[
                pl.BlockSpec((CH, inner), lambda i, q: (back_order(i) ^ q[0], 0)),
                pl.BlockSpec((dim, inner), lambda i, q: (0, 1)),
            ],
            out_specs=[
                pl.BlockSpec((CH, dim), lambda i, q: (jnp.minimum(i, 1), 0)),
                pl.BlockSpec((CH, dim), lambda i, q: (jnp.minimum(3 - i, 1), 0)),
            ],
        ),
        out_shape=[half, half],
        compiler_params=params(),
        cost_estimate=cost(2 * rows * dim * inner, 2 * rows * inner + 4 * rows * dim, 0),
    )(place, out_in, w_rest)


def early_kernel(grad_t, out_in, normed_t, ggate, out):
    inner = out_in.shape[1]
    out[:, 0:inner] = dot_nn(grad_t[...], out_in[...]).astype(BF16)
    out[:, inner:] = dot_nn(normed_t[...], ggate[...]).astype(BF16)


def early_grads(grad_t, out_in, normed_t, ggate):
    dim, rows = grad_t.shape
    inner = out_in.shape[1]
    tile = dim // 4
    return pl.pallas_call(
        early_kernel,
        name="early_grads",
        grid=(4,),
        in_specs=[
            pl.BlockSpec((tile, rows), lambda i: (i, 0)),
            whole((rows, inner)),
            pl.BlockSpec((tile, rows), lambda i: (i, 0)),
            whole((rows, inner)),
        ],
        out_specs=pl.BlockSpec((tile, 2 * inner), lambda i: (i, 0)),
        out_shape=jax.ShapeDtypeStruct((dim, 2 * inner), BF16),
        compiler_params=params(),
        cost_estimate=cost(4 * rows * dim * inner, 4 * dim * (rows + inner) + 4 * rows * inner, 0),
    )(grad_t, out_in, normed_t, ggate)


def lower_decay(mask, cum, cum_t, h):
    gap = jnp.where(mask, cum[:, h : h + 1] - cum_t[h : h + 1, :], 0.0)
    return jnp.where(mask, jnp.exp(gap), 0.0)


def ssd_back_kernel(
    heads, xa_ref, bm_ref, cm_ref, gy_ref, y_ref, dt_ref, sig_ref, cum_ref, seq_ref, cum_t_ref,
    start_ref, in_state, gstart_ref, gin, pre_ref, taps, rate, skip, onehot,
    gcat_ref, graw_ref, head_ref, tail_ref, rows_sum, heads_sum, gx, after, ext,
):
    step = pl.program_id(0)
    hot = onehot[...]

    @pl.when(step == 0)
    def _():
        rows_sum[...] = jnp.zeros_like(rows_sum)
        heads_sum[...] = jnp.zeros_like(heads_sum)
        after[...] = gin[...].astype(F32)
        ext[0:HALO, :] = jnp.zeros((HALO, ext.shape[1]), F32)

    cum, cum_t, dt = cum_ref[...], cum_t_ref[...], dt_ref[...]
    bm, cm = bm_ref[...], cm_ref[...]
    rows = cum.shape[0]
    last = cum[rows - 1 : rows, :]
    ahead = seq_ref[rows - 1 : rows, :] - last
    start = start_ref[0] + row_of(jnp.exp(ahead), hot) * in_state[...].astype(F32)
    grad_after = after[...]

    gy = gy_ref[...]
    xa = xa_ref[...].astype(F32)
    inner = xa.shape[1]
    dt_wide = by_heads(dt, hot)
    x_dt = xa * dt_wide
    x_low = x_dt.astype(BF16)
    scores = dot_nt(cm, bm)
    mask = lax.broadcasted_iota(jnp.int32, (rows, rows), 0) >= lax.broadcasted_iota(jnp.int32, (rows, rows), 1)
    width = inner // heads
    per = LANES // width
    lane = lax.broadcasted_iota(jnp.int32, (rows, LANES), 1) // width
    grad_scores = jnp.zeros((rows, rows), F32)
    for group in range(heads // per):
        at = slice(group * LANES, (group + 1) * LANES)
        gy_group, x_group = gy[:, at], x_low[:, at]
        total = jnp.zeros((rows, LANES), F32)
        for k in range(per):
            decay = lower_decay(mask, cum, cum_t, group * per + k)
            gy_head = jnp.where(lane == k, gy_group, jnp.zeros_like(gy_group))
            total = total + dot_tn((decay * scores).astype(BF16), gy_head)
            grad_scores = grad_scores + dot_nt(gy_head, x_group) * decay
        gx[:, at] = total

    end_wide = by_heads(jnp.exp(last - cum), hot)
    after_low = grad_after.astype(BF16)
    from_end = dot_nn(bm, after_low)
    to_end = (x_dt * end_wide).astype(BF16)
    gx_intra = gx[...]
    gx_all = gx_intra + end_wide * from_end
    end_term = to_end.astype(F32) * from_end
    gy_f = gy.astype(F32)
    grad_xa = dt_wide * gx_all + skip[...] * gy_f
    scores_low = grad_scores.astype(BF16)
    gy_scaled = (gy_f * by_heads(jnp.exp(cum), hot)).astype(BF16)
    grad_bm = dot_tn(scores_low, cm) + dot_nt(to_end, after_low)
    grad_cm = dot_nn(scores_low, bm) + dot_nt(gy_scaled, start.astype(BF16))

    grad_dt = by_heads_t(xa * gx_all, hot)
    grad_cum = by_heads_t(
        gy_f * (y_ref[...] - skip[...] * xa) - x_low.astype(F32) * gx_intra - end_term, hot
    )
    decay_row = row_of(jnp.exp(last), hot)
    end_rows = fold_rows(end_term)
    state_rows = fold_rows(grad_after * start) * decay_row
    grad_last = jnp.sum(by_heads_t(end_rows + state_rows, hot), axis=0, keepdims=True)
    upper = (
        lax.broadcasted_iota(jnp.int32, (rows, rows), 0) <= lax.broadcasted_iota(jnp.int32, (rows, rows), 1)
    ).astype(BF16)
    grad_a = jnp.broadcast_to(grad_last, grad_cum.shape)
    for part in exact_parts(grad_cum):
        grad_a = grad_a + dot_nn(upper, part)
    grad_raw = (grad_dt + rate[...] * grad_a) * sig_ref[...]
    graw_ref[...] = grad_raw.astype(BF16)
    heads_sum[0:8, :] += fold_rows(grad_raw)
    heads_sum[8:16, :] += fold_rows(grad_a * dt * rate[...])
    after[...] = gstart_ref[0] + decay_row * grad_after

    tap_count = 4
    first = HALO - tap_count + 1
    base = pl.multiple_of((pl.num_programs(0) - 1 - step) * rows, rows)
    ext[rows : rows + HALO, :] = ext[0:HALO, :]
    rows_sum[8 * tap_count + 8 : 8 * tap_count + 16, 0:inner] += fold_rows(gy_f * xa)
    for at, grad in (
        (slice(0, inner), grad_xa),
        (slice(inner, inner + 2 * LANES), jnp.concatenate([grad_bm, grad_cm], axis=1)),
    ):
        window = pre_ref[pl.ds(base, rows + HALO), at]
        conv = taps[tap_count : tap_count + 1, at] + taps[0:1, at] * window[first : first + rows]
        for k in range(1, tap_count):
            conv = conv + taps[k : k + 1, at] * window[first + k : first + k + rows]
        sig = sigmoid(conv)
        gconv = grad * (sig * (1.0 + conv * (1.0 - sig)))
        ext[0:rows, at] = gconv
        for k in range(tap_count):
            rows_sum[8 * k : 8 * k + 8, at] += fold_rows(gconv * window[first + k : first + k + rows])
        rows_sum[8 * tap_count : 8 * tap_count + 8, at] += fold_rows(gconv)
        gpre = taps[tap_count - 1 : tap_count, at] * gconv
        for k in range(tap_count - 1):
            ahead_by = tap_count - 1 - k
            gpre = gpre + taps[k : k + 1, at] * ext[ahead_by : ahead_by + rows, at]
        gcat_ref[:, at] = gpre.astype(BF16)

        @pl.when(step == 0)
        def _():
            tail_ref[:, at] = gpre[rows - 2 * HALO :, :]

    head_ref[...] = ext[0:HALO, :]


def ssd_backward(act, gy, y, dt, sig, cum, seq, cum_t, starts, in_state, gstart, gin, pre, taps, rate, skip, onehot, heads):
    rows, inner = gy.shape
    col = inner // LANES
    blocks = rows // CH
    total = pre.shape[1]
    top = blocks - 1
    block = pl.BlockSpec((CH, inner), lambda i: (top - i, 0))
    wide = pl.BlockSpec((CH, LANES), lambda i: (top - i, 0))
    state = pl.BlockSpec((1, LANES, inner), lambda i: (top - i, 0, 0))
    return pl.pallas_call(
        functools.partial(ssd_back_kernel, heads),
        name="ssd_backward",
        grid=(blocks,),
        in_specs=[
            block,
            pl.BlockSpec((CH, LANES), lambda i: (top - i, col)),
            pl.BlockSpec((CH, LANES), lambda i: (top - i, col + 1)),
            block,
            block,
            wide,
            wide,
            wide,
            wide,
            pl.BlockSpec((16, CH), lambda i: (0, top - i)),
            state,
            whole((LANES, inner)),
            state,
            whole((LANES, inner)),
            whole((rows + HALO, total)),
            whole((8, total)),
            whole((1, LANES)),
            whole((1, inner)),
            whole((LANES, inner)),
        ],
        out_specs=[
            pl.BlockSpec((CH, total), lambda i: (top - i, 0)),
            wide,
            whole((HALO, total)),
            whole((2 * HALO, total)),
            whole((48, total)),
            whole((16, LANES)),
        ],
        out_shape=[
            jax.ShapeDtypeStruct((rows, total), BF16),
            jax.ShapeDtypeStruct((rows, LANES), BF16),
            jax.ShapeDtypeStruct((HALO, total), F32),
            jax.ShapeDtypeStruct((2 * HALO, total), F32),
            jax.ShapeDtypeStruct((48, total), F32),
            jax.ShapeDtypeStruct((16, LANES), F32),
        ],
        scratch_shapes=[
            pltpu.VMEM((CH, inner), F32),
            pltpu.VMEM((LANES, inner), F32),
            pltpu.VMEM((CH + HALO, total), F32),
        ],
        compiler_params=params(),
        cost_estimate=cost(12 * rows * CH * inner, 24 * rows * inner, rows * CH * heads),
    )(act, act, act, gy, y, dt, sig, cum, seq, cum_t, starts, in_state, gstart, gin, pre, taps, rate, skip, onehot)


def input_kernel(where, gcat, ggate, graw, x_ref, w_gate, w_cat, w_dt, send, keep, gain_sum):
    step = pl.program_id(0)

    @pl.when(step == 0)
    def _():
        gain_sum[...] = jnp.zeros_like(gain_sum)

    total = dot_nt(ggate[...], w_gate[...]) + dot_nt(gcat[...], w_cat[...]) + dot_nt(graw[...], w_dt[...])
    xf = x_ref[...].astype(F32)
    scale = lax.rsqrt(jnp.mean(xf * xf, axis=1, keepdims=True) + EPSILON)
    gain_sum[...] += fold_rows(total * (xf * scale))
    part = total.astype(BF16)

    @pl.when(step < 2)
    def _():
        send[...] = part

    @pl.when(step >= 2)
    def _():
        keep[...] = part


def input_stage(where, gcat, ggate, graw, x, w_rest, w_first):
    rows, dim = x.shape
    inner, total = ggate.shape[1], gcat.shape[1]
    blocks = rows // CH
    at = lambda i, q: (back_order(i) ^ q[0], 0)
    half = jax.ShapeDtypeStruct((rows // 2, dim), BF16)
    return pl.pallas_call(
        input_kernel,
        name="input_stage",
        grid_spec=pltpu.PrefetchScalarGridSpec(
            num_scalar_prefetch=1,
            grid=(blocks,),
            in_specs=[
                pl.BlockSpec((CH, total), at),
                pl.BlockSpec((CH, inner), at),
                pl.BlockSpec((CH, LANES), at),
                pl.BlockSpec((CH, dim), at),
                pl.BlockSpec((dim, inner), lambda i, q: (0, 0)),
                pl.BlockSpec((dim, total), lambda i, q: (0, 0)),
                pl.BlockSpec((dim, LANES), lambda i, q: (0, total // LANES)),
            ],
            out_specs=[
                pl.BlockSpec((CH, dim), lambda i, q: (jnp.minimum(i, 1), 0)),
                pl.BlockSpec((CH, dim), lambda i, q: (jnp.minimum(3 - i, 1), 0)),
                pl.BlockSpec((8, dim), lambda i, q: (0, 0)),
            ],
        ),
        out_shape=[half, half, jax.ShapeDtypeStruct((8, dim), F32)],
        compiler_params=params(),
        cost_estimate=cost(4 * rows * dim * inner, 10 * rows * inner + 2 * rows * dim, 0),
    )(where, gcat, ggate, graw, x, w_rest, w_first, w_first)


def late_kernel(side, normed_t, gcat, keep_a, send_a, keep_b, send_b):
    step = pl.program_id(0)
    result = dot_nn(normed_t[...], gcat[...]).astype(BF16)
    rows = result.shape[0] // 2
    top, bottom = result[:rows], result[rows:]
    mine = side[0] == 0
    keep, send = jnp.where(mine, top, bottom), jnp.where(mine, bottom, top)

    @pl.when(step < 2)
    def _():
        keep_a[0], send_a[0] = keep, send

    @pl.when(step >= 2)
    def _():
        keep_b[0], send_b[0] = keep, send


def late_grads(side, normed_t, gcat):
    dim, rows = normed_t.shape
    width = gcat.shape[1]
    tile = dim // 4
    outer = pl.BlockSpec((1, tile // 2, width), lambda i, q: (jnp.minimum(i, 1), 0, 0))
    inner = pl.BlockSpec((1, tile // 2, width), lambda i, q: (jnp.maximum(i - 2, 0), 0, 0))
    return pl.pallas_call(
        late_kernel,
        name="late_grads",
        grid_spec=pltpu.PrefetchScalarGridSpec(
            num_scalar_prefetch=1,
            grid=(4,),
            in_specs=[
                pl.BlockSpec((tile, rows), lambda i, q: (jnp.where(i < 2, 3 * i, i - 1), 0)),
                pl.BlockSpec((rows, width), lambda i, q: (0, 0)),
            ],
            out_specs=[outer, outer, inner, inner],
        ),
        out_shape=[jax.ShapeDtypeStruct((2, tile // 2, width), BF16)] * 4,
        compiler_params=params(),
        cost_estimate=cost(2 * rows * dim * width, 2 * dim * (rows + width) + 2 * rows * width, 0),
    )(side, normed_t, gcat)


def on_device(
    hidden_in,
    norm_gain,
    w_in_zx,
    w_in_bc,
    w_in_dt,
    conv_x,
    conv_bc,
    dt_bias,
    a_log,
    d_skip,
    out_gain,
    w_out,
    cotangent,
):
    seq_count, rows, dim = hidden_in.shape
    inner = w_in_zx.shape[2]
    heads = w_in_dt.shape[1]
    head_dim = inner // heads
    tap_count = conv_x.shape[0] - 1
    tensor_size, shards, contexts = lax.axis_size("tensor"), lax.axis_size("shard"), lax.axis_size("context")
    inner_all = inner * tensor_size
    blocks = rows // CH
    assert seq_count == 1 and tensor_size == 4 and blocks == 4 and contexts == 2
    shard_rows = w_in_zx.shape[0]
    place = lax.axis_index("tensor")
    context = lax.axis_index("context")
    side_num = place % 2
    quarter = side_num * 2 + place // 2
    where = jnp.stack([quarter, side_num]).astype(jnp.int32)
    col = inner // LANES

    x_rows = hidden_in.reshape(rows, dim)
    g_rows = cotangent.reshape(rows, dim)

    pad_dt = jnp.zeros((shard_rows, LANES - heads), BF16)
    w_front = jnp.concatenate([w_in_zx[:, 1], w_in_bc, w_in_dt, pad_dt], axis=1)
    w_front, w_gate_local, w_out_local = together(w_front, w_in_zx[:, 0], w_out)
    w_back = jnp.concatenate([w_gate_local, w_out_local.T], axis=1)
    half_rows = shard_rows // contexts
    line = shards == 4
    all_rows = ("shard", "context")
    own_half = lambda v: lax.dynamic_slice_in_dim(v, context * half_rows, half_rows, 0)
    w_rest = lax.all_gather(own_half(w_back), all_rows, axis=0, tiled=True)
    if line:
        front = Gather(w_front)
        front.step()
    halo_rows = shifted(x_rows[rows - HALO :], "context", 1)

    def norm_of(values):
        wide = values.astype(F32)
        scale = lax.rsqrt(jnp.mean(wide * wide, axis=-1, keepdims=True) + EPSILON)
        return (wide * scale * norm_gain).astype(BF16)

    normed = norm_of(x_rows)
    halo = norm_of(halo_rows)

    pad_heads = lambda v: jnp.pad(v, (0, LANES - heads)).reshape(1, LANES)
    rate = pad_heads(-jnp.exp(a_log))
    bias = pad_heads(dt_bias)
    skip = jnp.repeat(d_skip, head_dim).reshape(1, inner)
    gain = out_gain.reshape(1, inner)
    taps = jnp.pad(jnp.concatenate([conv_x, conv_bc], axis=1), ((0, 8 - tap_count - 1), (0, 0)))
    onehot = (
        lax.broadcasted_iota(jnp.int32, (LANES, inner), 0)
        == lax.broadcasted_iota(jnp.int32, (LANES, inner), 1) // head_dim
    ).astype(BF16)

    if line:
        front.plus, front.minus, normed = together(front.plus, front.minus, normed)
        front.cross()
        front.step()
        front.plus, front.minus, halo = together(front.plus, front.minus, halo)
        front.cross()
        front.step()
        front.plus, front.minus = together(front.plus, front.minus)
        front.cross()
        w_first = front.full()
    else:
        w_first = lax.all_gather(own_half(w_front), all_rows, axis=0, tiled=True)

    act, pre = conv_front(normed, halo, w_first, taps)
    dt, sig, cum, seq, cum_t = step_sizes(normed, w_first, bias, rate, col + 2)
    y_local, starts, end_state = ssd_forward(act, dt, cum, cum_t, skip, onehot, heads)
    in_state = shifted(end_state.astype(BF16), "context", 1)
    normed_low, g_low, y_local = together(normed, g_rows, y_local)
    normed_t, grad_t = normed_low.T, g_low.T
    in_state, normed_t, grad_t = together(in_state, normed_t, grad_t)
    gate, y, grad_on, stat = gate_stage(normed, g_rows, w_rest, y_local, act, seq, in_state, gain, onehot)
    stat = butterfly(stat, "tensor")
    out_in, gy, ggate, gog, gstart, gin_first = norm_stage(
        gate, y, grad_on, stat, act, cum, seq, gain, onehot, inner_all
    )
    gin = shifted(gin_first, "context", -1)
    early = early_grads(grad_t, out_in, normed_t, ggate)
    out_in, gin, early = together(out_in, gin, early)
    early_share = lax.psum_scatter(early, all_rows, scatter_dimension=0, tiled=True)

    own_rows = rows // 4
    send, keep = mix_stage(where, out_in, w_rest, dim)
    got = to_core(send)
    gy, gin, got = together(gy, gin, got)
    got_mine = to_chip(add_low(keep[own_rows:], got[own_rows:]))
    gcat, graw, head, end_rows, rows_sum, heads_sum = ssd_backward(
        act, gy, y, dt, sig, cum, seq, cum_t, starts, in_state, gstart, gin, pre, taps, rate, skip, onehot, heads
    )
    gcat, head, got_mine = together(gcat, head, got_mine)
    halo_in = shifted(head, "context", -1)
    mixed_mine = keep[:own_rows].astype(F32) + got[:own_rows].astype(F32) + got_mine.astype(F32)
    x_mine = lax.dynamic_slice_in_dim(x_rows, quarter * own_rows, own_rows, 0).astype(F32)
    stream_mine = x_mine + mixed_mine
    out_mine = stream_mine.astype(BF16)
    out_chip = to_chip(out_mine)
    out_a = to_core(out_mine)
    halo_in, out_mine = together(halo_in, out_mine)
    beyond = jnp.concatenate([jnp.zeros((2 * HALO, halo_in.shape[1]), F32), halo_in], axis=0)
    for k in range(tap_count - 1):
        ahead = tap_count - 1 - k
        end_rows = end_rows + taps[k : k + 1] * beyond[ahead : ahead + 2 * HALO]
    gcat = lax.dynamic_update_slice_in_dim(gcat, end_rows.astype(BF16), rows - 2 * HALO, 0)
    wide_bc = 2 * LANES
    if line:
        keep_a, send_a, keep_b, send_b = late_grads(context.astype(jnp.int32).reshape(1), normed_t, gcat)
        gcat, keep_a, send_a, send_b = together(gcat, keep_a, send_a, send_b)
        x_got_a = lax.ppermute(send_a, "context", swap_pairs(2, 1))
    send, keep, gain_sum = input_stage(where, gcat, ggate, graw, x_rows, w_rest, w_first)

    send, keep, gain_sum, out_chip, out_a, rows_sum, graw, gog, stream_late, mixed_late = together(
        send, keep, gain_sum, out_chip, out_a, rows_sum, graw, gog, stream_mine, mixed_mine
    )
    if line:
        send, gain_sum, x_got_a, send_b = together(send, gain_sum, x_got_a, send_b)
        x_got_b = lax.ppermute(send_b, "context", swap_pairs(2, 1))
        late_sum = LineSum()
        late_sum.first(keep_a, x_got_a)
    got = to_core(send)
    out_b = to_core(out_chip)

    wide = dim // inner
    tap_rows = -(-5 * wide_bc // inner)
    tap_sums = rows_sum.reshape(6, 8, -1).sum(1)
    taps_flat = jnp.pad(tap_sums[:5, inner:].reshape(-1), (0, tap_rows * inner - 5 * wide_bc))
    shared = jnp.concatenate(
        [
            gain_sum.sum(0).reshape(wide, inner),
            taps_flat.reshape(tap_rows, inner),
            jnp.pad(
                jnp.stack([jnp.sum(stream_late * stream_late), jnp.sum(mixed_late * mixed_late)]).reshape(1, 2),
                ((0, 0), (0, inner - 2)),
            ),
        ],
        axis=0,
    )
    shared = jnp.pad(shared, ((0, -shared.shape[0] % 8), (0, 0)))
    shared_rows = shared.shape[0]
    grad_dt_t = dot_tn(graw[:, :16], normed)
    local = jnp.concatenate(
        [
            grad_dt_t.reshape(-1, inner),
            tap_sums[:, :inner],
            gog.sum(0, keepdims=True),
            jnp.pad(heads_sum.reshape(2, 8, LANES).sum(1), ((0, 0), (0, inner - LANES))),
        ],
        axis=0,
    )
    local = jnp.pad(local, ((0, -local.shape[0] % 8), (0, 0)))
    local = jnp.concatenate([shared, local], axis=0)
    if line:
        got, local, out_b, late_sum.plus, late_sum.minus = together(got, local, out_b, late_sum.plus, late_sum.minus)
    got_mine = to_chip(add_low(keep[own_rows:], got[own_rows:]))
    out = assemble(out_mine, out_chip, out_a, out_b, where, BF16)
    if line:
        local = local + lax.ppermute(local, "shard", swap_pairs(shards, 1))
        x_got_b, out, local, early_share = together(x_got_b, out, local, early_share)
        late_sum.second(keep_b, x_got_b)
        local = local + lax.ppermute(local, "shard", swap_pairs(shards, 2))
        got_mine, late_sum.inner = together(got_mine, late_sum.inner)

    grad_normed = keep[:own_rows].astype(F32) + got[:own_rows].astype(F32) + got_mine.astype(F32)
    scale_mine = lax.rsqrt(jnp.mean(x_mine * x_mine, axis=-1, keepdims=True) + EPSILON)
    g_mine = lax.dynamic_slice_in_dim(g_rows, quarter * own_rows, own_rows, 0).astype(F32)
    grad_un = grad_normed * norm_gain
    grad_mine = (
        g_mine
        + scale_mine * grad_un
        - x_mine * scale_mine**3 * jnp.mean(grad_un * x_mine, axis=-1, keepdims=True)
    ).astype(BF16)
    in_chip = to_chip(grad_mine)
    in_a = to_core(grad_mine)
    if line:
        late_sum.plus, late_sum.minus, local, grad_mine = together(late_sum.plus, late_sum.minus, local, grad_mine)
        late_sum.third()
        local = local + lax.ppermute(local, "context", swap_pairs(2, 1))
        late_sum.plus, late_sum.minus, local, in_chip, in_a = together(
            late_sum.plus, late_sum.minus, local, in_chip, in_a
        )
        in_b = to_core(in_chip)
        late_share = late_sum.result()
    else:
        late = dot_nn(normed_t, gcat).astype(BF16)
        late_share = lax.psum_scatter(late, all_rows, scatter_dimension=0, tiled=True).astype(F32)
        local = butterfly(butterfly(local, "context"), "shard")
        in_b = to_core(in_chip)
    early_share = early_share.astype(F32)

    shared, local = local[:shared_rows], local[shared_rows:]
    sums = jnp.concatenate([late_share[:, inner:], shared.reshape(-1, wide_bc)], axis=0)
    sums = sums + to_core(sums)
    sums, in_b = together(sums, in_b)
    sums = sums + to_chip(sums)
    grad_input = assemble(grad_mine, in_chip, in_a, in_b, where, F32)
    bc_sum, shared = sums[:half_rows], sums[half_rows:].reshape(shared_rows, inner)
    first = 16 * dim // inner
    grad_dt_all = local[:first].reshape(16, dim)
    local = local[first:]
    totals = shared[wide + tap_rows]
    entry_count = rows * dim * shards * contexts
    own_features = (lax.axis_index("shard") * contexts + context) * half_rows
    return (
        out.reshape(hidden_in.shape),
        grad_input.reshape(hidden_in.shape),
        shared[:wide].reshape(dim),
        jnp.stack([early_share[:, inner:], late_share[:, :inner]], axis=1),
        bc_sum,
        lax.dynamic_slice_in_dim(grad_dt_all, own_features, half_rows, 1)[:heads].T,
        local[: tap_count + 1],
        shared[wide : wide + tap_rows].reshape(-1)[: 5 * wide_bc].reshape(5, wide_bc),
        local[tap_count + 3, :heads],
        local[tap_count + 4, :heads],
        local[tap_count + 1].reshape(heads, head_dim).sum(1),
        local[tap_count + 2],
        early_share[:, :inner].T,
        jnp.sqrt(totals[0] / entry_count),
        jnp.sqrt(totals[1] / entry_count),
    )


def solution(mesh):
    placed = (
        P("shard", "context", None),
        P(),
        P("shard", None, "tensor"),
        P("shard", None),
        P("shard", "tensor"),
        P(None, "tensor"),
        P(),
        P("tensor"),
        P("tensor"),
        P("tensor"),
        P("tensor"),
        P("tensor", "shard"),
        P("shard", "context", None),
    )
    return jax.shard_map(
        on_device,
        mesh=mesh,
        in_specs=placed,
        out_specs=(
            P("shard", "context", None),
            P("shard", "context", None),
            P(),
            P(("shard", "context"), None, "tensor"),
            P(("shard", "context"), None),
            P(("shard", "context"), "tensor"),
            P(None, "tensor"),
            P(),
            P("tensor"),
            P("tensor"),
            P("tensor"),
            P("tensor"),
            P("tensor", ("shard", "context")),
            P(),
            P(),
        ),
        check_vma=False,
    )
```
